512 devices in a mesh: sx: 32 (over y_lo, z), sy: 16 (over y_hi, x, core).
Axes of the slice: x: 4, y: 8 (y_hi: 2, y_lo: 4; y = y_hi * 4 + y_lo), z: 8, core: 2. Of those that a mesh axis runs over, the one named last changes fastest.
Arguments:
- right_vectors: bfloat16 [32, 1024, 4096], P(None, 'sx', 'sy'), may hold values from -6 to 6
- left_vectors: bfloat16 [64, 1024, 4096], P(None, 'sx', 'sy'), may hold values from -6 to 6
- classes: int32 [1024, 4096], P('sx', 'sy'), may hold values from 0 to 3
- class_energy: float32 [4], replicated, may hold values from -1.5 to 1.5
- bond_mask_grid: int32 [2, 1024, 4096], P(None, 'sx', 'sy'), may hold values 0 or 1
- order: int32 [5], replicated, may hold values from 0 to 4, each once
Outputs:
- gamma: float32 [5, 64, 32], P(None, 'sy')
The draws below stay inside these ranges and needn't reach their ends.
Inputs may be any that keep to these rules, and one draw needn't show every extreme that they name: Each order from 0 to 4 appears once.
All inputs are finite; a program needn't handle non-finite values. No bound on the sum of `bond_mask_grid` on one device may be relied on, other than what follows from the above.
Results may differ from the reference program's by a relative error of at most 0.0003.
Values sent between devices are 32-bit elements; how exact they have to be, the bound alone decides.
No kernel may reach another device: no remote copies, remote signals or barrier semaphores. Data moves between devices by JAX's collectives and lax.ppermute only.
A program may use at most 64 MiB of HBM per device.

```python
import jax
import jax.numpy as jnp
from jax import lax

RIGHT = 32
LEFT = 64
MOMENTS = 5
CLASSES = 4
NX = 1024
NY = 4096


def touch_ends(array, rng, low, high):
    shape = array.shape
    spot = [jax.random.randint(jax.random.fold_in(rng, axis), (), 0, shape[axis]) for axis in range(len(shape))]
    array = array.at[tuple(spot)].set(low)
    longest = shape.index(max(shape))
    spot[longest] = (spot[longest] + 1) % shape[longest]
    return array.at[tuple(spot)].set(high)


def block_levels(stream_key, extent, cuts, least, high):
    def one(axis_at, blocks):
        heights = jax.random.uniform(jax.random.fold_in(jax.random.fold_in(stream_key, 6), axis_at), (blocks,), jnp.float32, least / len(cuts), high / len(cuts))
        return jnp.repeat(jnp.exp(heights), extent[axis_at] // blocks).reshape((-1,) + (1,) * (len(extent) - axis_at - 1))

    factor_of = one(*cuts[0])
    for cut in cuts[1:]:
        factor_of = factor_of * one(*cut)
    return factor_of


def centred(own_key, dims, spread, bound, split=(), kind=jnp.bfloat16):
    array = jax.random.normal(own_key, dims, jnp.float32) * spread
    if len(split) > 0:
        array = block_levels(own_key, dims, split, -0.22, 0.18) * array
    return jnp.clip(array, min=-bound, max=bound).astype(kind)


def setup_inputs(seed: int = 0) -> dict:
    streams_of = jax.random.split(jax.random.key(seed), 7)
    right_vectors = centred(streams_of[0], (RIGHT, NX, NY), 1.0, 6.0, ((1, 32), (2, 16)))
    left_vectors = centred(streams_of[1], (LEFT, NX, NY), 1.0, 6.0, ((1, 32), (2, 16)))
    classes = touch_ends(jax.random.randint(streams_of[2], (NX, NY), 0, CLASSES), jax.random.fold_in(streams_of[2], 1), 0, CLASSES - 1).astype(jnp.int32)
    class_energy = jnp.clip(jax.random.uniform(streams_of[3], (CLASSES,), jnp.float32, -1.5, 1.5), -1.5, 1.5)
    bond_mask_grid = touch_ends((jax.random.randint(streams_of[4], (2, NX, NY), 0, 10) < 9).astype(jnp.int32), jax.random.fold_in(streams_of[4], 1), 0, 1)
    order = jax.random.permutation(streams_of[5], MOMENTS).astype(jnp.int32)
    return {"right_vectors": right_vectors, "left_vectors": left_vectors, "classes": classes, "class_energy": class_energy, "bond_mask_grid": bond_mask_grid, "order": order}


half_root = 0.8660254037844386
spectral_scale = 4.6

def couplings(classes, class_energy, bond_mask_grid):
    hmask = bond_mask_grid[0].astype(jnp.float32)
    vertical_mask = bond_mask_grid[1].astype(jnp.float32)
    xpos = jnp.arange(NX, dtype=jnp.int32)[:, None]
    ypos = jnp.arange(NY, dtype=jnp.int32)[None, :]
    sublattice_first = ((xpos + ypos) % 2 == 0).astype(jnp.float32)
    sublattice_second = 1.0 - sublattice_first
    east = hmask
    west = jnp.roll(hmask, 1, axis=0)
    upper_neighbour = vertical_mask * sublattice_first
    lower_neighbour = jnp.roll(vertical_mask, 1, axis=1) * sublattice_second
    energy = jnp.zeros((NX, NY), jnp.float32)
    for level in range(CLASSES):
        energy = energy + (classes == level).astype(jnp.float32) * class_energy[level]
    return (east, west, upper_neighbour, lower_neighbour, energy, sublattice_first - sublattice_second)

def neighbours(field):
    return (jnp.roll(field, -1, axis=1), jnp.roll(field, 1, axis=1), jnp.roll(field, -1, axis=2), jnp.roll(field, 1, axis=2))

def reference(right_vectors, left_vectors, classes, class_energy, bond_mask_grid, order):
    east, west, upper_neighbour, lower_neighbour, energy, sign = couplings(classes, class_energy, bond_mask_grid)

    def hamilton(field):
        pe, pw, pn, ps = neighbours(field)
        return (energy * field - east * pe - west * pw - upper_neighbour * pn - lower_neighbour * ps) / spectral_scale

    def vel_x(field):
        pe, pw, pn, ps = neighbours(field)
        return -half_root * (east * pe - west * pw)

    def vel_y(field):
        pe, pw, pn, ps = neighbours(field)
        return 0.5 * sign * (east * pe + west * pw) - upper_neighbour * pn + lower_neighbour * ps
    left_flat = left_vectors.astype(jnp.float32).reshape(LEFT, NX * NY)

    def moment(field):
        return jnp.dot(left_flat, vel_x(field).reshape(RIGHT, NX * NY).T, precision=lax.Precision.HIGHEST, preferred_element_type=jnp.float32)
    u_prev = vel_y(right_vectors.astype(jnp.float32))
    moments = [moment(u_prev)]
    u_now = hamilton(u_prev)
    moments.append(moment(u_now))
    for step in range(MOMENTS - 2):
        u_next = 2.0 * hamilton(u_now) - u_prev
        u_prev, u_now = (u_now, u_next)
        moments.append(moment(u_now))
    stacked = jnp.stack(moments) * (1.0 / jnp.sqrt(jnp.float32(NX * NY)))
    return stacked[order]
```

```python
import functools

import jax
import jax.numpy as jnp
from jax import lax
from jax.experimental import pallas as pl
from jax.experimental.pallas import tpu as pltpu
from jax.sharding import PartitionSpec as P

MOMENTS = 5
HALF_ROOT = 0.8660254037844386
SPECTRAL = 4.6
TWICE = 2.0 / SPECTRAL
DEPTH_X = MOMENTS + 1
SLOT = 4
REACH_Y = 3
LANES = 128
SUB = 8
PAD = 5


def slot_of(row, tile, tiles):
    at = row * tiles + tile
    per = LANES // SLOT
    return at // per, (at % per) * SLOT


def lane_iota():
    return lax.broadcasted_iota(jnp.int32, (SUB, LANES), 1)


def ext_block(own_ref, lo_ref, hi_ref, row, tile, lanes):
    depth, rows = lo_ref.shape[0], own_ref.shape[0]
    sub = pl.ds(tile * SUB, SUB)
    if row < depth:
        return lo_ref[row, sub, lanes]
    if row < depth + rows:
        return own_ref[row - depth, sub, lanes]
    return hi_ref[row - depth - rows, sub, lanes]


def pack_kernel(own_ref, lo_ref, hi_ref, first_ref, last_ref):
    rows = own_ref.shape[0] + 2 * lo_ref.shape[0]
    tiles = own_ref.shape[1] // SUB
    width = own_ref.shape[2]
    lane = lane_iota()
    first = [jnp.zeros((SUB, LANES), jnp.float32) for _ in range(first_ref.shape[0])]
    last = list(first)
    for row in range(rows):
        for tile in range(tiles):
            v, at = slot_of(row, tile, tiles)
            here = (lane >= at) & (lane < at + REACH_Y)
            a = ext_block(own_ref, lo_ref, hi_ref, row, tile, pl.ds(0, LANES))
            b = ext_block(own_ref, lo_ref, hi_ref, row, tile, pl.ds(width - LANES, LANES))
            first[v] = jnp.where(here, pltpu.roll(a, at, 1) if at else a, first[v])
            turn = (at + REACH_Y) % LANES
            last[v] = jnp.where(here, pltpu.roll(b, turn, 1) if turn else b, last[v])
    for v in range(first_ref.shape[0]):
        first_ref[v] = first[v]
        last_ref[v] = last[v]


def pack(own, lo, hi):
    rows = own.shape[0] + 2 * lo.shape[0]
    tiles = own.shape[1] // SUB
    count = -(-rows * tiles * SLOT // LANES)
    strip = jax.ShapeDtypeStruct((count, SUB, LANES), jnp.float32)
    return pl.pallas_call(
        pack_kernel,
        out_shape=(strip, strip),
        in_specs=[pl.BlockSpec(memory_space=pltpu.VMEM)] * 3,
        out_specs=(pl.BlockSpec(memory_space=pltpu.VMEM),) * 2,
        compiler_params=pltpu.CompilerParams(vmem_limit_bytes=12 << 20),
        name="pack_strips",
    )(own, lo, hi)


def partner(blocks, lane, odd):
    low = (lane & 1) == (1 if odd else 0)
    swapped = [
        jnp.where(low, pltpu.roll(b, LANES - 1, 1), pltpu.roll(b, 1, 1)) for b in blocks
    ]
    if not odd:
        return swapped
    n = len(blocks)
    return [
        jnp.where(
            lane == 0,
            swapped[(i - 1) % n],
            jnp.where(lane == LANES - 1, swapped[(i + 1) % n], swapped[i]),
        )
        for i in range(n)
    ]


def main_kernel(nright, own_ref, lo_ref, hi_ref, before_ref, after_ref, left_ref, out_ref, field, coup, acc, spaced):
    depth, rows_x, width = lo_ref.shape[0], own_ref.shape[0], own_ref.shape[2]
    rows = rows_x + 2 * depth
    tiles = own_ref.shape[1] // SUB
    rtiles = nright // SUB
    inner = width // LANES
    ntile = inner + 1
    lane = lane_iota()
    zero = jnp.zeros((SUB, LANES), jnp.float32)

    for row in range(rows):
        for tile in range(tiles):
            v, at = slot_of(row, tile, tiles)
            right_part = pltpu.roll(after_ref[v], (LANES - at) % LANES, 1) if at else after_ref[v]
            turn = (LANES - REACH_Y - at) % LANES
            left_part = pltpu.roll(before_ref[v], turn, 1) if turn else before_ref[v]
            rim = jnp.where(lane < REACH_Y, right_part, jnp.where(lane >= LANES - REACH_Y, left_part, zero))
            blocks = [
                ext_block(own_ref, lo_ref, hi_ref, row, tile, pl.ds(i * LANES, LANES)) for i in range(inner)
            ] + [rim]
            if tile < rtiles:
                for i in range(ntile):
                    field[0, row + PAD, tile * SUB : (tile + 1) * SUB, i * LANES : (i + 1) * LANES] = blocks[i]
            else:
                odd = (row - depth) % 2 == 1
                turned = partner(blocks, lane, odd)
                first_kind = ((lane + row - depth) & 1) == 0
                for i in range(ntile):
                    both = jnp.where(first_kind, blocks[i], turned[i])
                    for c, source in enumerate((blocks[i][0:1], both[1:2], blocks[i][2:3])):
                        coup[row + PAD, c, :, i * LANES : (i + 1) * LANES] = jnp.broadcast_to(source, (SUB, LANES))

    acc[...] = jnp.zeros_like(acc)

    def load(k, row, t, i):
        return field[k, row, t * SUB : (t + 1) * SUB, i * LANES : (i + 1) * LANES]

    def coupling(c, row, i):
        return coup[row, c, :, i * LANES : (i + 1) * LANES]

    def advance(k, row, odd):
        east = [coupling(0, row, i) for i in range(ntile)]
        west = [coupling(0, row - 1, i) for i in range(ntile)]
        vertical = [coupling(1, row, i) for i in range(ntile)]
        site = [coupling(2, row, i) for i in range(ntile)] if k else None
        sign = jnp.where((lane & 1) == (1 if odd else 0), 1.0 / TWICE, -1.0 / TWICE)
        for t in range(rtiles):
            here = [load(k, row, t, i) for i in range(ntile)]
            turned = partner(here, lane, odd)
            for i in range(ntile):
                a = east[i] * load(k, row + 1, t, i)
                b = west[i] * load(k, row - 1, t, i)
                if k == 0:
                    new = sign * (0.5 * (a + b) - vertical[i] * turned[i])
                else:
                    new = site[i] * here[i] - (a + b) - vertical[i] * turned[i]
                    new = 0.5 * new if k == 1 else new - load(k - 1, row, t, i)
                field[k + 1, row, t * SUB : (t + 1) * SUB, i * LANES : (i + 1) * LANES] = new

    def contract(row):
        east = [coupling(0, row, i) for i in range(inner)]
        west = [coupling(0, row - 1, i) for i in range(inner)]
        high, low = [], []
        for k in range(MOMENTS):
            parts = []
            for t in range(rtiles):
                parts.append(
                    jnp.concatenate(
                        [
                            east[i] * load(k + 1, row + 1, t, i) - west[i] * load(k + 1, row - 1, t, i)
                            for i in range(inner)
                        ],
                        axis=1,
                    )
                )
            value = jnp.concatenate(parts, axis=0)
            top = value.astype(jnp.bfloat16)
            high.append(top)
            low.append((value - top.astype(jnp.float32)).astype(jnp.bfloat16))
        block = left_ref[row - PAD - depth]
        dims = (((1,), (1,)), ((), ()))
        acc[...] += lax.dot_general(
            block, jnp.concatenate(high, axis=0), dims, preferred_element_type=jnp.float32
        ) + lax.dot_general(block, jnp.concatenate(low, axis=0), dims, preferred_element_type=jnp.float32)

    def step(front, odd, moments):
        for k in range(MOMENTS):
            advance(k, front - k, (odd + k) % 2 == 1)
        if moments:
            contract(front - MOMENTS)

    begin = 1 + PAD
    lead = 2 * MOMENTS

    def warm(n, _):
        front = begin + 2 * n
        step(front, (1 - depth) % 2, False)
        step(front + 1, (2 - depth) % 2, False)
        return 0

    lax.fori_loop(0, lead // 2, warm, 0)

    def full(n, _):
        front = begin + lead + 2 * n
        step(front, (1 + lead - depth) % 2, True)
        step(front + 1, (2 + lead - depth) % 2, True)
        return 0

    lax.fori_loop(0, rows_x // 2, full, 0)
    groups, _, flat = out_ref.shape
    owned = flat // nright
    for k in range(MOMENTS):
        spaced[:, 0:nright] = acc[:, k * nright : (k + 1) * nright]
        rows_of = [spaced[pl.ds(q, groups, stride=owned), :] for q in range(owned)]
        out_ref[:, k, :] = jnp.concatenate([r[:, 0:nright] for r in rows_of], axis=1)


def finish_kernel(scale, order_ref, blocks_ref, out_ref, total):
    total[...] = jnp.sum(blocks_ref[...], axis=0) * scale
    _, owned, nright = out_ref.shape
    for j in range(MOMENTS):
        row = total[pl.ds(order_ref[j], 1), :]
        for q in range(owned):
            out_ref[j, q : q + 1, :] = row[:, q * nright : (q + 1) * nright]


def moments_of_tile(own, lo, hi, before, after, left, nright, groups):
    rows = own.shape[0] + 2 * lo.shape[0]
    width = own.shape[2]
    nleft = left.shape[1]
    return pl.pallas_call(
        functools.partial(main_kernel, nright),
        out_shape=jax.ShapeDtypeStruct((groups, MOMENTS, nleft // groups * nright), jnp.float32),
        in_specs=[pl.BlockSpec(memory_space=pltpu.VMEM)] * 6,
        out_specs=pl.BlockSpec(memory_space=pltpu.VMEM),
        scratch_shapes=[
            pltpu.VMEM((MOMENTS + 1, rows + PAD, nright, width + LANES), jnp.float32),
            pltpu.VMEM((rows + PAD, 3, SUB, width + LANES), jnp.float32),
            pltpu.VMEM((nleft, MOMENTS * nright), jnp.float32),
            pltpu.VMEM((nleft, LANES), jnp.float32),
        ],
        compiler_params=pltpu.CompilerParams(vmem_limit_bytes=36 << 20),
        name="chebyshev_moments",
    )(own, lo, hi, before, after, left)


def ring(axis, by):
    size = lax.axis_size(axis)
    return [(i, (i + by) % size) for i in range(size)]


def shards(right_vectors, left_vectors, classes, class_energy, bond_mask_grid, order):
    rows_x, rows_y = classes.shape
    nright, nleft = right_vectors.shape[0], left_vectors.shape[0]

    def channels(start, size):
        right = lax.slice_in_dim(right_vectors, start, start + size, axis=1).astype(jnp.float32)
        masks = lax.slice_in_dim(bond_mask_grid, start, start + size, axis=1).astype(jnp.float32) * TWICE
        kinds = lax.slice_in_dim(classes, start, start + size, axis=0)
        energy = jnp.zeros((size, rows_y), jnp.float32)
        for level in range(class_energy.shape[0]):
            energy = jnp.where(kinds == level, class_energy[level] * TWICE, energy)
        rest = jnp.zeros((size, SUB - 3, rows_y), jnp.float32)
        return jnp.concatenate(
            [right.transpose(1, 0, 2), masks.transpose(1, 0, 2), energy[:, None], rest], axis=1
        )

    with jax.named_scope("halo_x"):
        lo = lax.ppermute(channels(rows_x - DEPTH_X, DEPTH_X), "sx", ring("sx", 1))
        hi = lax.ppermute(channels(0, DEPTH_X), "sx", ring("sx", -1))
    own = channels(0, rows_x)
    left = left_vectors.transpose(1, 0, 2)
    first, last = pack(own, lo, hi)
    with jax.named_scope("halo_y"):
        before = lax.ppermute(last, "sy", ring("sy", 1))
        after = lax.ppermute(first, "sy", ring("sy", -1))
    nsx, nsy = lax.axis_size("sx"), lax.axis_size("sy")
    owned = nleft // nsy
    tile = moments_of_tile(own, lo, hi, before, after, left, nright, nsy)
    with jax.named_scope("reduce_sy"):
        mine = jnp.sum(lax.all_to_all(tile, "sy", 0, 0), axis=0)
    with jax.named_scope("reduce_sx"):
        shares = lax.all_to_all(jnp.broadcast_to(mine[None], (nsx,) + mine.shape), "sx", 0, 0)
    sites = rows_x * rows_y * nsx * nsy
    return pl.pallas_call(
        functools.partial(finish_kernel, -HALF_ROOT / TWICE / sites**0.5),
        out_shape=jax.ShapeDtypeStruct((MOMENTS, owned, nright), jnp.float32),
        in_specs=[pl.BlockSpec(memory_space=pltpu.SMEM), pl.BlockSpec(memory_space=pltpu.VMEM)],
        out_specs=pl.BlockSpec(memory_space=pltpu.VMEM),
        scratch_shapes=[pltpu.VMEM(mine.shape, jnp.float32)],
        compiler_params=pltpu.CompilerParams(vmem_limit_bytes=4 << 20),
        name="finish",
    )(order, shares)


def solution(mesh):
    in_specs = (
        P(None, "sx", "sy"),
        P(None, "sx", "sy"),
        P("sx", "sy"),
        P(),
        P(None, "sx", "sy"),
        P(),
    )
    out_specs = P(None, "sy", None)
    return jax.shard_map(shards, mesh=mesh, in_specs=in_specs, out_specs=out_specs, check_vma=False)
```

```python
import functools

import jax
import jax.numpy as jnp
from jax import lax
from jax.experimental import pallas as pl
from jax.experimental.pallas import tpu as pltpu
from jax.sharding import PartitionSpec as P

MOMENTS = 5
HALF_ROOT = 0.8660254037844386
SPECTRAL = 4.6
TWICE = 2.0 / SPECTRAL
DEPTH = MOMENTS + 1
REACH = 3
SLOT = 4
COUPLINGS = 3
LANES = 128
SUB = 8
SPAN = 32


def lane_iota():
    return lax.broadcasted_iota(jnp.int32, (SUB, LANES), 1)


def turn(value, by):
    by %= LANES
    return pltpu.roll(value, by, 1) if by else value


def swap_major(blocks, sub):
    for s in (4, 2, 1):
        keep = (sub & s) == 0
        for i in range(SUB):
            if i & s == 0:
                a, b = blocks[i], blocks[i + s]
                blocks[i] = jnp.where(keep, a, pltpu.roll(b, s, 0))
                blocks[i + s] = jnp.where(keep, pltpu.roll(a, SUB - s, 0), b)
    return blocks


def prepare_kernel(energy_ref, right_ref, class_ref, bond_ref, own_ref, coup_ref, top_ref, bottom_ref, first_ref, last_ref):
    nright, rows, width = right_ref.shape
    lane = lane_iota()
    sub = lax.broadcasted_iota(jnp.int32, (SUB, LANES), 0)
    xtiles, rtiles, inner = rows // SUB, nright // SUB, width // LANES
    zero = jnp.zeros((SUB, LANES), jnp.float32)
    first, last = [zero] * (xtiles + 1), [zero] * (xtiles + 1)

    def strip(v, at, i, block):
        here = (lane >= at) & (lane < at + REACH)
        if i == 0:
            first[v] = jnp.where(here, turn(block, at), first[v])
        if i == inner - 1:
            last[v] = jnp.where(here, turn(block, at + REACH), last[v])

    for half in range(xtiles // 2):
        for i in range(inner):
            lanes = slice(i * LANES, (i + 1) * LANES)
            for t in range(rtiles):
                wide = [
                    right_ref[t * SUB + q, half * 2 * SUB : (half + 1) * 2 * SUB, lanes].astype(jnp.float32)
                    for q in range(SUB)
                ]
                for part in range(2):
                    xt = half * 2 + part
                    turned = swap_major([w[part * SUB : (part + 1) * SUB] for w in wide], sub)
                    for j in range(SUB):
                        x = xt * SUB + j
                        own_ref[x, t * SUB : (t + 1) * SUB, lanes] = turned[j]
                        if x < DEPTH:
                            top_ref[x * nright + t * SUB : x * nright + (t + 1) * SUB, lanes] = turned[j]
                        if x >= rows - DEPTH:
                            at = (x - rows + DEPTH) * nright + t * SUB
                            bottom_ref[at : at + SUB, lanes] = turned[j]
                        strip(xt, t * SPAN + j * SLOT, i, turned[j])
    for xt in range(xtiles):
        here = slice(xt * SUB, (xt + 1) * SUB)
        for i in range(inner):
            lanes = slice(i * LANES, (i + 1) * LANES)
            kinds = class_ref[here, lanes]
            energy = zero
            for level in range(energy_ref.shape[0]):
                energy = jnp.where(kinds == level, energy_ref[level] * TWICE, energy)
            fields = [bond_ref[c, here, lanes].astype(jnp.float32) * TWICE for c in range(2)] + [energy]
            for c in range(COUPLINGS):
                coup_ref[c, here, lanes] = fields[c]
                strip(xtiles, (c * xtiles + xt) * SLOT, i, fields[c])
                at = DEPTH * nright + c * SUB
                if xt == 0:
                    top_ref[at : at + SUB, lanes] = fields[c]
                if xt == xtiles - 1:
                    bottom_ref[at : at + SUB, lanes] = fields[c]
    for v in range(xtiles + 1):
        first_ref[v] = first[v]
        last_ref[v] = last[v]


def prepare(right, classes, energy, bonds):
    nright, rows, width = right.shape
    rim = jax.ShapeDtypeStruct((DEPTH * nright + COUPLINGS * SUB, width), jnp.float32)
    strip = jax.ShapeDtypeStruct((rows // SUB + 1, SUB, LANES), jnp.float32)
    return pl.pallas_call(
        prepare_kernel,
        out_shape=(
            jax.ShapeDtypeStruct((rows, nright, width), jnp.float32),
            jax.ShapeDtypeStruct((COUPLINGS, rows, width), jnp.float32),
            rim,
            rim,
            strip,
            strip,
        ),
        in_specs=[pl.BlockSpec(memory_space=pltpu.SMEM)] + [pl.BlockSpec(memory_space=pltpu.VMEM)] * 3,
        out_specs=(pl.BlockSpec(memory_space=pltpu.VMEM),) * 6,
        compiler_params=pltpu.CompilerParams(vmem_limit_bytes=8 << 20),
        name="prepare",
    )(energy, right, classes, bonds)


def swapped(block, lane, odd):
    low = (lane & 1) == (1 if odd else 0)
    target = jnp.where(low, lane + 1, lane + LANES - 1) & (LANES - 1)
    return jnp.take_along_axis(block, target, axis=1)


def main_kernel(own_ref, coup_ref, lo_ref, hi_ref, before_ref, after_ref, clo_ref, chi_ref, left_ref, out_ref, field, rim, coup, acc, spaced):
    rows_x, nright, width = own_ref.shape
    rows = rows_x + 2 * DEPTH
    rtiles, inner, xtiles = nright // SUB, width // LANES, rows_x // SUB
    lane = lane_iota()
    sub = lax.broadcasted_iota(jnp.int32, (SUB, LANES), 0)
    zero = jnp.zeros((SUB, LANES), jnp.float32)

    def lanes_of(i):
        return slice(i * LANES, (i + 1) * LANES)

    for e in range(rows):
        x = (e - DEPTH) % rows_x
        if e < DEPTH:
            before, after = clo_ref[0], clo_ref[2]
        elif e >= DEPTH + rows_x:
            before, after = chi_ref[0], chi_ref[2]
        else:
            before, after = before_ref[x // SUB], after_ref[x // SUB]
        shift = (x % SUB) * SLOT
        rim[0, e] = jnp.where(
            lane % SPAN < REACH,
            turn(after, -shift),
            jnp.where(lane % SPAN >= SPAN - REACH, turn(before, -shift - REACH), zero),
        )
        if e < DEPTH:
            field[0, e] = lo_ref[e * nright : (e + 1) * nright, :]
        elif e >= DEPTH + rows_x:
            at = (e - DEPTH - rows_x) * nright
            field[0, e] = hi_ref[at : at + nright, :]
        else:
            field[0, e] = own_ref[x]

    for g in range(xtiles + 2):
        xt = (g - 1) % xtiles
        if g == 0:
            before, after = clo_ref[1], clo_ref[3]
        elif g == xtiles + 1:
            before, after = chi_ref[1], chi_ref[3]
        else:
            before, after = before_ref[xtiles], after_ref[xtiles]
        whole = []
        for c in range(COUPLINGS):
            at = DEPTH * nright + c * SUB
            if g == 0:
                blocks = [lo_ref[at : at + SUB, lanes_of(i)] for i in range(inner)]
            elif g == xtiles + 1:
                blocks = [hi_ref[at : at + SUB, lanes_of(i)] for i in range(inner)]
            else:
                blocks = [coup_ref[c, xt * SUB : (xt + 1) * SUB, lanes_of(i)] for i in range(inner)]
            shift = (c * xtiles + xt) * SLOT
            blocks.append(
                jnp.where(
                    lane < REACH,
                    turn(after, -shift),
                    jnp.where(lane >= LANES - REACH, turn(before, -shift - REACH), zero),
                )
            )
            if c == 1:
                even = [swapped(b, lane, False) for b in blocks]
                odd = [swapped(b, lane, True) for b in blocks]
                n = len(blocks)
                odd = [
                    jnp.where(lane == 0, odd[(i - 1) % n], jnp.where(lane == LANES - 1, odd[(i + 1) % n], odd[i]))
                    for i in range(n)
                ]
                blocks = [
                    jnp.where(((lane + sub) & 1) == 0, b, jnp.where((sub & 1) == 1, o, v))
                    for b, o, v in zip(blocks, odd, even)
                ]
            edge = blocks[inner]
            edge = edge + turn(edge, LANES // 2)
            blocks[inner] = edge + turn(edge, LANES // 4)
            whole.append(blocks)
        for s in range(SUB):
            e = (g - 1) * SUB + s + DEPTH
            if 0 <= e < rows:
                for c in range(COUPLINGS):
                    for i in range(inner + 1):
                        coup[e, c, :, lanes_of(i)] = jnp.broadcast_to(whole[c][i][s : s + 1], (SUB, LANES))

    acc[...] = jnp.zeros_like(acc)

    def load(k, row, t, i):
        if i == inner:
            return rim[k, row]
        return field[k, row, t * SUB : (t + 1) * SUB, lanes_of(i)]

    def coupling(c, row, i):
        return coup[row, c, :, lanes_of(i)]

    where = [(t, i) for t in range(rtiles) for i in range(inner)] + [(0, inner)]

    def partners(here, odd):
        moved = {at: swapped(value, lane, odd) for at, value in here.items()}
        if not odd:
            return moved
        edge = moved[0, inner]
        start, end = lane == 0, lane == LANES - 1
        result, fill = {}, edge
        for t in range(rtiles):
            outer = turn(edge, -t * SPAN)
            for i in range(inner):
                left = moved[t, i - 1] if i else outer
                right = moved[t, i + 1] if i < inner - 1 else outer
                result[t, i] = jnp.where(start, left, jnp.where(end, right, moved[t, i]))
            facing = turn(jnp.where(lane < LANES // 2, moved[t, inner - 1], moved[t, 0]), t * SPAN)
            fill = jnp.where((lane == t * SPAN) | (lane == (t * SPAN - 1) % LANES), facing, fill)
        result[0, inner] = fill
        return result

    def advance(k, row, odd):
        here = {at: load(k, row, *at) for at in where}
        turned = partners(here, odd)
        east = [coupling(0, row, i) for i in range(inner + 1)]
        west = [coupling(0, row - 1, i) for i in range(inner + 1)]
        vertical = [coupling(1, row, i) for i in range(inner + 1)]
        site = [coupling(2, row, i) for i in range(inner + 1)] if k else None
        sign = jnp.where((lane & 1) == (1 if odd else 0), 1.0 / TWICE, -1.0 / TWICE)
        new = {}
        for t, i in where:
            beside = east[i] * load(k, row + 1, t, i) + west[i] * load(k, row - 1, t, i)
            across = vertical[i] * turned[t, i]
            if k == 0:
                new[t, i] = sign * (0.5 * beside - across)
            else:
                image = site[i] * here[t, i] - beside - across
                new[t, i] = 0.5 * image if k == 1 else image - load(k - 1, row, t, i)
        for t, i in where:
            if i == inner:
                rim[k + 1, row] = new[t, i]
            else:
                field[k + 1, row, t * SUB : (t + 1) * SUB, lanes_of(i)] = new[t, i]

    def contract(row):
        east = [coupling(0, row, i) for i in range(inner)]
        west = [coupling(0, row - 1, i) for i in range(inner)]
        high, low = [], []
        for k in range(MOMENTS):
            parts = []
            for t in range(rtiles):
                parts.append(
                    jnp.concatenate(
                        [
                            east[i] * load(k + 1, row + 1, t, i) - west[i] * load(k + 1, row - 1, t, i)
                            for i in range(inner)
                        ],
                        axis=1,
                    )
                )
            value = jnp.concatenate(parts, axis=0)
            top = value.astype(jnp.bfloat16)
            high.append(top)
            low.append((value - top.astype(jnp.float32)).astype(jnp.bfloat16))
        block = left_ref[row - DEPTH]
        dims = (((1,), (1,)), ((), ()))
        acc[...] += lax.dot_general(
            block, jnp.concatenate(high, axis=0), dims, preferred_element_type=jnp.float32
        ) + lax.dot_general(block, jnp.concatenate(low, axis=0), dims, preferred_element_type=jnp.float32)

    lead = DEPTH + 2 * MOMENTS
    for front in range(1, lead):
        for k in reversed(range(MOMENTS)):
            if front >= 3 * k + 1:
                advance(k, front - 2 * k, front % 2 == 1)

    def both(n, _):
        for part in range(2):
            front = lead + 2 * n + part
            contract(front - 2 * MOMENTS)
            for k in reversed(range(MOMENTS)):
                advance(k, front - 2 * k, (lead + part) % 2 == 1)
        return 0

    lax.fori_loop(0, rows_x // 2, both, 0)
    groups, _, flat = out_ref.shape
    owned = flat // nright
    for k in range(MOMENTS):
        spaced[:, 0:nright] = acc[:, k * nright : (k + 1) * nright]
        rows_of = [spaced[pl.ds(q, groups, stride=owned), :] for q in range(owned)]
        out_ref[:, k, :] = jnp.concatenate([r[:, 0:nright] for r in rows_of], axis=1)


def finish_kernel(scale, order_ref, blocks_ref, out_ref, total):
    total[...] = jnp.sum(blocks_ref[...], axis=0) * scale
    _, owned, nright = out_ref.shape
    for j in range(MOMENTS):
        row = total[pl.ds(order_ref[j], 1), :]
        for q in range(owned):
            out_ref[j, q : q + 1, :] = row[:, q * nright : (q + 1) * nright]


def moments_of_tile(own, coup, lo, hi, before, after, clo, chi, left, groups):
    rows_x, nright, width = own.shape
    rows = rows_x + 2 * DEPTH + MOMENTS
    nleft = left.shape[1]
    return pl.pallas_call(
        main_kernel,
        out_shape=jax.ShapeDtypeStruct((groups, MOMENTS, nleft // groups * nright), jnp.float32),
        in_specs=[pl.BlockSpec(memory_space=pltpu.VMEM)] * 9,
        out_specs=pl.BlockSpec(memory_space=pltpu.VMEM),
        scratch_shapes=[
            pltpu.VMEM((MOMENTS + 1, rows, nright, width), jnp.float32),
            pltpu.VMEM((MOMENTS + 1, rows, SUB, LANES), jnp.float32),
            pltpu.VMEM((rows, COUPLINGS, SUB, width + LANES), jnp.float32),
            pltpu.VMEM((nleft, MOMENTS * nright), jnp.float32),
            pltpu.VMEM((nleft, LANES), jnp.float32),
        ],
        compiler_params=pltpu.CompilerParams(vmem_limit_bytes=28 << 20),
        name="chebyshev_moments",
    )(own, coup, lo, hi, before, after, clo, chi, left)


def ring(axis, by):
    size = lax.axis_size(axis)
    return [(i, (i + by) % size) for i in range(size)]


def shards(right_vectors, left_vectors, classes, class_energy, bond_mask_grid, order):
    rows_x, rows_y = classes.shape
    nright, nleft = right_vectors.shape[0], left_vectors.shape[0]
    nsx, nsy = lax.axis_size("sx"), lax.axis_size("sy")
    owned = nleft // nsy

    own, coup, top, bottom, first, last = prepare(right_vectors, classes, class_energy, bond_mask_grid)
    with jax.named_scope("halo_y"):
        before = lax.ppermute(last, "sy", ring("sy", 1))
        after = lax.ppermute(first, "sy", ring("sy", -1))
    with jax.named_scope("halo_x"):
        lo = lax.ppermute(bottom, "sx", ring("sx", 1))
        hi = lax.ppermute(top, "sx", ring("sx", -1))
    with jax.named_scope("halo_corner"):
        up = jnp.concatenate([before[-2:], after[-2:]], axis=0)
        down = jnp.concatenate([before[:1], before[-1:], after[:1], after[-1:]], axis=0)
        clo = lax.ppermute(up, "sx", ring("sx", 1))
        chi = lax.ppermute(down, "sx", ring("sx", -1))
    left = left_vectors.transpose(1, 0, 2)
    tile = moments_of_tile(own, coup, lo, hi, before, after, clo, chi, left, nsy)
    with jax.named_scope("reduce_sy"):
        mine = jnp.sum(lax.all_to_all(tile, "sy", 0, 0), axis=0)
    with jax.named_scope("reduce_sx"):
        shares = lax.all_to_all(jnp.broadcast_to(mine[None], (nsx,) + mine.shape), "sx", 0, 0)
    sites = rows_x * rows_y * nsx * nsy
    return pl.pallas_call(
        functools.partial(finish_kernel, -HALF_ROOT / TWICE / sites**0.5),
        out_shape=jax.ShapeDtypeStruct((MOMENTS, owned, nright), jnp.float32),
        in_specs=[pl.BlockSpec(memory_space=pltpu.SMEM), pl.BlockSpec(memory_space=pltpu.VMEM)],
        out_specs=pl.BlockSpec(memory_space=pltpu.VMEM),
        scratch_shapes=[pltpu.VMEM(mine.shape, jnp.float32)],
        compiler_params=pltpu.CompilerParams(vmem_limit_bytes=4 << 20),
        name="finish",
    )(order, shares)


def solution(mesh):
    in_specs = (
        P(None, "sx", "sy"),
        P(None, "sx", "sy"),
        P("sx", "sy"),
        P(),
        P(None, "sx", "sy"),
        P(),
    )
    out_specs = P(None, "sy", None)
    return jax.shard_map(shards, mesh=mesh, in_specs=in_specs, out_specs=out_specs, check_vma=False)
```

```python
import functools

import jax
import jax.numpy as jnp
from jax import lax
from jax.experimental import pallas as pl
from jax.experimental.pallas import tpu as pltpu
from jax.sharding import PartitionSpec as P

MOMENTS = 5
HALF_ROOT = 0.8660254037844386
SPECTRAL = 4.6
TWICE = 2.0 / SPECTRAL
DEPTH = MOMENTS + 1
REACH = 3
SLOT = 4
COUPLINGS = 3
LANES = 128
SUB = 8
SPAN = 32


def lane_iota():
    return lax.broadcasted_iota(jnp.int32, (SUB, LANES), 1)


def turn(value, by):
    by %= LANES
    return pltpu.roll(value, by, 1) if by else value


def swap_major(blocks, sub):
    for s in (4, 2, 1):
        keep = (sub & s) == 0
        for i in range(SUB):
            if i & s == 0:
                a, b = blocks[i], blocks[i + s]
                blocks[i] = jnp.where(keep, a, pltpu.roll(b, s, 0))
                blocks[i + s] = jnp.where(keep, pltpu.roll(a, SUB - s, 0), b)
    return blocks


def prepare_kernel(*refs):
    sources, outputs, held, sems = refs[:4], refs[4:10], refs[10:14], refs[14]
    copies = [pltpu.make_async_copy(a, b, sems.at[n]) for n, (a, b) in enumerate(zip(sources, held))]
    for copy in copies:
        copy.start()
    for copy in copies:
        copy.wait()
    energy_ref, right_ref, class_ref, bond_ref = held
    own_ref, coup_ref, top_ref, bottom_ref, first_ref, last_ref = outputs
    nright, rows, width = right_ref.shape
    lane = lane_iota()
    sub = lax.broadcasted_iota(jnp.int32, (SUB, LANES), 0)
    xtiles, rtiles, inner = rows // SUB, nright // SUB, width // LANES
    zero = jnp.zeros((SUB, LANES), jnp.float32)
    first, last = [zero] * (xtiles + 1), [zero] * (xtiles + 1)

    def strip(v, at, i, block):
        here = (lane >= at) & (lane < at + REACH)
        if i == 0:
            first[v] = jnp.where(here, turn(block, at), first[v])
        if i == inner - 1:
            last[v] = jnp.where(here, turn(block, at + REACH), last[v])

    for half in range(xtiles // 2):
        for i in range(inner):
            lanes = slice(i * LANES, (i + 1) * LANES)
            for t in range(rtiles):
                wide = [
                    right_ref[t * SUB + q, half * 2 * SUB : (half + 1) * 2 * SUB, lanes].astype(jnp.float32)
                    for q in range(SUB)
                ]
                for part in range(2):
                    xt = half * 2 + part
                    turned = swap_major([w[part * SUB : (part + 1) * SUB] for w in wide], sub)
                    for j in range(SUB):
                        x = xt * SUB + j
                        own_ref[x, t * SUB : (t + 1) * SUB, lanes] = turned[j]
                        if x < DEPTH:
                            top_ref[x * nright + t * SUB : x * nright + (t + 1) * SUB, lanes] = turned[j]
                        if x >= rows - DEPTH:
                            at = (x - rows + DEPTH) * nright + t * SUB
                            bottom_ref[at : at + SUB, lanes] = turned[j]
                        strip(xt, t * SPAN + j * SLOT, i, turned[j])
    for xt in range(xtiles):
        here = slice(xt * SUB, (xt + 1) * SUB)
        for i in range(inner):
            lanes = slice(i * LANES, (i + 1) * LANES)
            kinds = class_ref[here, lanes]
            energy = zero
            for level in range(energy_ref.shape[0]):
                energy = jnp.where(kinds == level, energy_ref[level] * TWICE, energy)
            fields = [bond_ref[c, here, lanes].astype(jnp.float32) * TWICE for c in range(2)] + [energy]
            for c in range(COUPLINGS):
                coup_ref[c, here, lanes] = fields[c]
                strip(xtiles, (c * xtiles + xt) * SLOT, i, fields[c])
                at = DEPTH * nright + c * SUB
                if xt == 0:
                    top_ref[at : at + SUB, lanes] = fields[c]
                if xt == xtiles - 1:
                    bottom_ref[at : at + SUB, lanes] = fields[c]
    for v in range(xtiles + 1):
        first_ref[v] = first[v]
        last_ref[v] = last[v]


def prepare(right, classes, energy, bonds):
    nright, rows, width = right.shape
    rim = jax.ShapeDtypeStruct((DEPTH * nright + COUPLINGS * SUB, width), jnp.float32)
    strip = jax.ShapeDtypeStruct((rows // SUB + 1, SUB, LANES), jnp.float32)
    return pl.pallas_call(
        prepare_kernel,
        out_shape=(
            jax.ShapeDtypeStruct((rows, nright, width), jnp.float32),
            jax.ShapeDtypeStruct((COUPLINGS, rows, width), jnp.float32),
            rim,
            rim,
            strip,
            strip,
        ),
        in_specs=[pl.BlockSpec(memory_space=pltpu.HBM)] * 4,
        out_specs=(pl.BlockSpec(memory_space=pltpu.VMEM),) * 6,
        scratch_shapes=[
            pltpu.SMEM(energy.shape, energy.dtype),
            pltpu.VMEM(right.shape, right.dtype),
            pltpu.VMEM(classes.shape, classes.dtype),
            pltpu.VMEM(bonds.shape, bonds.dtype),
            pltpu.SemaphoreType.DMA((4,)),
        ],
        name="prepare",
    )(energy, right, classes, bonds)


def swapped(block, lane, odd):
    low = (lane & 1) == (1 if odd else 0)
    target = jnp.where(low, lane + 1, lane + LANES - 1) & (LANES - 1)
    return jnp.take_along_axis(block, target, axis=1)


def main_kernel(own_ref, coup_ref, lo_ref, hi_ref, before_ref, after_ref, clo_ref, chi_ref, left_ref, out_ref, field, rim, coup, open_bond, acc, spaced):
    rows_x, nright, width = own_ref.shape
    rows = rows_x + 2 * DEPTH
    rtiles, inner, xtiles = nright // SUB, width // LANES, rows_x // SUB
    lane = lane_iota()
    sub = lax.broadcasted_iota(jnp.int32, (SUB, LANES), 0)
    zero = jnp.zeros((SUB, LANES), jnp.float32)

    def lanes_of(i):
        return slice(i * LANES, (i + 1) * LANES)

    for e in range(rows):
        x = (e - DEPTH) % rows_x
        if e < DEPTH:
            before, after = clo_ref[0], clo_ref[2]
        elif e >= DEPTH + rows_x:
            before, after = chi_ref[0], chi_ref[2]
        else:
            before, after = before_ref[x // SUB], after_ref[x // SUB]
        shift = (x % SUB) * SLOT
        rim[0, e] = jnp.where(
            lane % SPAN < REACH,
            turn(after, -shift),
            jnp.where(lane % SPAN >= SPAN - REACH, turn(before, -shift - REACH), zero),
        )
        if e < DEPTH:
            field[0, e] = lo_ref[e * nright : (e + 1) * nright, :]
        elif e >= DEPTH + rows_x:
            at = (e - DEPTH - rows_x) * nright
            field[0, e] = hi_ref[at : at + nright, :]
        else:
            field[0, e] = own_ref[x]

    for g in range(xtiles + 2):
        xt = (g - 1) % xtiles
        if g == 0:
            before, after = clo_ref[1], clo_ref[3]
        elif g == xtiles + 1:
            before, after = chi_ref[1], chi_ref[3]
        else:
            before, after = before_ref[xtiles], after_ref[xtiles]
        whole = []
        for c in range(COUPLINGS):
            at = DEPTH * nright + c * SUB
            if g == 0:
                blocks = [lo_ref[at : at + SUB, lanes_of(i)] for i in range(inner)]
            elif g == xtiles + 1:
                blocks = [hi_ref[at : at + SUB, lanes_of(i)] for i in range(inner)]
            else:
                blocks = [coup_ref[c, xt * SUB : (xt + 1) * SUB, lanes_of(i)] for i in range(inner)]
            shift = (c * xtiles + xt) * SLOT
            blocks.append(
                jnp.where(
                    lane < REACH,
                    turn(after, -shift),
                    jnp.where(lane >= LANES - REACH, turn(before, -shift - REACH), zero),
                )
            )
            if c == 1:
                even = [swapped(b, lane, False) for b in blocks]
                odd = [swapped(b, lane, True) for b in blocks]
                n = len(blocks)
                odd = [
                    jnp.where(lane == 0, odd[(i - 1) % n], jnp.where(lane == LANES - 1, odd[(i + 1) % n], odd[i]))
                    for i in range(n)
                ]
                blocks = [
                    jnp.where(((lane + sub) & 1) == 0, b, jnp.where((sub & 1) == 1, o, v))
                    for b, o, v in zip(blocks, odd, even)
                ]
            edge = blocks[inner]
            edge = edge + turn(edge, LANES // 2)
            blocks[inner] = edge + turn(edge, LANES // 4)
            whole.append(blocks)
        for s in range(SUB):
            e = (g - 1) * SUB + s + DEPTH
            if 0 <= e < rows:
                for c in range(COUPLINGS):
                    for i in range(inner + 1):
                        wide = jnp.broadcast_to(whole[c][i][s : s + 1], (SUB, LANES))
                        coup[e, c, :, lanes_of(i)] = wide
                        if c == 0 and i < inner:
                            shown = (wide > 0.0).astype(jnp.float32)
                            open_bond[e, :, lanes_of(i)] = jnp.concatenate([shown, shown], axis=0).astype(jnp.bfloat16)

    acc[...] = jnp.zeros_like(acc)

    def load(k, row, t, i):
        if i == inner:
            return rim[k, row]
        return field[k, row, t * SUB : (t + 1) * SUB, lanes_of(i)]

    def coupling(c, row, i):
        return coup[row, c, :, lanes_of(i)]

    where = [(t, i) for t in range(rtiles) for i in range(inner)] + [(0, inner)]

    def partners(here, odd):
        moved = {at: swapped(value, lane, odd) for at, value in here.items()}
        if not odd:
            return moved
        edge = moved[0, inner]
        start, end = lane == 0, lane == LANES - 1
        result, fill = {}, edge
        for t in range(rtiles):
            outer = turn(edge, -t * SPAN)
            for i in range(inner):
                left = moved[t, i - 1] if i else outer
                right = moved[t, i + 1] if i < inner - 1 else outer
                result[t, i] = jnp.where(start, left, jnp.where(end, right, moved[t, i]))
            facing = turn(jnp.where(lane < LANES // 2, moved[t, inner - 1], moved[t, 0]), t * SPAN)
            fill = jnp.where((lane == t * SPAN) | (lane == (t * SPAN - 1) % LANES), facing, fill)
        result[0, inner] = fill
        return result

    def advance(k, row, odd):
        here = {at: load(k, row, *at) for at in where}
        turned = partners(here, odd)
        east = [coupling(0, row, i) for i in range(inner + 1)]
        west = [coupling(0, row - 1, i) for i in range(inner + 1)]
        vertical = [coupling(1, row, i) for i in range(inner + 1)]
        site = [coupling(2, row, i) for i in range(inner + 1)] if k else None
        sign = jnp.where((lane & 1) == (1 if odd else 0), 1.0 / TWICE, -1.0 / TWICE)
        new = {}
        for t, i in where:
            beside = east[i] * load(k, row + 1, t, i) + west[i] * load(k, row - 1, t, i)
            across = vertical[i] * turned[t, i]
            if k == 0:
                new[t, i] = sign * (0.5 * beside - across)
            else:
                image = site[i] * here[t, i] - beside - across
                new[t, i] = 0.5 * image if k == 1 else image - load(k - 1, row, t, i)
        for t, i in where:
            if i == inner:
                rim[k + 1, row] = new[t, i]
            else:
                field[k + 1, row, t * SUB : (t + 1) * SUB, lanes_of(i)] = new[t, i]

    def contract(row, below=True, above=True):
        parts = []
        for t in range(rtiles * MOMENTS):
            k, q = divmod(t, rtiles)
            parts.append(field[k + 1, row, q * SUB : (q + 1) * SUB, :])
        value = jnp.concatenate(parts, axis=0)
        high = value.astype(jnp.bfloat16)
        low = (value - high.astype(jnp.float32)).astype(jnp.bfloat16)
        sides = []
        for there, bond, wanted in ((row - 1, row - 1, below), (row + 1, row, above)):
            for q in range(left_ref.shape[1] // (2 * SUB)):
                if wanted:
                    sides.append(left_ref[there - DEPTH, q * 2 * SUB : (q + 1) * 2 * SUB, :] * open_bond[bond])
                else:
                    sides.append(jnp.zeros((2 * SUB, width), jnp.bfloat16))
        block = jnp.concatenate(sides, axis=0)
        acc[...] += lax.dot_general(
            jnp.concatenate([high, low], axis=1),
            jnp.concatenate([block, block], axis=1),
            (((1,), (1,)), ((), ())),
            preferred_element_type=jnp.float32,
        )

    lag = 2 * MOMENTS - 1
    lead = DEPTH + 1 + lag
    for front in range(1, lead):
        if front >= lead - 2:
            contract(front - lag, below=False)
        for k in reversed(range(MOMENTS)):
            if front >= 3 * k + 1:
                advance(k, front - 2 * k, front % 2 == 1)

    def both(n, _):
        for part in range(2):
            front = lead + 2 * n + part
            contract(front - lag)
            for k in reversed(range(MOMENTS)):
                advance(k, front - 2 * k, (lead + part) % 2 == 1)
        return 0

    lax.fori_loop(0, rows_x // 2 - 1, both, 0)
    end = rows_x + DEPTH
    advance(MOMENTS - 1, end, end % 2 == 1)
    contract(end - 1, above=False)
    contract(end, above=False)
    groups, _, flat = out_ref.shape
    owned = flat // nright
    both_sides = acc[...].T
    half = both_sides.shape[0] // 2
    total = both_sides[:half] - both_sides[half:]
    for k in range(MOMENTS):
        spaced[:, 0:nright] = total[:, k * nright : (k + 1) * nright]
        rows_of = [spaced[pl.ds(q, groups, stride=owned), :] for q in range(owned)]
        out_ref[:, k, :] = jnp.concatenate([r[:, 0:nright] for r in rows_of], axis=1)


def finish_kernel(scale, order_ref, blocks_ref, out_ref, total):
    total[...] = jnp.sum(blocks_ref[...], axis=0) * scale
    _, owned, nright = out_ref.shape
    for j in range(MOMENTS):
        row = total[pl.ds(order_ref[j], 1), :]
        for q in range(owned):
            out_ref[j, q : q + 1, :] = row[:, q * nright : (q + 1) * nright]


def moments_of_tile(own, coup, lo, hi, before, after, clo, chi, left, groups):
    rows_x, nright, width = own.shape
    rows = rows_x + 2 * DEPTH + MOMENTS
    nleft = left.shape[1]
    return pl.pallas_call(
        main_kernel,
        out_shape=jax.ShapeDtypeStruct((groups, MOMENTS, nleft // groups * nright), jnp.float32),
        in_specs=[pl.BlockSpec(memory_space=pltpu.VMEM)] * 9,
        out_specs=pl.BlockSpec(memory_space=pltpu.VMEM),
        scratch_shapes=[
            pltpu.VMEM((MOMENTS + 1, rows, nright, width), jnp.float32),
            pltpu.VMEM((MOMENTS + 1, rows, SUB, LANES), jnp.float32),
            pltpu.VMEM((rows, COUPLINGS, SUB, width + LANES), jnp.float32),
            pltpu.VMEM((rows, 2 * SUB, width), jnp.bfloat16),
            pltpu.VMEM((MOMENTS * nright, 2 * nleft), jnp.float32),
            pltpu.VMEM((nleft, LANES), jnp.float32),
        ],
        compiler_params=pltpu.CompilerParams(vmem_limit_bytes=28 << 20),
        name="chebyshev_moments",
    )(own, coup, lo, hi, before, after, clo, chi, left)


def ring(axis, by):
    size = lax.axis_size(axis)
    return [(i, (i + by) % size) for i in range(size)]


def shards(right_vectors, left_vectors, classes, class_energy, bond_mask_grid, order):
    rows_x, rows_y = classes.shape
    nright, nleft = right_vectors.shape[0], left_vectors.shape[0]
    nsx, nsy = lax.axis_size("sx"), lax.axis_size("sy")
    owned = nleft // nsy

    own, coup, top, bottom, first, last = prepare(right_vectors, classes, class_energy, bond_mask_grid)
    with jax.named_scope("halo_y"):
        before = lax.ppermute(last, "sy", ring("sy", 1))
        after = lax.ppermute(first, "sy", ring("sy", -1))
    with jax.named_scope("halo_x"):
        lo = lax.ppermute(bottom, "sx", ring("sx", 1))
        hi = lax.ppermute(top, "sx", ring("sx", -1))
    with jax.named_scope("halo_corner"):
        up = jnp.concatenate([before[-2:], after[-2:]], axis=0)
        down = jnp.concatenate([before[:1], before[-1:], after[:1], after[-1:]], axis=0)
        clo = lax.ppermute(up, "sx", ring("sx", 1))
        chi = lax.ppermute(down, "sx", ring("sx", -1))
    left = left_vectors.transpose(1, 0, 2)
    tile = moments_of_tile(own, coup, lo, hi, before, after, clo, chi, left, nsy)
    with jax.named_scope("reduce_sy"):
        mine = jnp.sum(lax.all_to_all(tile, "sy", 0, 0), axis=0)
    with jax.named_scope("reduce_sx"):
        shares = lax.all_to_all(jnp.broadcast_to(mine[None], (nsx,) + mine.shape), "sx", 0, 0)
    sites = rows_x * rows_y * nsx * nsy
    return pl.pallas_call(
        functools.partial(finish_kernel, -HALF_ROOT / sites**0.5),
        out_shape=jax.ShapeDtypeStruct((MOMENTS, owned, nright), jnp.float32),
        in_specs=[pl.BlockSpec(memory_space=pltpu.SMEM), pl.BlockSpec(memory_space=pltpu.VMEM)],
        out_specs=pl.BlockSpec(memory_space=pltpu.VMEM),
        scratch_shapes=[pltpu.VMEM(mine.shape, jnp.float32)],
        compiler_params=pltpu.CompilerParams(vmem_limit_bytes=4 << 20),
        name="finish",
    )(order, shares)


def solution(mesh):
    in_specs = (
        P(None, "sx", "sy"),
        P(None, "sx", "sy"),
        P("sx", "sy"),
        P(),
        P(None, "sx", "sy"),
        P(),
    )
    out_specs = P(None, "sy", None)
    return jax.shard_map(shards, mesh=mesh, in_specs=in_specs, out_specs=out_specs, check_vma=False)
```

```python
import functools

import jax
import jax.numpy as jnp
from jax import lax
from jax.experimental import pallas as pl
from jax.experimental.pallas import tpu as pltpu
from jax.sharding import PartitionSpec as P

MOMENTS = 5
HALF_ROOT = 0.8660254037844386
SPECTRAL = 4.6
TWICE = 2.0 / SPECTRAL
DEPTH = MOMENTS + 1
REACH = 3
SLOT = 4
COUPLINGS = 3
LANES = 128
SUB = 8
SPAN = 32


def lane_iota():
    return lax.broadcasted_iota(jnp.int32, (SUB, LANES), 1)


def turn(value, by):
    by %= LANES
    return pltpu.roll(value, by, 1) if by else value


def swap_major(blocks, sub):
    for s in (4, 2, 1):
        keep = (sub & s) == 0
        for i in range(SUB):
            if i & s == 0:
                a, b = blocks[i], blocks[i + s]
                blocks[i] = jnp.where(keep, a, pltpu.roll(b, s, 0))
                blocks[i + s] = jnp.where(keep, pltpu.roll(a, SUB - s, 0), b)
    return blocks


def prepare_kernel(*refs):
    sources, outputs, held, sems = refs[:4], refs[4:10], refs[10:14], refs[14]
    copies = [pltpu.make_async_copy(a, b, sems.at[n]) for n, (a, b) in enumerate(zip(sources, held))]
    for copy in copies:
        copy.start()
    for copy in copies:
        copy.wait()
    energy_ref, right_ref, class_ref, bond_ref = held
    own_ref, coup_ref, top_ref, bottom_ref, first_ref, last_ref = outputs
    nright, rows, width = right_ref.shape
    lane = lane_iota()
    sub = lax.broadcasted_iota(jnp.int32, (SUB, LANES), 0)
    xtiles, rtiles, inner = rows // SUB, nright // SUB, width // LANES
    zero = jnp.zeros((SUB, LANES), jnp.float32)
    first, last = [zero] * (xtiles + 1), [zero] * (xtiles + 1)

    def strip(v, at, i, block):
        here = (lane >= at) & (lane < at + REACH)
        if i == 0:
            first[v] = jnp.where(here, turn(block, at), first[v])
        if i == inner - 1:
            last[v] = jnp.where(here, turn(block, at + REACH), last[v])

    for half in range(xtiles // 2):
        for i in range(inner):
            lanes = slice(i * LANES, (i + 1) * LANES)
            for t in range(rtiles):
                wide = [
                    right_ref[t * SUB + q, half * 2 * SUB : (half + 1) * 2 * SUB, lanes].astype(jnp.float32)
                    for q in range(SUB)
                ]
                for part in range(2):
                    xt = half * 2 + part
                    turned = swap_major([w[part * SUB : (part + 1) * SUB] for w in wide], sub)
                    for j in range(SUB):
                        x = xt * SUB + j
                        own_ref[x, t * SUB : (t + 1) * SUB, lanes] = turned[j]
                        if x < DEPTH:
                            top_ref[x * nright + t * SUB : x * nright + (t + 1) * SUB, lanes] = turned[j]
                        if x >= rows - DEPTH:
                            at = (x - rows + DEPTH) * nright + t * SUB
                            bottom_ref[at : at + SUB, lanes] = turned[j]
                        strip(xt, t * SPAN + j * SLOT, i, turned[j])
    for xt in range(xtiles):
        here = slice(xt * SUB, (xt + 1) * SUB)
        for i in range(inner):
            lanes = slice(i * LANES, (i + 1) * LANES)
            kinds = class_ref[here, lanes]
            energy = zero
            for level in range(energy_ref.shape[0]):
                energy = jnp.where(kinds == level, energy_ref[level] * TWICE, energy)
            fields = [bond_ref[c, here, lanes].astype(jnp.float32) * TWICE for c in range(2)] + [energy]
            for c in range(COUPLINGS):
                coup_ref[c, here, lanes] = fields[c]
                strip(xtiles, (c * xtiles + xt) * SLOT, i, fields[c])
                at = DEPTH * nright + c * SUB
                if xt == 0:
                    top_ref[at : at + SUB, lanes] = fields[c]
                if xt == xtiles - 1:
                    bottom_ref[at : at + SUB, lanes] = fields[c]
    for v in range(xtiles + 1):
        first_ref[v] = first[v]
        last_ref[v] = last[v]


def prepare(right, classes, energy, bonds):
    nright, rows, width = right.shape
    rim = jax.ShapeDtypeStruct((DEPTH * nright + COUPLINGS * SUB, width), jnp.float32)
    strip = jax.ShapeDtypeStruct((rows // SUB + 1, SUB, LANES), jnp.float32)
    return pl.pallas_call(
        prepare_kernel,
        out_shape=(
            jax.ShapeDtypeStruct((rows, nright, width), jnp.float32),
            jax.ShapeDtypeStruct((COUPLINGS, rows, width), jnp.float32),
            rim,
            rim,
            strip,
            strip,
        ),
        in_specs=[pl.BlockSpec(memory_space=pltpu.HBM)] * 4,
        out_specs=(pl.BlockSpec(memory_space=pltpu.VMEM),) * 6,
        scratch_shapes=[
            pltpu.SMEM(energy.shape, energy.dtype),
            pltpu.VMEM(right.shape, right.dtype),
            pltpu.VMEM(classes.shape, classes.dtype),
            pltpu.VMEM(bonds.shape, bonds.dtype),
            pltpu.SemaphoreType.DMA((4,)),
        ],
        name="prepare",
    )(energy, right, classes, bonds)


def swapped(block, lane, odd):
    low = (lane & 1) == (1 if odd else 0)
    target = jnp.where(low, lane + 1, lane + LANES - 1) & (LANES - 1)
    return jnp.take_along_axis(block, target, axis=1)


def coupling_rows(blocks_of, strips_of, groups, xtiles, inner, coup, open_bond, rows):
    lane = lane_iota()
    sub = lax.broadcasted_iota(jnp.int32, (SUB, LANES), 0)
    zero = jnp.zeros((SUB, LANES), jnp.float32)
    for g in groups:
        xt = (g - 1) % xtiles
        before, after = strips_of(g)
        whole = []
        for c in range(COUPLINGS):
            blocks = blocks_of(g, c, xt)
            shift = (c * xtiles + xt) * SLOT
            blocks.append(
                jnp.where(
                    lane < REACH,
                    turn(after, -shift),
                    jnp.where(lane >= LANES - REACH, turn(before, -shift - REACH), zero),
                )
            )
            if c == 1:
                even = [swapped(b, lane, False) for b in blocks]
                odd = [swapped(b, lane, True) for b in blocks]
                n = len(blocks)
                odd = [
                    jnp.where(lane == 0, odd[(i - 1) % n], jnp.where(lane == LANES - 1, odd[(i + 1) % n], odd[i]))
                    for i in range(n)
                ]
                blocks = [
                    jnp.where(((lane + sub) & 1) == 0, b, jnp.where((sub & 1) == 1, o, v))
                    for b, o, v in zip(blocks, odd, even)
                ]
            edge = blocks[inner]
            edge = edge + turn(edge, LANES // 2)
            blocks[inner] = edge + turn(edge, LANES // 4)
            whole.append(blocks)
        for s in range(SUB):
            e = (g - 1) * SUB + s + DEPTH
            if 0 <= e < rows:
                for c in range(COUPLINGS):
                    for i in range(inner + 1):
                        wide = jnp.broadcast_to(whole[c][i][s : s + 1], (SUB, LANES))
                        coup[e, c, :, i * LANES : (i + 1) * LANES] = wide
                        if c == 0 and i < inner:
                            shown = (wide > 0.0).astype(jnp.float32)
                            open_bond[e, :, i * LANES : (i + 1) * LANES] = jnp.concatenate(
                                [shown, shown], axis=0
                            ).astype(jnp.bfloat16)


def rim_row(before, after, x):
    lane = lane_iota()
    shift = (x % SUB) * SLOT
    return jnp.where(
        lane % SPAN < REACH,
        turn(after, -shift),
        jnp.where(lane % SPAN >= SPAN - REACH, turn(before, -shift - REACH), jnp.zeros((SUB, LANES), jnp.float32)),
    )


def stepper(field, rim, coup, open_bond, acc, left_ref):
    nright, width = field.shape[2:]
    rtiles, inner = nright // SUB, width // LANES
    rows_x = left_ref.shape[0]
    lane = lane_iota()

    def lanes_of(i):
        return slice(i * LANES, (i + 1) * LANES)

    def load(k, row, t, i):
        if i == inner:
            return rim[k, row]
        return field[k, row, t * SUB : (t + 1) * SUB, lanes_of(i)]

    def coupling(c, row, i):
        return coup[row, c, :, lanes_of(i)]

    where = [(t, i) for t in range(rtiles) for i in range(inner)] + [(0, inner)]

    def partners(here, odd):
        moved = {at: swapped(value, lane, odd) for at, value in here.items()}
        if not odd:
            return moved
        edge = moved[0, inner]
        start, end = lane == 0, lane == LANES - 1
        result, fill = {}, edge
        for t in range(rtiles):
            outer = turn(edge, -t * SPAN)
            for i in range(inner):
                left = moved[t, i - 1] if i else outer
                right = moved[t, i + 1] if i < inner - 1 else outer
                result[t, i] = jnp.where(start, left, jnp.where(end, right, moved[t, i]))
            facing = turn(jnp.where(lane < LANES // 2, moved[t, inner - 1], moved[t, 0]), t * SPAN)
            fill = jnp.where((lane == t * SPAN) | (lane == (t * SPAN - 1) % LANES), facing, fill)
        result[0, inner] = fill
        return result

    def advance(k, row, odd):
        here = {at: load(k, row, *at) for at in where}
        turned = partners(here, odd)
        east = [coupling(0, row, i) for i in range(inner + 1)]
        west = [coupling(0, row - 1, i) for i in range(inner + 1)]
        vertical = [coupling(1, row, i) for i in range(inner + 1)]
        site = [coupling(2, row, i) for i in range(inner + 1)] if k else None
        sign = jnp.where((lane & 1) == (1 if odd else 0), 1.0 / TWICE, -1.0 / TWICE)
        new = {}
        for t, i in where:
            beside = east[i] * load(k, row + 1, t, i) + west[i] * load(k, row - 1, t, i)
            across = vertical[i] * turned[t, i]
            if k == 0:
                new[t, i] = sign * (0.5 * beside - across)
            else:
                image = site[i] * here[t, i] - beside - across
                new[t, i] = 0.5 * image if k == 1 else image - load(k - 1, row, t, i)
        for t, i in where:
            if i == inner:
                rim[k + 1, row] = new[t, i]
            else:
                field[k + 1, row, t * SUB : (t + 1) * SUB, lanes_of(i)] = new[t, i]

    def contract(row, below=True, above=True):
        parts = []
        for t in range(rtiles * MOMENTS):
            k, q = divmod(t, rtiles)
            parts.append(field[k + 1, row, q * SUB : (q + 1) * SUB, :])
        value = jnp.concatenate(parts, axis=0)
        high = value.astype(jnp.bfloat16)
        low = (value - high.astype(jnp.float32)).astype(jnp.bfloat16)
        sides = []
        for there, bond, wanted in ((row - 1, row - 1, below), (row + 1, row, above)):
            for q in range(left_ref.shape[1] // (2 * SUB)):
                if wanted:
                    sides.append(left_ref[there - DEPTH, q * 2 * SUB : (q + 1) * 2 * SUB, :] * open_bond[bond])
                else:
                    sides.append(jnp.zeros((2 * SUB, width), jnp.bfloat16))
        block = jnp.concatenate(sides, axis=0)
        acc[...] += lax.dot_general(
            jnp.concatenate([high, low], axis=1),
            jnp.concatenate([block, block], axis=1),
            (((1,), (1,)), ((), ())),
            preferred_element_type=jnp.float32,
        )

    return advance, contract


def interior_kernel(own_ref, coup_ref, before_ref, after_ref, left_ref, acc, edge_field, edge_rim, field, rim, coup, open_bond):
    rows_x, nright, width = own_ref.shape
    rows = rows_x + 2 * DEPTH
    inner, xtiles = width // LANES, rows_x // SUB
    for x in range(rows_x):
        rim[0, x + DEPTH] = rim_row(before_ref[x // SUB], after_ref[x // SUB], x)
        field[0, x + DEPTH] = own_ref[x]

    def blocks_of(g, c, xt):
        return [coup_ref[c, xt * SUB : (xt + 1) * SUB, i * LANES : (i + 1) * LANES] for i in range(inner)]

    def strips_of(g):
        return before_ref[xtiles], after_ref[xtiles]

    coupling_rows(blocks_of, strips_of, range(1, xtiles + 1), xtiles, inner, coup, open_bond, rows)
    acc[...] = jnp.zeros_like(acc)
    advance, contract = stepper(field, rim, coup, open_bond, acc, left_ref)

    first, last = DEPTH + 1, DEPTH + rows_x - 2
    lag = 2 * MOMENTS - 1

    def front_step(front):
        if first + MOMENTS - 1 <= front - lag <= last - MOMENTS + 1:
            contract(front - lag)
        for k in reversed(range(MOMENTS)):
            if first + 3 * k <= front <= last + k:
                advance(k, front - 2 * k, front % 2 == 1)

    lead = first + MOMENTS - 1 + lag
    pairs = (last - lead + 1) // 2
    for front in range(first, lead):
        front_step(front)

    def both(n, _):
        for part in range(2):
            front = lead + 2 * n + part
            contract(front - lag)
            for k in reversed(range(MOMENTS)):
                advance(k, front - 2 * k, (lead + part) % 2 == 1)
        return 0

    lax.fori_loop(0, pairs, both, 0)
    for front in range(lead + 2 * pairs, last - MOMENTS + 1 + lag + 1):
        front_step(front)
    for k in range(MOMENTS - 1):
        for side, at in enumerate((first, last - MOMENTS + 1)):
            edge_field[side, k] = field[k + 1, at : at + MOMENTS]
            edge_rim[side, k] = rim[k + 1, at : at + MOMENTS]


def border_kernel(ends_ref, coup_ref, lo_ref, hi_ref, before_ref, after_ref, left_ref, part_ref, edge_field, edge_rim, out_ref, field, rim, coup, open_bond, acc, spaced):
    nright, width = ends_ref.shape[1:]
    rows_x = left_ref.shape[0]
    rows = rows_x + 2 * DEPTH
    inner, xtiles = width // LANES, rows_x // SUB
    base = DEPTH * nright + COUPLINGS * SUB

    def corner(ref, which, v):
        return ref[base + which * SUB : base + (which + 1) * SUB, v * LANES : (v + 1) * LANES]

    for e in range(DEPTH):
        rim[0, e] = rim_row(corner(lo_ref, 0, 0), corner(lo_ref, 1, 0), e - DEPTH)
        field[0, e] = lo_ref[e * nright : (e + 1) * nright, :]
        rim[0, e + DEPTH + rows_x] = rim_row(corner(hi_ref, 0, 0), corner(hi_ref, 1, 0), e)
        field[0, e + DEPTH + rows_x] = hi_ref[e * nright : (e + 1) * nright, :]
    for n, x in enumerate((0, 1, rows_x - 2, rows_x - 1)):
        rim[0, x + DEPTH] = rim_row(before_ref[x // SUB], after_ref[x // SUB], x)
        field[0, x + DEPTH] = ends_ref[n]

    def blocks_of(g, c, xt):
        at = DEPTH * nright + c * SUB
        lanes = [slice(i * LANES, (i + 1) * LANES) for i in range(inner)]
        if g == 0:
            return [lo_ref[at : at + SUB, i] for i in lanes]
        if g == xtiles + 1:
            return [hi_ref[at : at + SUB, i] for i in lanes]
        return [coup_ref[c, xt * SUB : (xt + 1) * SUB, i] for i in lanes]

    def strips_of(g):
        if g == 0:
            return corner(lo_ref, 0, 1), corner(lo_ref, 1, 1)
        if g == xtiles + 1:
            return corner(hi_ref, 0, 1), corner(hi_ref, 1, 1)
        return before_ref[xtiles], after_ref[xtiles]

    coupling_rows(blocks_of, strips_of, (0, 1, xtiles, xtiles + 1), xtiles, inner, coup, open_bond, rows)
    first, last = DEPTH + 1, DEPTH + rows_x - 2
    for k in range(MOMENTS - 1):
        for side, at in enumerate((first, last - MOMENTS + 1)):
            field[k + 1, at : at + MOMENTS] = edge_field[side, k]
            rim[k + 1, at : at + MOMENTS] = edge_rim[side, k]
    acc[...] = part_ref[...]
    advance, contract = stepper(field, rim, coup, open_bond, acc, left_ref)

    for front in range(1, DEPTH + 3 * (MOMENTS - 1) + 1):
        for k in reversed(range(MOMENTS)):
            if 3 * k + 1 <= front <= 3 * k + DEPTH:
                row = front - 2 * k
                advance(k, row, row % 2 == 1)
                advance(k, rows - 1 - row, (rows - 1 - row) % 2 == 1)
    for n in range(DEPTH):
        for row in (DEPTH - 1 + n, rows - DEPTH - n):
            contract(row, 0 <= row - 1 - DEPTH < rows_x, 0 <= row + 1 - DEPTH < rows_x)

    groups, _, flat = out_ref.shape
    owned = flat // nright
    both_sides = acc[...].T
    half = both_sides.shape[0] // 2
    total = both_sides[:half] - both_sides[half:]
    for k in range(MOMENTS):
        spaced[:, 0:nright] = total[:, k * nright : (k + 1) * nright]
        rows_of = [spaced[pl.ds(q, groups, stride=owned), :] for q in range(owned)]
        out_ref[:, k, :] = jnp.concatenate([r[:, 0:nright] for r in rows_of], axis=1)


def finish_kernel(scale, order_ref, blocks_ref, out_ref, total):
    total[...] = jnp.sum(blocks_ref[...], axis=0) * scale
    _, owned, nright = out_ref.shape
    for j in range(MOMENTS):
        row = total[pl.ds(order_ref[j], 1), :]
        for q in range(owned):
            out_ref[j, q : q + 1, :] = row[:, q * nright : (q + 1) * nright]


def vmem_call(kernel, name, out_shape, scratch, flops, *args):
    several = isinstance(out_shape, tuple)
    spec = pl.BlockSpec(memory_space=pltpu.VMEM)
    return pl.pallas_call(
        kernel,
        out_shape=out_shape,
        in_specs=[spec] * len(args),
        out_specs=(spec,) * len(out_shape) if several else spec,
        scratch_shapes=scratch,
        compiler_params=pltpu.CompilerParams(vmem_limit_bytes=28 << 20),
        cost_estimate=pl.CostEstimate(flops=flops, bytes_accessed=1 << 22, transcendentals=0),
        name=name,
    )(*args)


def scratch_of(rows_x, nright, width):
    rows = rows_x + 2 * DEPTH
    return [
        pltpu.VMEM((MOMENTS + 1, rows, nright, width), jnp.float32),
        pltpu.VMEM((MOMENTS + 1, rows, SUB, LANES), jnp.float32),
        pltpu.VMEM((rows, COUPLINGS, SUB, width + LANES), jnp.float32),
        pltpu.VMEM((rows, 2 * SUB, width), jnp.bfloat16),
    ]


def ring(axis, by):
    size = lax.axis_size(axis)
    return [(i, (i + by) % size) for i in range(size)]


def shards(right_vectors, left_vectors, classes, class_energy, bond_mask_grid, order):
    rows_x, rows_y = classes.shape
    nright, nleft = right_vectors.shape[0], left_vectors.shape[0]
    nsx, nsy = lax.axis_size("sx"), lax.axis_size("sy")
    owned = nleft // nsy

    own, coup, top, bottom, first, last = prepare(right_vectors, classes, class_energy, bond_mask_grid)
    with jax.named_scope("halo_y"):
        before = lax.ppermute(last, "sy", ring("sy", 1))
        after = lax.ppermute(first, "sy", ring("sy", -1))
    with jax.named_scope("halo_x"):
        def with_corners(rows, v):
            corners = [jnp.concatenate([part[v], part[-1]], axis=1) for part in (before, after)]
            return jnp.concatenate([rows] + corners, axis=0)

        lo = lax.ppermute(with_corners(bottom, -2), "sx", ring("sx", 1))
        hi = lax.ppermute(with_corners(top, 0), "sx", ring("sx", -1))
    left = left_vectors.transpose(1, 0, 2)
    f32 = jnp.float32
    part, edge_field, edge_rim = vmem_call(
        interior_kernel,
        "interior",
        (
            jax.ShapeDtypeStruct((MOMENTS * nright, 2 * nleft), f32),
            jax.ShapeDtypeStruct((2, MOMENTS - 1, MOMENTS, nright, rows_y), f32),
            jax.ShapeDtypeStruct((2, MOMENTS - 1, MOMENTS, SUB, LANES), f32),
        ),
        scratch_of(rows_x, nright, rows_y),
        1 << 33,
        own, coup, before, after, left,
    )
    ends = jnp.concatenate([own[:2], own[-2:]], axis=0)
    tile = vmem_call(
        border_kernel,
        "border",
        jax.ShapeDtypeStruct((nsy, MOMENTS, owned * nright), f32),
        scratch_of(rows_x, nright, rows_y)
        + [pltpu.VMEM((MOMENTS * nright, 2 * nleft), f32), pltpu.VMEM((nleft, LANES), f32)],
        1 << 32,
        ends, coup, lo, hi, before, after, left, part, edge_field, edge_rim,
    )
    with jax.named_scope("reduce_sy"):
        mine = jnp.sum(lax.all_to_all(tile, "sy", 0, 0), axis=0)
    with jax.named_scope("reduce_sx"):
        shares = lax.all_to_all(jnp.broadcast_to(mine[None], (nsx,) + mine.shape), "sx", 0, 0)
    sites = rows_x * rows_y * nsx * nsy
    return pl.pallas_call(
        functools.partial(finish_kernel, -HALF_ROOT / sites**0.5),
        out_shape=jax.ShapeDtypeStruct((MOMENTS, owned, nright), jnp.float32),
        in_specs=[pl.BlockSpec(memory_space=pltpu.SMEM), pl.BlockSpec(memory_space=pltpu.VMEM)],
        out_specs=pl.BlockSpec(memory_space=pltpu.VMEM),
        scratch_shapes=[pltpu.VMEM(mine.shape, jnp.float32)],
        compiler_params=pltpu.CompilerParams(vmem_limit_bytes=4 << 20),
        name="finish",
    )(order, shares)


def solution(mesh):
    in_specs = (
        P(None, "sx", "sy"),
        P(None, "sx", "sy"),
        P("sx", "sy"),
        P(),
        P(None, "sx", "sy"),
        P(),
    )
    out_specs = P(None, "sy", None)
    return jax.shard_map(shards, mesh=mesh, in_specs=in_specs, out_specs=out_specs, check_vma=False)
```

```python
import functools

import jax
import jax.numpy as jnp
from jax import lax
from jax.experimental import pallas as pl
from jax.experimental.pallas import tpu as pltpu
from jax.sharding import PartitionSpec as P

MOMENTS = 5
HALF_ROOT = 0.8660254037844386
SPECTRAL = 4.6
TWICE = 2.0 / SPECTRAL
DEPTH = MOMENTS + 1
REACH = 3
SLOT = 4
COUPLINGS = 3
LANES = 128
SUB = 8
SPAN = 32


def lane_iota():
    return lax.broadcasted_iota(jnp.int32, (SUB, LANES), 1)


def turn(value, by):
    by %= LANES
    return pltpu.roll(value, by, 1) if by else value


def swap_major(blocks, sub):
    for s in (4, 2, 1):
        keep = (sub & s) == 0
        for i in range(SUB):
            if i & s == 0:
                a, b = blocks[i], blocks[i + s]
                blocks[i] = jnp.where(keep, a, pltpu.roll(b, s, 0))
                blocks[i + s] = jnp.where(keep, pltpu.roll(a, SUB - s, 0), b)
    return blocks


def prepare_kernel(*refs):
    sources, outputs, held, sems = refs[:4], refs[4:8], refs[8:12], refs[12]
    copies = [pltpu.make_async_copy(a, b, sems.at[n]) for n, (a, b) in enumerate(zip(sources, held))]
    for copy in copies:
        copy.start()
    for copy in copies:
        copy.wait()
    energy_ref, right_ref, class_ref, bond_ref = held
    own_ref, coup_ref, rows_ref, strips_ref = outputs
    top_at, first_at = lax.axis_index("sx") % 2, lax.axis_index("sy") % 2
    nright, rows, width = right_ref.shape
    lane = lane_iota()
    sub = lax.broadcasted_iota(jnp.int32, (SUB, LANES), 0)
    xtiles, rtiles, inner = rows // SUB, nright // SUB, width // LANES
    zero = jnp.zeros((SUB, LANES), jnp.float32)
    first, last = [zero] * (xtiles + 1), [zero] * (xtiles + 1)

    def strip(v, at, i, block):
        here = (lane >= at) & (lane < at + REACH)
        if i == 0:
            first[v] = jnp.where(here, turn(block, at), first[v])
        if i == inner - 1:
            last[v] = jnp.where(here, turn(block, at + REACH), last[v])

    for half in range(xtiles // 2):
        for i in range(inner):
            lanes = slice(i * LANES, (i + 1) * LANES)
            for t in range(rtiles):
                wide = [
                    right_ref[t * SUB + q, half * 2 * SUB : (half + 1) * 2 * SUB, lanes].astype(jnp.float32)
                    for q in range(SUB)
                ]
                for part in range(2):
                    xt = half * 2 + part
                    turned = swap_major([w[part * SUB : (part + 1) * SUB] for w in wide], sub)
                    for j in range(SUB):
                        x = xt * SUB + j
                        own_ref[x, t * SUB : (t + 1) * SUB, lanes] = turned[j]
                        if x < DEPTH:
                            rows_ref[top_at, x * nright + t * SUB : x * nright + (t + 1) * SUB, lanes] = turned[j]
                        if x >= rows - DEPTH:
                            at = (x - rows + DEPTH) * nright + t * SUB
                            rows_ref[1 - top_at, at : at + SUB, lanes] = turned[j]
                        strip(xt, t * SPAN + j * SLOT, i, turned[j])
    for xt in range(xtiles):
        here = slice(xt * SUB, (xt + 1) * SUB)
        for i in range(inner):
            lanes = slice(i * LANES, (i + 1) * LANES)
            kinds = class_ref[here, lanes]
            energy = zero
            for level in range(energy_ref.shape[0]):
                energy = jnp.where(kinds == level, energy_ref[level] * TWICE, energy)
            fields = [bond_ref[c, here, lanes].astype(jnp.float32) * TWICE for c in range(2)] + [energy]
            for c in range(COUPLINGS):
                coup_ref[c, here, lanes] = fields[c]
                strip(xtiles, (c * xtiles + xt) * SLOT, i, fields[c])
                at = DEPTH * nright + c * SUB
                if xt == 0:
                    rows_ref[top_at, at : at + SUB, lanes] = fields[c]
                if xt == xtiles - 1:
                    rows_ref[1 - top_at, at : at + SUB, lanes] = fields[c]
    for v in range(xtiles + 1):
        strips_ref[first_at, v] = first[v]
        strips_ref[1 - first_at, v] = last[v]


def prepare(right, classes, energy, bonds):
    nright, rows, width = right.shape
    rim = jax.ShapeDtypeStruct((2, DEPTH * nright + COUPLINGS * SUB, width), jnp.float32)
    strip = jax.ShapeDtypeStruct((2, rows // SUB + 1, SUB, LANES), jnp.float32)
    return pl.pallas_call(
        prepare_kernel,
        out_shape=(
            jax.ShapeDtypeStruct((rows, nright, width), jnp.float32),
            jax.ShapeDtypeStruct((COUPLINGS, rows, width), jnp.float32),
            rim,
            strip,
        ),
        in_specs=[pl.BlockSpec(memory_space=pltpu.HBM)] * 4,
        out_specs=(pl.BlockSpec(memory_space=pltpu.VMEM),) * 4,
        scratch_shapes=[
            pltpu.SMEM(energy.shape, energy.dtype),
            pltpu.VMEM(right.shape, right.dtype),
            pltpu.VMEM(classes.shape, classes.dtype),
            pltpu.VMEM(bonds.shape, bonds.dtype),
            pltpu.SemaphoreType.DMA((4,)),
        ],
        name="prepare",
    )(energy, right, classes, bonds)


def swapped(block, lane, odd):
    low = (lane & 1) == (1 if odd else 0)
    target = jnp.where(low, lane + 1, lane + LANES - 1) & (LANES - 1)
    return jnp.take_along_axis(block, target, axis=1)


def coupling_rows(blocks_of, strips_of, groups, xtiles, inner, coup, open_bond, rows):
    lane = lane_iota()
    sub = lax.broadcasted_iota(jnp.int32, (SUB, LANES), 0)
    zero = jnp.zeros((SUB, LANES), jnp.float32)
    for g in groups:
        xt = (g - 1) % xtiles
        before, after = strips_of(g)
        whole = []
        for c in range(COUPLINGS):
            blocks = blocks_of(g, c, xt)
            shift = (c * xtiles + xt) * SLOT
            blocks.append(
                jnp.where(
                    lane < REACH,
                    turn(after, -shift),
                    jnp.where(lane >= LANES - REACH, turn(before, -shift - REACH), zero),
                )
            )
            if c == 1:
                even = [swapped(b, lane, False) for b in blocks]
                odd = [swapped(b, lane, True) for b in blocks]
                n = len(blocks)
                odd = [
                    jnp.where(lane == 0, odd[(i - 1) % n], jnp.where(lane == LANES - 1, odd[(i + 1) % n], odd[i]))
                    for i in range(n)
                ]
                blocks = [
                    jnp.where(((lane + sub) & 1) == 0, b, jnp.where((sub & 1) == 1, o, v))
                    for b, o, v in zip(blocks, odd, even)
                ]
            edge = blocks[inner]
            edge = edge + turn(edge, LANES // 2)
            blocks[inner] = edge + turn(edge, LANES // 4)
            whole.append(blocks)
        for s in range(SUB):
            e = (g - 1) * SUB + s + DEPTH
            if 0 <= e < rows:
                for c in range(COUPLINGS):
                    for i in range(inner + 1):
                        wide = jnp.broadcast_to(whole[c][i][s : s + 1], (SUB, LANES))
                        coup[e, c, :, i * LANES : (i + 1) * LANES] = wide
                        if c == 0 and i < inner:
                            shown = (wide > 0.0).astype(jnp.float32)
                            open_bond[e, :, i * LANES : (i + 1) * LANES] = jnp.concatenate(
                                [shown, shown], axis=0
                            ).astype(jnp.bfloat16)


def rim_row(before, after, x):
    lane = lane_iota()
    shift = (x % SUB) * SLOT
    return jnp.where(
        lane % SPAN < REACH,
        turn(after, -shift),
        jnp.where(lane % SPAN >= SPAN - REACH, turn(before, -shift - REACH), jnp.zeros((SUB, LANES), jnp.float32)),
    )


def stepper(field, rim, coup, open_bond, acc, left_ref):
    nright, width = field.shape[2:]
    rtiles, inner = nright // SUB, width // LANES
    rows_x = left_ref.shape[0]
    lane = lane_iota()

    def lanes_of(i):
        return slice(i * LANES, (i + 1) * LANES)

    def load(k, row, t, i):
        if i == inner:
            return rim[k, row]
        return field[k, row, t * SUB : (t + 1) * SUB, lanes_of(i)]

    def coupling(c, row, i):
        return coup[row, c, :, lanes_of(i)]

    where = [(t, i) for t in range(rtiles) for i in range(inner)] + [(0, inner)]

    def partners(here, odd):
        moved = {at: swapped(value, lane, odd) for at, value in here.items()}
        if not odd:
            return moved
        edge = moved[0, inner]
        start, end = lane == 0, lane == LANES - 1
        result, fill = {}, edge
        for t in range(rtiles):
            outer = turn(edge, -t * SPAN)
            for i in range(inner):
                left = moved[t, i - 1] if i else outer
                right = moved[t, i + 1] if i < inner - 1 else outer
                result[t, i] = jnp.where(start, left, jnp.where(end, right, moved[t, i]))
            facing = turn(jnp.where(lane < LANES // 2, moved[t, inner - 1], moved[t, 0]), t * SPAN)
            fill = jnp.where((lane == t * SPAN) | (lane == (t * SPAN - 1) % LANES), facing, fill)
        result[0, inner] = fill
        return result

    def advance(k, row, odd):
        here = {at: load(k, row, *at) for at in where}
        turned = partners(here, odd)
        east = [coupling(0, row, i) for i in range(inner + 1)]
        west = [coupling(0, row - 1, i) for i in range(inner + 1)]
        vertical = [coupling(1, row, i) for i in range(inner + 1)]
        site = [coupling(2, row, i) for i in range(inner + 1)] if k else None
        sign = jnp.where((lane & 1) == (1 if odd else 0), 1.0 / TWICE, -1.0 / TWICE)
        new = {}
        for t, i in where:
            beside = east[i] * load(k, row + 1, t, i) + west[i] * load(k, row - 1, t, i)
            across = vertical[i] * turned[t, i]
            if k == 0:
                new[t, i] = sign * (0.5 * beside - across)
            else:
                image = site[i] * here[t, i] - beside - across
                new[t, i] = 0.5 * image if k == 1 else image - load(k - 1, row, t, i)
        for t, i in where:
            if i == inner:
                rim[k + 1, row] = new[t, i]
            else:
                field[k + 1, row, t * SUB : (t + 1) * SUB, lanes_of(i)] = new[t, i]

    def contract(row, below=True, above=True):
        parts = []
        for t in range(rtiles * MOMENTS):
            k, q = divmod(t, rtiles)
            parts.append(field[k + 1, row, q * SUB : (q + 1) * SUB, :])
        value = jnp.concatenate(parts, axis=0)
        high = value.astype(jnp.bfloat16)
        low = (value - high.astype(jnp.float32)).astype(jnp.bfloat16)
        sides = []
        for there, bond, wanted in ((row - 1, row - 1, below), (row + 1, row, above)):
            for q in range(left_ref.shape[1] // (2 * SUB)):
                if wanted:
                    sides.append(left_ref[there - DEPTH, q * 2 * SUB : (q + 1) * 2 * SUB, :] * open_bond[bond])
                else:
                    sides.append(jnp.zeros((2 * SUB, width), jnp.bfloat16))
        block = jnp.concatenate(sides, axis=0)
        acc[...] += lax.dot_general(
            jnp.concatenate([high, low], axis=1),
            jnp.concatenate([block, block], axis=1),
            (((1,), (1,)), ((), ())),
            preferred_element_type=jnp.float32,
        )

    return advance, contract


def interior_kernel(own_ref, coup_ref, before_ref, after_ref, left_ref, acc, edge_field, edge_rim, ends_ref, field, rim, coup, open_bond):
    rows_x, nright, width = own_ref.shape
    rows = rows_x + 2 * DEPTH
    inner, xtiles = width // LANES, rows_x // SUB
    for x in range(rows_x):
        rim[0, x + DEPTH] = rim_row(before_ref[x // SUB], after_ref[x // SUB], x)
        field[0, x + DEPTH] = own_ref[x]

    def blocks_of(g, c, xt):
        return [coup_ref[c, xt * SUB : (xt + 1) * SUB, i * LANES : (i + 1) * LANES] for i in range(inner)]

    def strips_of(g):
        return before_ref[xtiles], after_ref[xtiles]

    coupling_rows(blocks_of, strips_of, range(1, xtiles + 1), xtiles, inner, coup, open_bond, rows)
    acc[...] = jnp.zeros_like(acc)
    advance, contract = stepper(field, rim, coup, open_bond, acc, left_ref)

    first, last = DEPTH + 1, DEPTH + rows_x - 2
    lag = 2 * MOMENTS - 1

    def front_step(front):
        if first + MOMENTS - 1 <= front - lag <= last - MOMENTS + 1:
            contract(front - lag)
        for k in reversed(range(MOMENTS)):
            if first + 3 * k <= front <= last + k:
                advance(k, front - 2 * k, front % 2 == 1)

    lead = first + MOMENTS - 1 + lag
    pairs = (last - lead + 1) // 2
    for front in range(first, lead):
        front_step(front)

    def both(n, _):
        for part in range(2):
            front = lead + 2 * n + part
            contract(front - lag)
            for k in reversed(range(MOMENTS)):
                advance(k, front - 2 * k, (lead + part) % 2 == 1)
        return 0

    lax.fori_loop(0, pairs, both, 0)
    for front in range(lead + 2 * pairs, last - MOMENTS + 1 + lag + 1):
        front_step(front)
    for k in range(MOMENTS - 1):
        for side, at in enumerate((first, last - MOMENTS + 1)):
            edge_field[side, k] = field[k + 1, at : at + MOMENTS]
            edge_rim[side, k] = rim[k + 1, at : at + MOMENTS]
    for n, x in enumerate((0, 1, rows_x - 2, rows_x - 1)):
        ends_ref[n] = own_ref[x]


class Either:
    def __init__(self, flag, one, other):
        self.flag, self.one, self.other = flag, one, other

    def __getitem__(self, at):
        return jnp.where(self.flag, self.one[at], self.other[at])


def border_kernel(scale, order_ref, ends_ref, coup_ref, near_ref, next_ref, before_ref, after_ref, left_ref, part_ref, edge_field, edge_rim, out_ref, field, rim, coup, open_bond, acc, spaced, ranked):
    nright, width = ends_ref.shape[1:]
    rows_x = left_ref.shape[0]
    rows = rows_x + 2 * DEPTH
    inner, xtiles = width // LANES, rows_x // SUB
    base = DEPTH * nright + COUPLINGS * SUB
    even = lax.axis_index("sx") % 2 == 0
    lo_ref, hi_ref = Either(even, near_ref, next_ref), Either(even, next_ref, near_ref)

    def corner(ref, which, v):
        return ref[base + which * SUB : base + (which + 1) * SUB, v * LANES : (v + 1) * LANES]

    for e in range(DEPTH):
        rim[0, e] = rim_row(corner(lo_ref, 0, 0), corner(lo_ref, 1, 0), e - DEPTH)
        field[0, e] = lo_ref[e * nright : (e + 1) * nright, :]
        rim[0, e + DEPTH + rows_x] = rim_row(corner(hi_ref, 0, 0), corner(hi_ref, 1, 0), e)
        field[0, e + DEPTH + rows_x] = hi_ref[e * nright : (e + 1) * nright, :]
    for n, x in enumerate((0, 1, rows_x - 2, rows_x - 1)):
        rim[0, x + DEPTH] = rim_row(before_ref[x // SUB], after_ref[x // SUB], x)
        field[0, x + DEPTH] = ends_ref[n]

    def blocks_of(g, c, xt):
        at = DEPTH * nright + c * SUB
        lanes = [slice(i * LANES, (i + 1) * LANES) for i in range(inner)]
        if g == 0:
            return [lo_ref[at : at + SUB, i] for i in lanes]
        if g == xtiles + 1:
            return [hi_ref[at : at + SUB, i] for i in lanes]
        return [coup_ref[c, xt * SUB : (xt + 1) * SUB, i] for i in lanes]

    def strips_of(g):
        if g == 0:
            return corner(lo_ref, 0, 1), corner(lo_ref, 1, 1)
        if g == xtiles + 1:
            return corner(hi_ref, 0, 1), corner(hi_ref, 1, 1)
        return before_ref[xtiles], after_ref[xtiles]

    coupling_rows(blocks_of, strips_of, (0, 1, xtiles, xtiles + 1), xtiles, inner, coup, open_bond, rows)
    first, last = DEPTH + 1, DEPTH + rows_x - 2
    for k in range(MOMENTS - 1):
        for side, at in enumerate((first, last - MOMENTS + 1)):
            field[k + 1, at : at + MOMENTS] = edge_field[side, k]
            rim[k + 1, at : at + MOMENTS] = edge_rim[side, k]
    acc[...] = part_ref[...]
    advance, contract = stepper(field, rim, coup, open_bond, acc, left_ref)

    for front in range(1, DEPTH + 3 * (MOMENTS - 1) + 1):
        for k in reversed(range(MOMENTS)):
            if 3 * k + 1 <= front <= 3 * k + DEPTH:
                row = front - 2 * k
                advance(k, row, row % 2 == 1)
                advance(k, rows - 1 - row, (rows - 1 - row) % 2 == 1)
    for n in range(DEPTH):
        for row in (DEPTH - 1 + n, rows - DEPTH - n):
            contract(row, 0 <= row - 1 - DEPTH < rows_x, 0 <= row + 1 - DEPTH < rows_x)

    groups, _, flat = out_ref.shape
    owned = flat // nright
    both_sides = acc[...].T
    half = both_sides.shape[0] // 2
    total = (both_sides[:half] - both_sides[half:]) * scale
    for k in range(MOMENTS):
        spaced[:, 0:nright] = total[:, k * nright : (k + 1) * nright]
        rows_of = [spaced[pl.ds(q, groups, stride=owned), :] for q in range(owned)]
        ranked[k] = jnp.concatenate([r[:, 0:nright] for r in rows_of], axis=1)
    for j in range(MOMENTS):
        out_ref[:, j, :] = ranked[order_ref[j]]


def vmem_call(kernel, name, out_shape, scratch, flops, *args, scalars=()):
    several = isinstance(out_shape, tuple)
    spec = pl.BlockSpec(memory_space=pltpu.VMEM)
    return pl.pallas_call(
        kernel,
        out_shape=out_shape,
        in_specs=[pl.BlockSpec(memory_space=pltpu.SMEM)] * len(scalars) + [spec] * len(args),
        out_specs=(spec,) * len(out_shape) if several else spec,
        scratch_shapes=scratch,
        compiler_params=pltpu.CompilerParams(vmem_limit_bytes=28 << 20),
        cost_estimate=pl.CostEstimate(flops=flops, bytes_accessed=1 << 22, transcendentals=0),
        name=name,
    )(*scalars, *args)


def scratch_of(rows_x, nright, width):
    rows = rows_x + 2 * DEPTH
    return [
        pltpu.VMEM((MOMENTS + 1, rows, nright, width), jnp.float32),
        pltpu.VMEM((MOMENTS + 1, rows, SUB, LANES), jnp.float32),
        pltpu.VMEM((rows, COUPLINGS, SUB, width + LANES), jnp.float32),
        pltpu.VMEM((rows, 2 * SUB, width), jnp.bfloat16),
    ]


def pairs(axis, start):
    size = lax.axis_size(axis)
    swaps = [(i % size, (i + 1) % size) for i in range(start, size + start, 2)]
    return swaps + [(b, a) for a, b in swaps]


def shards(right_vectors, left_vectors, classes, class_energy, bond_mask_grid, order):
    rows_x, rows_y = classes.shape
    nright, nleft = right_vectors.shape[0], left_vectors.shape[0]
    nsx, nsy = lax.axis_size("sx"), lax.axis_size("sy")
    owned = nleft // nsy
    even_x, even_y = lax.axis_index("sx") % 2 == 0, lax.axis_index("sy") % 2 == 0

    own, coup, rows, strips = prepare(right_vectors, classes, class_energy, bond_mask_grid)
    with jax.named_scope("halo_y"):
        near = lax.ppermute(strips[0], "sy", pairs("sy", -1))
        across = lax.ppermute(strips[1], "sy", pairs("sy", 0))
    before, after = jnp.where(even_y, near, across), jnp.where(even_y, across, near)
    with jax.named_scope("halo_x"):
        def with_corners(slot):
            upper = even_x == (slot == 0)
            corners = [
                jnp.concatenate([jnp.where(upper, part[0], part[-2]), part[-1]], axis=1) for part in (before, after)
            ]
            return jnp.concatenate([rows[slot]] + corners, axis=0)

        near_rows = lax.ppermute(with_corners(0), "sx", pairs("sx", -1))
        next_rows = lax.ppermute(with_corners(1), "sx", pairs("sx", 0))
    left = left_vectors.transpose(1, 0, 2)
    f32 = jnp.float32
    part, edge_field, edge_rim, ends = vmem_call(
        interior_kernel,
        "interior",
        (
            jax.ShapeDtypeStruct((MOMENTS * nright, 2 * nleft), f32),
            jax.ShapeDtypeStruct((2, MOMENTS - 1, MOMENTS, nright, rows_y), f32),
            jax.ShapeDtypeStruct((2, MOMENTS - 1, MOMENTS, SUB, LANES), f32),
            jax.ShapeDtypeStruct((4, nright, rows_y), f32),
        ),
        scratch_of(rows_x, nright, rows_y),
        1 << 33,
        own, coup, before, after, left,
    )
    sites = rows_x * rows_y * nsx * nsy
    tile = vmem_call(
        functools.partial(border_kernel, -HALF_ROOT / sites**0.5),
        "border",
        jax.ShapeDtypeStruct((nsy, MOMENTS, owned * nright), f32),
        scratch_of(rows_x, nright, rows_y)
        + [
            pltpu.VMEM((MOMENTS * nright, 2 * nleft), f32),
            pltpu.VMEM((nleft, LANES), f32),
            pltpu.VMEM((MOMENTS, nsy, owned * nright), f32),
        ],
        1 << 32,
        ends, coup, near_rows, next_rows, before, after, left, part, edge_field, edge_rim,
        scalars=(order,),
    )
    with jax.named_scope("reduce_sy"):
        mine = jnp.sum(lax.all_to_all(tile, "sy", 0, 0), axis=0)
    with jax.named_scope("reduce_sx"):
        shares = lax.all_to_all(jnp.broadcast_to(mine[None], (nsx,) + mine.shape), "sx", 0, 0)
    return jnp.sum(shares, axis=0).reshape(MOMENTS, owned, nright)


def solution(mesh):
    in_specs = (
        P(None, "sx", "sy"),
        P(None, "sx", "sy"),
        P("sx", "sy"),
        P(),
        P(None, "sx", "sy"),
        P(),
    )
    out_specs = P(None, "sy", None)
    return jax.shard_map(shards, mesh=mesh, in_specs=in_specs, out_specs=out_specs, check_vma=False)
```

```python
import functools

import jax
import jax.numpy as jnp
from jax import lax
from jax.experimental import pallas as pl
from jax.experimental.pallas import tpu as pltpu
from jax.sharding import PartitionSpec as P

MOMENTS = 5
HALF_ROOT = 0.8660254037844386
SPECTRAL = 4.6
TWICE = 2.0 / SPECTRAL
DEPTH = MOMENTS + 1
REACH = 3
SLOT = 4
COUPLINGS = 3
LANES = 128
SUB = 8
SPAN = 32


def lane_iota():
    return lax.broadcasted_iota(jnp.int32, (SUB, LANES), 1)


def turn(value, by):
    by %= LANES
    return pltpu.roll(value, by, 1) if by else value


def swap_major(blocks, sub):
    for s in (4, 2, 1):
        keep = (sub & s) == 0
        for i in range(SUB):
            if i & s == 0:
                a, b = blocks[i], blocks[i + s]
                blocks[i] = jnp.where(keep, a, pltpu.roll(b, s, 0))
                blocks[i + s] = jnp.where(keep, pltpu.roll(a, SUB - s, 0), b)
    return blocks


def prepare_kernel(energy_hbm, right_hbm, class_hbm, bond_hbm, own_hbm, coup_hbm, near_hbm, next_hbm, beside_hbm, across_hbm,
                   energy_ref, right_ref, class_ref, bond_ref, own_ref, coup_ref, rows_ref, strips_ref, in_sem, out_sem):
    nright, rows, width = right_ref.shape
    lane = lane_iota()
    sub = lax.broadcasted_iota(jnp.int32, (SUB, LANES), 0)
    xtiles, rtiles, inner = rows // SUB, nright // SUB, width // LANES
    halves = [pl.ds(h * 2 * SUB, 2 * SUB) for h in range(xtiles // 2)]
    reads = [pltpu.make_async_copy(right_hbm.at[:, h, :], right_ref.at[:, h, :], in_sem.at[n]) for n, h in enumerate(halves)]
    for n, (a, b) in enumerate(((energy_hbm, energy_ref), (class_hbm, class_ref), (bond_hbm, bond_ref))):
        reads.append(pltpu.make_async_copy(a, b, in_sem.at[len(halves) + n]))
    for copy in reads:
        copy.start()
    writes = []

    def write(source, target):
        copy = pltpu.make_async_copy(source, target, out_sem.at[len(writes)])
        copy.start()
        writes.append(copy)

    top_at, first_at = lax.axis_index("sx") % 2, lax.axis_index("sy") % 2
    zero = jnp.zeros((SUB, LANES), jnp.float32)
    first, last = [zero] * (xtiles + 1), [zero] * (xtiles + 1)

    def strip(v, at, i, block):
        here = (lane >= at) & (lane < at + REACH)
        if i == 0:
            first[v] = jnp.where(here, turn(block, at), first[v])
        if i == inner - 1:
            last[v] = jnp.where(here, turn(block, at + REACH), last[v])

    for half in range(xtiles // 2):
        reads[half].wait()
        for i in range(inner):
            lanes = slice(i * LANES, (i + 1) * LANES)
            for t in range(rtiles):
                wide = [
                    right_ref[t * SUB + q, half * 2 * SUB : (half + 1) * 2 * SUB, lanes].astype(jnp.float32)
                    for q in range(SUB)
                ]
                for part in range(2):
                    xt = half * 2 + part
                    turned = swap_major([w[part * SUB : (part + 1) * SUB] for w in wide], sub)
                    for j in range(SUB):
                        x = xt * SUB + j
                        own_ref[x, t * SUB : (t + 1) * SUB, lanes] = turned[j]
                        if x < DEPTH:
                            rows_ref[top_at, x * nright + t * SUB : x * nright + (t + 1) * SUB, lanes] = turned[j]
                        if x >= rows - DEPTH:
                            at = (x - rows + DEPTH) * nright + t * SUB
                            rows_ref[1 - top_at, at : at + SUB, lanes] = turned[j]
                        strip(xt, t * SPAN + j * SLOT, i, turned[j])
        write(own_ref.at[halves[half]], own_hbm.at[halves[half]])
    for copy in reads[len(halves) :]:
        copy.wait()
    for xt in range(xtiles):
        here = slice(xt * SUB, (xt + 1) * SUB)
        for i in range(inner):
            lanes = slice(i * LANES, (i + 1) * LANES)
            kinds = class_ref[here, lanes]
            energy = zero
            for level in range(energy_ref.shape[0]):
                energy = jnp.where(kinds == level, energy_ref[level] * TWICE, energy)
            fields = [bond_ref[c, here, lanes].astype(jnp.float32) * TWICE for c in range(2)] + [energy]
            for c in range(COUPLINGS):
                coup_ref[c, here, lanes] = fields[c]
                strip(xtiles, (c * xtiles + xt) * SLOT, i, fields[c])
                at = DEPTH * nright + c * SUB
                if xt == 0:
                    rows_ref[top_at, at : at + SUB, lanes] = fields[c]
                if xt == xtiles - 1:
                    rows_ref[1 - top_at, at : at + SUB, lanes] = fields[c]
    for v in range(xtiles + 1):
        strips_ref[first_at, v] = first[v]
        strips_ref[1 - first_at, v] = last[v]
    write(strips_ref.at[0], beside_hbm)
    write(strips_ref.at[1], across_hbm)
    filled = pl.ds(0, rows_ref.shape[1])
    write(rows_ref.at[0], near_hbm.at[filled])
    write(rows_ref.at[1], next_hbm.at[filled])
    write(coup_ref, coup_hbm)
    for copy in writes:
        copy.wait()


def prepare(right, classes, energy, bonds):
    nright, rows, width = right.shape
    edge = DEPTH * nright + COUPLINGS * SUB
    f32 = jnp.float32
    own, coup = (rows, nright, width), (COUPLINGS, rows, width)
    strip = (rows // SUB + 1, SUB, LANES)
    halves = rows // (2 * SUB)
    return pl.pallas_call(
        prepare_kernel,
        out_shape=tuple(
            jax.ShapeDtypeStruct(shape, f32)
            for shape in (own, coup, (edge + 2 * SUB, width), (edge + 2 * SUB, width), strip, strip)
        ),
        in_specs=[pl.BlockSpec(memory_space=pltpu.HBM)] * 4,
        out_specs=(pl.BlockSpec(memory_space=pltpu.HBM),) * 6,
        scratch_shapes=[
            pltpu.SMEM(energy.shape, energy.dtype),
            pltpu.VMEM(right.shape, right.dtype),
            pltpu.VMEM(classes.shape, classes.dtype),
            pltpu.VMEM(bonds.shape, bonds.dtype),
            pltpu.VMEM(own, f32),
            pltpu.VMEM(coup, f32),
            pltpu.VMEM((2, edge, width), f32),
            pltpu.VMEM((2,) + strip, f32),
            pltpu.SemaphoreType.DMA((halves + 3,)),
            pltpu.SemaphoreType.DMA((halves + 5,)),
        ],
        name="prepare",
    )(energy, right, classes, bonds)


def swapped(block, lane, odd):
    low = (lane & 1) == (1 if odd else 0)
    target = jnp.where(low, lane + 1, lane + LANES - 1) & (LANES - 1)
    return jnp.take_along_axis(block, target, axis=1)


def coupling_rows(blocks_of, strips_of, groups, xtiles, inner, coup, open_bond, rows):
    lane = lane_iota()
    sub = lax.broadcasted_iota(jnp.int32, (SUB, LANES), 0)
    zero = jnp.zeros((SUB, LANES), jnp.float32)
    for g in groups:
        xt = (g - 1) % xtiles
        before, after = strips_of(g)
        whole = []
        for c in range(COUPLINGS):
            blocks = blocks_of(g, c, xt)
            shift = (c * xtiles + xt) * SLOT
            blocks.append(
                jnp.where(
                    lane < REACH,
                    turn(after, -shift),
                    jnp.where(lane >= LANES - REACH, turn(before, -shift - REACH), zero),
                )
            )
            if c == 1:
                even = [swapped(b, lane, False) for b in blocks]
                odd = [swapped(b, lane, True) for b in blocks]
                n = len(blocks)
                odd = [
                    jnp.where(lane == 0, odd[(i - 1) % n], jnp.where(lane == LANES - 1, odd[(i + 1) % n], odd[i]))
                    for i in range(n)
                ]
                blocks = [
                    jnp.where(((lane + sub) & 1) == 0, b, jnp.where((sub & 1) == 1, o, v))
                    for b, o, v in zip(blocks, odd, even)
                ]
            edge = blocks[inner]
            edge = edge + turn(edge, LANES // 2)
            blocks[inner] = edge + turn(edge, LANES // 4)
            whole.append(blocks)
        for s in range(SUB):
            e = (g - 1) * SUB + s + DEPTH
            if 0 <= e < rows:
                for c in range(COUPLINGS):
                    for i in range(inner + 1):
                        wide = jnp.broadcast_to(whole[c][i][s : s + 1], (SUB, LANES))
                        coup[e, c, :, i * LANES : (i + 1) * LANES] = wide
                        if c == 0 and i < inner:
                            shown = (wide > 0.0).astype(jnp.float32)
                            open_bond[e, :, i * LANES : (i + 1) * LANES] = jnp.concatenate(
                                [shown, shown], axis=0
                            ).astype(jnp.bfloat16)


def rim_row(before, after, x):
    lane = lane_iota()
    shift = (x % SUB) * SLOT
    return jnp.where(
        lane % SPAN < REACH,
        turn(after, -shift),
        jnp.where(lane % SPAN >= SPAN - REACH, turn(before, -shift - REACH), jnp.zeros((SUB, LANES), jnp.float32)),
    )


def stepper(field, rim, coup, open_bond, acc, left_ref):
    nright, width = field.shape[2:]
    rtiles, inner = nright // SUB, width // LANES
    rows_x = left_ref.shape[0]
    lane = lane_iota()

    def lanes_of(i):
        return slice(i * LANES, (i + 1) * LANES)

    def load(k, row, t, i):
        if i == inner:
            return rim[k, row]
        return field[k, row, t * SUB : (t + 1) * SUB, lanes_of(i)]

    def coupling(c, row, i):
        return coup[row, c, :, lanes_of(i)]

    where = [(t, i) for t in range(rtiles) for i in range(inner)] + [(0, inner)]

    def partners(here, odd):
        moved = {at: swapped(value, lane, odd) for at, value in here.items()}
        if not odd:
            return moved
        edge = moved[0, inner]
        start, end = lane == 0, lane == LANES - 1
        result, fill = {}, edge
        for t in range(rtiles):
            outer = turn(edge, -t * SPAN)
            for i in range(inner):
                left = moved[t, i - 1] if i else outer
                right = moved[t, i + 1] if i < inner - 1 else outer
                result[t, i] = jnp.where(start, left, jnp.where(end, right, moved[t, i]))
            facing = turn(jnp.where(lane < LANES // 2, moved[t, inner - 1], moved[t, 0]), t * SPAN)
            fill = jnp.where((lane == t * SPAN) | (lane == (t * SPAN - 1) % LANES), facing, fill)
        result[0, inner] = fill
        return result

    def advance(k, row, odd):
        here = {at: load(k, row, *at) for at in where}
        turned = partners(here, odd)
        east = [coupling(0, row, i) for i in range(inner + 1)]
        west = [coupling(0, row - 1, i) for i in range(inner + 1)]
        vertical = [coupling(1, row, i) for i in range(inner + 1)]
        site = [coupling(2, row, i) for i in range(inner + 1)] if k else None
        sign = jnp.where((lane & 1) == (1 if odd else 0), 1.0 / TWICE, -1.0 / TWICE)
        new = {}
        for t, i in where:
            beside = east[i] * load(k, row + 1, t, i) + west[i] * load(k, row - 1, t, i)
            across = vertical[i] * turned[t, i]
            if k == 0:
                new[t, i] = sign * (0.5 * beside - across)
            else:
                image = site[i] * here[t, i] - beside - across
                new[t, i] = 0.5 * image if k == 1 else image - load(k - 1, row, t, i)
        for t, i in where:
            if i == inner:
                rim[k + 1, row] = new[t, i]
            else:
                field[k + 1, row, t * SUB : (t + 1) * SUB, lanes_of(i)] = new[t, i]

    def contract(row, below=True, above=True):
        parts = []
        for t in range(rtiles * MOMENTS):
            k, q = divmod(t, rtiles)
            parts.append(field[k + 1, row, q * SUB : (q + 1) * SUB, :])
        value = jnp.concatenate(parts, axis=0)
        high = value.astype(jnp.bfloat16)
        low = (value - high.astype(jnp.float32)).astype(jnp.bfloat16)
        sides = []
        for there, bond, wanted in ((row - 1, row - 1, below), (row + 1, row, above)):
            for q in range(left_ref.shape[1] // (2 * SUB)):
                if wanted:
                    sides.append(left_ref[there - DEPTH, q * 2 * SUB : (q + 1) * 2 * SUB, :] * open_bond[bond])
                else:
                    sides.append(jnp.zeros((2 * SUB, width), jnp.bfloat16))
        block = jnp.concatenate(sides, axis=0)
        acc[...] += lax.dot_general(
            jnp.concatenate([high, low], axis=1),
            jnp.concatenate([block, block], axis=1),
            (((1,), (1,)), ((), ())),
            preferred_element_type=jnp.float32,
        )

    return advance, contract


def interior_kernel(own_ref, coup_ref, before_ref, after_ref, left_ref, acc, edge_field, edge_rim, ends_ref, field, rim, coup, open_bond):
    rows_x, nright, width = own_ref.shape
    rows = rows_x + 2 * DEPTH
    inner, xtiles = width // LANES, rows_x // SUB
    for x in range(rows_x):
        rim[0, x + DEPTH] = rim_row(before_ref[x // SUB], after_ref[x // SUB], x)
        field[0, x + DEPTH] = own_ref[x]

    def blocks_of(g, c, xt):
        return [coup_ref[c, xt * SUB : (xt + 1) * SUB, i * LANES : (i + 1) * LANES] for i in range(inner)]

    def strips_of(g):
        return before_ref[xtiles], after_ref[xtiles]

    coupling_rows(blocks_of, strips_of, range(1, xtiles + 1), xtiles, inner, coup, open_bond, rows)
    acc[...] = jnp.zeros_like(acc)
    advance, contract = stepper(field, rim, coup, open_bond, acc, left_ref)

    first, last = DEPTH + 1, DEPTH + rows_x - 2
    lag = 2 * MOMENTS - 1

    def front_step(front):
        if first + MOMENTS - 1 <= front - lag <= last - MOMENTS + 1:
            contract(front - lag)
        for k in reversed(range(MOMENTS)):
            if first + 3 * k <= front <= last + k:
                advance(k, front - 2 * k, front % 2 == 1)

    lead = first + MOMENTS - 1 + lag
    pairs = (last - lead + 1) // 2
    for front in range(first, lead):
        front_step(front)

    def both(n, _):
        for part in range(2):
            front = lead + 2 * n + part
            contract(front - lag)
            for k in reversed(range(MOMENTS)):
                advance(k, front - 2 * k, (lead + part) % 2 == 1)
        return 0

    lax.fori_loop(0, pairs, both, 0)
    for front in range(lead + 2 * pairs, last - MOMENTS + 1 + lag + 1):
        front_step(front)
    for k in range(MOMENTS - 1):
        for side, at in enumerate((first, last - MOMENTS + 1)):
            edge_field[side, k] = field[k + 1, at : at + MOMENTS]
            edge_rim[side, k] = rim[k + 1, at : at + MOMENTS]
    for n, x in enumerate((0, 1, rows_x - 2, rows_x - 1)):
        ends_ref[n] = own_ref[x]


class Either:
    def __init__(self, flag, one, other):
        self.flag, self.one, self.other = flag, one, other

    def __getitem__(self, at):
        return jnp.where(self.flag, self.one[at], self.other[at])


def border_kernel(scale, order_ref, ends_ref, coup_ref, near_ref, next_ref, before_ref, after_ref, left_ref, part_ref, edge_field, edge_rim, out_ref, field, rim, coup, open_bond, acc, spaced, ranked):
    nright, width = ends_ref.shape[1:]
    rows_x = left_ref.shape[0]
    rows = rows_x + 2 * DEPTH
    inner, xtiles = width // LANES, rows_x // SUB
    base = DEPTH * nright + COUPLINGS * SUB
    even = lax.axis_index("sx") % 2 == 0
    lo_ref, hi_ref = Either(even, near_ref, next_ref), Either(even, next_ref, near_ref)

    def corner(ref, which, v):
        return ref[base + which * SUB : base + (which + 1) * SUB, v * LANES : (v + 1) * LANES]

    for e in range(DEPTH):
        rim[0, e] = rim_row(corner(lo_ref, 0, 0), corner(lo_ref, 1, 0), e - DEPTH)
        field[0, e] = lo_ref[e * nright : (e + 1) * nright, :]
        rim[0, e + DEPTH + rows_x] = rim_row(corner(hi_ref, 0, 0), corner(hi_ref, 1, 0), e)
        field[0, e + DEPTH + rows_x] = hi_ref[e * nright : (e + 1) * nright, :]
    for n, x in enumerate((0, 1, rows_x - 2, rows_x - 1)):
        rim[0, x + DEPTH] = rim_row(before_ref[x // SUB], after_ref[x // SUB], x)
        field[0, x + DEPTH] = ends_ref[n]

    def blocks_of(g, c, xt):
        at = DEPTH * nright + c * SUB
        lanes = [slice(i * LANES, (i + 1) * LANES) for i in range(inner)]
        if g == 0:
            return [lo_ref[at : at + SUB, i] for i in lanes]
        if g == xtiles + 1:
            return [hi_ref[at : at + SUB, i] for i in lanes]
        return [coup_ref[c, xt * SUB : (xt + 1) * SUB, i] for i in lanes]

    def strips_of(g):
        if g == 0:
            return corner(lo_ref, 0, 1), corner(lo_ref, 1, 1)
        if g == xtiles + 1:
            return corner(hi_ref, 0, 1), corner(hi_ref, 1, 1)
        return before_ref[xtiles], after_ref[xtiles]

    coupling_rows(blocks_of, strips_of, (0, 1, xtiles, xtiles + 1), xtiles, inner, coup, open_bond, rows)
    first, last = DEPTH + 1, DEPTH + rows_x - 2
    for k in range(MOMENTS - 1):
        for side, at in enumerate((first, last - MOMENTS + 1)):
            field[k + 1, at : at + MOMENTS] = edge_field[side, k]
            rim[k + 1, at : at + MOMENTS] = edge_rim[side, k]
    acc[...] = part_ref[...]
    advance, contract = stepper(field, rim, coup, open_bond, acc, left_ref)

    for front in range(1, DEPTH + 3 * (MOMENTS - 1) + 1):
        for k in reversed(range(MOMENTS)):
            if 3 * k + 1 <= front <= 3 * k + DEPTH:
                row = front - 2 * k
                advance(k, row, row % 2 == 1)
                advance(k, rows - 1 - row, (rows - 1 - row) % 2 == 1)
    for n in range(DEPTH):
        for row in (DEPTH - 1 + n, rows - DEPTH - n):
            contract(row, 0 <= row - 1 - DEPTH < rows_x, 0 <= row + 1 - DEPTH < rows_x)

    near, far, _, flat = out_ref.shape
    groups, owned = near * far, flat // nright
    both_sides = acc[...].T
    half = both_sides.shape[0] // 2
    total = (both_sides[:half] - both_sides[half:]) * scale
    for k in range(MOMENTS):
        spaced[:, 0:nright] = total[:, k * nright : (k + 1) * nright]
        rows_of = [spaced[pl.ds(q, groups, stride=owned), :] for q in range(owned)]
        ranked[k] = jnp.concatenate([r[:, 0:nright] for r in rows_of], axis=1)
    for j in range(MOMENTS):
        for n in range(far):
            out_ref[:, n, j, :] = ranked[order_ref[j], n * near : (n + 1) * near]


def vmem_call(kernel, name, out_shape, scratch, flops, *args, scalars=()):
    several = isinstance(out_shape, tuple)
    spec = pl.BlockSpec(memory_space=pltpu.VMEM)
    return pl.pallas_call(
        kernel,
        out_shape=out_shape,
        in_specs=[pl.BlockSpec(memory_space=pltpu.SMEM)] * len(scalars) + [spec] * len(args),
        out_specs=(spec,) * len(out_shape) if several else spec,
        scratch_shapes=scratch,
        compiler_params=pltpu.CompilerParams(vmem_limit_bytes=28 << 20),
        cost_estimate=pl.CostEstimate(flops=flops, bytes_accessed=1 << 22, transcendentals=0),
        name=name,
    )(*scalars, *args)


def scratch_of(rows_x, nright, width):
    rows = rows_x + 2 * DEPTH
    return [
        pltpu.VMEM((MOMENTS + 1, rows, nright, width), jnp.float32),
        pltpu.VMEM((MOMENTS + 1, rows, SUB, LANES), jnp.float32),
        pltpu.VMEM((rows, COUPLINGS, SUB, width + LANES), jnp.float32),
        pltpu.VMEM((rows, 2 * SUB, width), jnp.bfloat16),
    ]


def pairs(axis, start):
    size = lax.axis_size(axis)
    swaps = [(i % size, (i + 1) % size) for i in range(start, size + start, 2)]
    return swaps + [(b, a) for a, b in swaps]


def near_part(size):
    return 8 if size % 8 == 0 else size


def shards(right_vectors, left_vectors, classes, class_energy, bond_mask_grid, order):
    rows_x, rows_y = classes.shape
    nright, nleft = right_vectors.shape[0], left_vectors.shape[0]
    nsx, nsy = lax.axis_size("sx"), lax.axis_size("sy")
    owned = nleft // nsy
    even_x, even_y = lax.axis_index("sx") % 2 == 0, lax.axis_index("sy") % 2 == 0

    own, coup, near_payload, next_payload, beside, across = prepare(
        right_vectors, classes, class_energy, bond_mask_grid
    )
    with jax.named_scope("halo_y"):
        beside = lax.ppermute(beside, "sy", pairs("sy", -1))
        across = lax.ppermute(across, "sy", pairs("sy", 0))
    before, after = jnp.where(even_y, beside, across), jnp.where(even_y, across, beside)
    with jax.named_scope("halo_x"):
        def with_corners(payload, upper):
            corners = [
                jnp.concatenate([jnp.where(upper, part[0], part[-2]), part[-1]], axis=1) for part in (before, after)
            ]
            corners = jnp.concatenate(corners, axis=0)
            return lax.dynamic_update_slice(payload, corners, (payload.shape[0] - corners.shape[0], 0))

        near_rows = lax.ppermute(with_corners(near_payload, even_x), "sx", pairs("sx", -1))
        next_rows = lax.ppermute(with_corners(next_payload, ~even_x), "sx", pairs("sx", 0))
    left = left_vectors.transpose(1, 0, 2)
    f32 = jnp.float32
    part, edge_field, edge_rim, ends = vmem_call(
        interior_kernel,
        "interior",
        (
            jax.ShapeDtypeStruct((MOMENTS * nright, 2 * nleft), f32),
            jax.ShapeDtypeStruct((2, MOMENTS - 1, MOMENTS, nright, rows_y), f32),
            jax.ShapeDtypeStruct((2, MOMENTS - 1, MOMENTS, SUB, LANES), f32),
            jax.ShapeDtypeStruct((4, nright, rows_y), f32),
        ),
        scratch_of(rows_x, nright, rows_y),
        1 << 33,
        own, coup, before, after, left,
    )
    near, depth_z = near_part(nsy), near_part(nsx)
    sites = rows_x * rows_y * nsx * nsy
    tile = vmem_call(
        functools.partial(border_kernel, -HALF_ROOT / sites**0.5),
        "border",
        jax.ShapeDtypeStruct((near, nsy // near, MOMENTS, owned * nright), f32),
        scratch_of(rows_x, nright, rows_y)
        + [
            pltpu.VMEM((MOMENTS * nright, 2 * nleft), f32),
            pltpu.VMEM((nleft, LANES), f32),
            pltpu.VMEM((MOMENTS, nsy, owned * nright), f32),
        ],
        1 << 32,
        ends, coup, near_rows, next_rows, before, after, left, part, edge_field, edge_rim,
        scalars=(order,),
    )
    far_y, far_x = nsy // near, nsx // depth_z
    block = tile.shape[2:]
    with jax.named_scope("reduce_near"):
        runs = [[n * near + i for i in range(near)] for n in range(far_y)]
        mine = jnp.sum(lax.all_to_all(tile, "sy", 0, 0, axis_index_groups=runs), axis=0)
    with jax.named_scope("reduce_far"):
        if far_y * far_x > 1:
            spread = jnp.broadcast_to(mine[:, None], (far_y, far_x) + block).reshape((far_y * far_x,) + block)
            rings = [
                [(m * depth_z + z) * nsy + n * near + i for n in range(far_y) for m in range(far_x)]
                for z in range(depth_z)
                for i in range(near)
            ]
            mine = lax.all_to_all(spread, ("sx", "sy"), 0, 0, axis_index_groups=rings)
        mine = jnp.sum(mine, axis=0)
    with jax.named_scope("reduce_z"):
        runs = [[m * depth_z + z for z in range(depth_z)] for m in range(far_x)]
        spread = jnp.broadcast_to(mine[None], (depth_z,) + block)
        shares = lax.all_to_all(spread, "sx", 0, 0, axis_index_groups=runs)
    return jnp.sum(shares, axis=0).reshape(MOMENTS, owned, nright)


def solution(mesh):
    in_specs = (
        P(None, "sx", "sy"),
        P(None, "sx", "sy"),
        P("sx", "sy"),
        P(),
        P(None, "sx", "sy"),
        P(),
    )
    out_specs = P(None, "sy", None)
    return jax.shard_map(shards, mesh=mesh, in_specs=in_specs, out_specs=out_specs, check_vma=False)
```

```python
import functools

import jax
import jax.numpy as jnp
from jax import lax
from jax.experimental import pallas as pl
from jax.experimental.pallas import tpu as pltpu
from jax.sharding import PartitionSpec as P

MOMENTS = 5
HALF_ROOT = 0.8660254037844386
SPECTRAL = 4.6
TWICE = 2.0 / SPECTRAL
DEPTH = MOMENTS + 1
REACH = 3
SLOT = 4
COUPLINGS = 3
LANES = 128
SUB = 8
SPAN = 32


def lane_iota():
    return lax.broadcasted_iota(jnp.int32, (SUB, LANES), 1)


def turn(value, by):
    by %= LANES
    return pltpu.roll(value, by, 1) if by else value


def swap_major(blocks, sub):
    for s in (4, 2, 1):
        keep = (sub & s) == 0
        for i in range(SUB):
            if i & s == 0:
                a, b = blocks[i], blocks[i + s]
                blocks[i] = jnp.where(keep, a, pltpu.roll(b, s, 0))
                blocks[i + s] = jnp.where(keep, pltpu.roll(a, SUB - s, 0), b)
    return blocks


def prepare_kernel(energy_hbm, right_hbm, class_hbm, bond_hbm, own_hbm, coup_hbm, near_hbm, next_hbm, beside_hbm, across_hbm,
                   energy_ref, right_ref, class_ref, bond_ref, own_ref, coup_ref, rows_ref, strips_ref, in_sem, out_sem):
    nright, rows, width = right_ref.shape
    lane = lane_iota()
    sub = lax.broadcasted_iota(jnp.int32, (SUB, LANES), 0)
    xtiles, rtiles, inner = rows // SUB, nright // SUB, width // LANES
    halves = [pl.ds(h * 2 * SUB, 2 * SUB) for h in range(xtiles // 2)]
    reads = [pltpu.make_async_copy(right_hbm.at[:, h, :], right_ref.at[:, h, :], in_sem.at[n]) for n, h in enumerate(halves)]
    for n, (a, b) in enumerate(((energy_hbm, energy_ref), (class_hbm, class_ref), (bond_hbm, bond_ref))):
        reads.append(pltpu.make_async_copy(a, b, in_sem.at[len(halves) + n]))
    for copy in reads:
        copy.start()
    writes = []

    def write(source, target):
        copy = pltpu.make_async_copy(source, target, out_sem.at[len(writes)])
        copy.start()
        writes.append(copy)

    top_at, first_at = lax.axis_index("sx") % 2, lax.axis_index("sy") % 2
    zero = jnp.zeros((SUB, LANES), jnp.float32)
    first, last = [zero] * (xtiles + 1), [zero] * (xtiles + 1)

    def strip(v, at, i, block):
        here = (lane >= at) & (lane < at + REACH)
        if i == 0:
            first[v] = jnp.where(here, turn(block, at), first[v])
        if i == inner - 1:
            last[v] = jnp.where(here, turn(block, at + REACH), last[v])

    for half in range(xtiles // 2):
        reads[half].wait()
        for i in range(inner):
            lanes = slice(i * LANES, (i + 1) * LANES)
            for t in range(rtiles):
                wide = [
                    right_ref[t * SUB + q, half * 2 * SUB : (half + 1) * 2 * SUB, lanes].astype(jnp.float32)
                    for q in range(SUB)
                ]
                for part in range(2):
                    xt = half * 2 + part
                    turned = swap_major([w[part * SUB : (part + 1) * SUB] for w in wide], sub)
                    for j in range(SUB):
                        x = xt * SUB + j
                        own_ref[x, t * SUB : (t + 1) * SUB, lanes] = turned[j]
                        if x < DEPTH:
                            rows_ref[top_at, x * nright + t * SUB : x * nright + (t + 1) * SUB, lanes] = turned[j]
                        if x >= rows - DEPTH:
                            at = (x - rows + DEPTH) * nright + t * SUB
                            rows_ref[1 - top_at, at : at + SUB, lanes] = turned[j]
                        strip(xt, t * SPAN + j * SLOT, i, turned[j])
        write(own_ref.at[halves[half]], own_hbm.at[halves[half]])
    for copy in reads[len(halves) :]:
        copy.wait()
    for xt in range(xtiles):
        here = slice(xt * SUB, (xt + 1) * SUB)
        for i in range(inner):
            lanes = slice(i * LANES, (i + 1) * LANES)
            kinds = class_ref[here, lanes]
            energy = zero
            for level in range(energy_ref.shape[0]):
                energy = jnp.where(kinds == level, energy_ref[level] * TWICE, energy)
            fields = [bond_ref[c, here, lanes].astype(jnp.float32) * TWICE for c in range(2)] + [energy]
            for c in range(COUPLINGS):
                coup_ref[c, here, lanes] = fields[c]
                strip(xtiles, (c * xtiles + xt) * SLOT, i, fields[c])
                at = DEPTH * nright + c * SUB
                if xt == 0:
                    rows_ref[top_at, at : at + SUB, lanes] = fields[c]
                if xt == xtiles - 1:
                    rows_ref[1 - top_at, at : at + SUB, lanes] = fields[c]
    for v in range(xtiles + 1):
        strips_ref[first_at, v] = first[v]
        strips_ref[1 - first_at, v] = last[v]
    write(strips_ref.at[0], beside_hbm)
    write(strips_ref.at[1], across_hbm)
    filled = pl.ds(0, rows_ref.shape[1])
    write(rows_ref.at[0], near_hbm.at[filled])
    write(rows_ref.at[1], next_hbm.at[filled])
    write(coup_ref, coup_hbm)
    for copy in writes:
        copy.wait()


def prepare(right, classes, energy, bonds):
    nright, rows, width = right.shape
    edge = DEPTH * nright + COUPLINGS * SUB
    f32 = jnp.float32
    own, coup = (rows, nright, width), (COUPLINGS, rows, width)
    strip = (rows // SUB + 1, SUB, LANES)
    halves = rows // (2 * SUB)
    return pl.pallas_call(
        prepare_kernel,
        out_shape=tuple(
            jax.ShapeDtypeStruct(shape, f32)
            for shape in (own, coup, (edge + 2 * SUB, width), (edge + 2 * SUB, width), strip, strip)
        ),
        in_specs=[pl.BlockSpec(memory_space=pltpu.HBM)] * 4,
        out_specs=(pl.BlockSpec(memory_space=pltpu.HBM),) * 6,
        scratch_shapes=[
            pltpu.SMEM(energy.shape, energy.dtype),
            pltpu.VMEM(right.shape, right.dtype),
            pltpu.VMEM(classes.shape, classes.dtype),
            pltpu.VMEM(bonds.shape, bonds.dtype),
            pltpu.VMEM(own, f32),
            pltpu.VMEM(coup, f32),
            pltpu.VMEM((2, edge, width), f32),
            pltpu.VMEM((2,) + strip, f32),
            pltpu.SemaphoreType.DMA((halves + 3,)),
            pltpu.SemaphoreType.DMA((halves + 5,)),
        ],
        name="prepare",
    )(energy, right, classes, bonds)


def swapped(block, lane, odd):
    low = (lane & 1) == (1 if odd else 0)
    target = jnp.where(low, lane + 1, lane + LANES - 1) & (LANES - 1)
    return jnp.take_along_axis(block, target, axis=1)


def coupling_rows(blocks_of, strips_of, groups, xtiles, inner, coup, open_bond, rows):
    lane = lane_iota()
    sub = lax.broadcasted_iota(jnp.int32, (SUB, LANES), 0)
    zero = jnp.zeros((SUB, LANES), jnp.float32)
    for g in groups:
        xt = (g - 1) % xtiles
        before, after = strips_of(g)
        whole = []
        for c in range(COUPLINGS):
            blocks = blocks_of(g, c, xt)
            shift = (c * xtiles + xt) * SLOT
            blocks.append(
                jnp.where(
                    lane < REACH,
                    turn(after, -shift),
                    jnp.where(lane >= LANES - REACH, turn(before, -shift - REACH), zero),
                )
            )
            if c == 1:
                even = [swapped(b, lane, False) for b in blocks]
                odd = [swapped(b, lane, True) for b in blocks]
                n = len(blocks)
                odd = [
                    jnp.where(lane == 0, odd[(i - 1) % n], jnp.where(lane == LANES - 1, odd[(i + 1) % n], odd[i]))
                    for i in range(n)
                ]
                blocks = [
                    jnp.where(((lane + sub) & 1) == 0, b, jnp.where((sub & 1) == 1, o, v))
                    for b, o, v in zip(blocks, odd, even)
                ]
            edge = blocks[inner]
            edge = edge + turn(edge, LANES // 2)
            blocks[inner] = edge + turn(edge, LANES // 4)
            whole.append(blocks)
        for s in range(SUB):
            e = (g - 1) * SUB + s + DEPTH
            if 0 <= e < rows:
                for c in range(COUPLINGS):
                    for i in range(inner + 1):
                        wide = jnp.broadcast_to(whole[c][i][s : s + 1], (SUB, LANES))
                        coup[e, c, :, i * LANES : (i + 1) * LANES] = wide
                        if c == 0 and i < inner:
                            shown = (wide > 0.0).astype(jnp.float32)
                            open_bond[e, :, i * LANES : (i + 1) * LANES] = jnp.concatenate(
                                [shown, shown], axis=0
                            ).astype(jnp.bfloat16)


def rim_row(before, after, x):
    lane = lane_iota()
    shift = (x % SUB) * SLOT
    return jnp.where(
        lane % SPAN < REACH,
        turn(after, -shift),
        jnp.where(lane % SPAN >= SPAN - REACH, turn(before, -shift - REACH), jnp.zeros((SUB, LANES), jnp.float32)),
    )


def stepper(field, rim, coup, open_bond, acc, left_ref):
    nright, width = field.shape[2:]
    rtiles, inner = nright // SUB, width // LANES
    rows_x = left_ref.shape[0]
    lane = lane_iota()

    def lanes_of(i):
        return slice(i * LANES, (i + 1) * LANES)

    def load(k, row, t, i):
        if i == inner:
            return rim[k, row]
        return field[k, row, t * SUB : (t + 1) * SUB, lanes_of(i)]

    def coupling(c, row, i):
        return coup[row, c, :, lanes_of(i)]

    where = [(t, i) for t in range(rtiles) for i in range(inner)] + [(0, inner)]

    def partners(here, odd):
        moved = {at: swapped(value, lane, odd) for at, value in here.items()}
        if not odd:
            return moved
        edge = moved[0, inner]
        start, end = lane == 0, lane == LANES - 1
        result, fill = {}, edge
        for t in range(rtiles):
            outer = turn(edge, -t * SPAN)
            for i in range(inner):
                left = moved[t, i - 1] if i else outer
                right = moved[t, i + 1] if i < inner - 1 else outer
                result[t, i] = jnp.where(start, left, jnp.where(end, right, moved[t, i]))
            facing = turn(jnp.where(lane < LANES // 2, moved[t, inner - 1], moved[t, 0]), t * SPAN)
            fill = jnp.where((lane == t * SPAN) | (lane == (t * SPAN - 1) % LANES), facing, fill)
        result[0, inner] = fill
        return result

    def advance(k, row, odd):
        here = {at: load(k, row, *at) for at in where}
        turned = partners(here, odd)
        east = [coupling(0, row, i) for i in range(inner + 1)]
        west = [coupling(0, row - 1, i) for i in range(inner + 1)]
        vertical = [coupling(1, row, i) for i in range(inner + 1)]
        site = [coupling(2, row, i) for i in range(inner + 1)] if k else None
        sign = jnp.where((lane & 1) == (1 if odd else 0), 1.0 / TWICE, -1.0 / TWICE)
        new = {}
        for t, i in where:
            beside = east[i] * load(k, row + 1, t, i) + west[i] * load(k, row - 1, t, i)
            across = vertical[i] * turned[t, i]
            if k == 0:
                new[t, i] = sign * (0.5 * beside - across)
            else:
                image = site[i] * here[t, i] - beside - across
                new[t, i] = 0.5 * image if k == 1 else image - load(k - 1, row, t, i)
        for t, i in where:
            if i == inner:
                rim[k + 1, row] = new[t, i]
            else:
                field[k + 1, row, t * SUB : (t + 1) * SUB, lanes_of(i)] = new[t, i]

    def contract(row, below=True, above=True):
        parts = []
        for t in range(rtiles * MOMENTS):
            k, q = divmod(t, rtiles)
            parts.append(field[k + 1, row, q * SUB : (q + 1) * SUB, :])
        value = jnp.concatenate(parts, axis=0)
        high = value.astype(jnp.bfloat16)
        low = (value - high.astype(jnp.float32)).astype(jnp.bfloat16)
        sides = []
        for there, bond, wanted in ((row - 1, row - 1, below), (row + 1, row, above)):
            for q in range(left_ref.shape[1] // (2 * SUB)):
                if wanted:
                    sides.append(left_ref[there - DEPTH, q * 2 * SUB : (q + 1) * 2 * SUB, :] * open_bond[bond])
                else:
                    sides.append(jnp.zeros((2 * SUB, width), jnp.bfloat16))
        block = jnp.concatenate(sides, axis=0)
        acc[...] += lax.dot_general(
            jnp.concatenate([high, low], axis=1),
            jnp.concatenate([block, block], axis=1),
            (((1,), (1,)), ((), ())),
            preferred_element_type=jnp.float32,
        )

    return advance, contract


def interior_kernel(own_ref, coup_ref, before_ref, after_ref, left_ref, acc, edge_field, edge_rim, ends_ref, field, rim, coup, open_bond):
    rows_x, nright, width = own_ref.shape
    rows = rows_x + 2 * DEPTH
    inner, xtiles = width // LANES, rows_x // SUB
    for x in range(rows_x):
        rim[0, x + DEPTH] = rim_row(before_ref[x // SUB], after_ref[x // SUB], x)
        field[0, x + DEPTH] = own_ref[x]

    def blocks_of(g, c, xt):
        return [coup_ref[c, xt * SUB : (xt + 1) * SUB, i * LANES : (i + 1) * LANES] for i in range(inner)]

    def strips_of(g):
        return before_ref[xtiles], after_ref[xtiles]

    coupling_rows(blocks_of, strips_of, range(1, xtiles + 1), xtiles, inner, coup, open_bond, rows)
    acc[...] = jnp.zeros_like(acc)
    advance, contract = stepper(field, rim, coup, open_bond, acc, left_ref)

    first, last = DEPTH + 1, DEPTH + rows_x - 2
    lag = 2 * MOMENTS - 1

    def front_step(front):
        if first + MOMENTS - 1 <= front - lag <= last - MOMENTS + 1:
            contract(front - lag)
        for k in reversed(range(MOMENTS)):
            if first + 3 * k <= front <= last + k:
                advance(k, front - 2 * k, front % 2 == 1)

    lead = first + MOMENTS - 1 + lag
    pairs = (last - lead + 1) // 2
    for front in range(first, lead):
        front_step(front)

    def both(n, _):
        for part in range(2):
            front = lead + 2 * n + part
            contract(front - lag)
            for k in reversed(range(MOMENTS)):
                advance(k, front - 2 * k, (lead + part) % 2 == 1)
        return 0

    lax.fori_loop(0, pairs, both, 0)
    for front in range(lead + 2 * pairs, last - MOMENTS + 1 + lag + 1):
        front_step(front)
    for k in range(MOMENTS - 1):
        for side, at in enumerate((first, last - MOMENTS + 1)):
            edge_field[side, k] = field[k + 1, at : at + MOMENTS]
            edge_rim[side, k] = rim[k + 1, at : at + MOMENTS]
    for n, x in enumerate((0, 1, rows_x - 2, rows_x - 1)):
        ends_ref[n] = own_ref[x]


class Either:
    def __init__(self, flag, one, other):
        self.flag, self.one, self.other = flag, one, other

    def __getitem__(self, at):
        return jnp.where(self.flag, self.one[at], self.other[at])


def border_kernel(scale, order_ref, ends_ref, coup_ref, near_ref, next_ref, before_ref, after_ref, left_ref, part_ref, edge_field, edge_rim, out_ref, field, rim, coup, open_bond, acc, spaced, ranked):
    nright, width = ends_ref.shape[1:]
    rows_x = left_ref.shape[0]
    rows = rows_x + 2 * DEPTH
    inner, xtiles = width // LANES, rows_x // SUB
    base = DEPTH * nright + COUPLINGS * SUB
    even = lax.axis_index("sx") % 2 == 0
    lo_ref, hi_ref = Either(even, near_ref, next_ref), Either(even, next_ref, near_ref)

    def corner(ref, which, v):
        return ref[base + which * SUB : base + (which + 1) * SUB, v * LANES : (v + 1) * LANES]

    for e in range(DEPTH):
        rim[0, e] = rim_row(corner(lo_ref, 0, 0), corner(lo_ref, 1, 0), e - DEPTH)
        field[0, e] = lo_ref[e * nright : (e + 1) * nright, :]
        rim[0, e + DEPTH + rows_x] = rim_row(corner(hi_ref, 0, 0), corner(hi_ref, 1, 0), e)
        field[0, e + DEPTH + rows_x] = hi_ref[e * nright : (e + 1) * nright, :]
    for n, x in enumerate((0, 1, rows_x - 2, rows_x - 1)):
        rim[0, x + DEPTH] = rim_row(before_ref[x // SUB], after_ref[x // SUB], x)
        field[0, x + DEPTH] = ends_ref[n]

    def blocks_of(g, c, xt):
        at = DEPTH * nright + c * SUB
        lanes = [slice(i * LANES, (i + 1) * LANES) for i in range(inner)]
        if g == 0:
            return [lo_ref[at : at + SUB, i] for i in lanes]
        if g == xtiles + 1:
            return [hi_ref[at : at + SUB, i] for i in lanes]
        return [coup_ref[c, xt * SUB : (xt + 1) * SUB, i] for i in lanes]

    def strips_of(g):
        if g == 0:
            return corner(lo_ref, 0, 1), corner(lo_ref, 1, 1)
        if g == xtiles + 1:
            return corner(hi_ref, 0, 1), corner(hi_ref, 1, 1)
        return before_ref[xtiles], after_ref[xtiles]

    coupling_rows(blocks_of, strips_of, (0, 1, xtiles, xtiles + 1), xtiles, inner, coup, open_bond, rows)
    first, last = DEPTH + 1, DEPTH + rows_x - 2
    for k in range(MOMENTS - 1):
        for side, at in enumerate((first, last - MOMENTS + 1)):
            field[k + 1, at : at + MOMENTS] = edge_field[side, k]
            rim[k + 1, at : at + MOMENTS] = edge_rim[side, k]
    acc[...] = part_ref[...]
    advance, contract = stepper(field, rim, coup, open_bond, acc, left_ref)

    for front in range(1, DEPTH + 3 * (MOMENTS - 1) + 1):
        for k in reversed(range(MOMENTS)):
            if 3 * k + 1 <= front <= 3 * k + DEPTH:
                row = front - 2 * k
                advance(k, row, row % 2 == 1)
                advance(k, rows - 1 - row, (rows - 1 - row) % 2 == 1)
    for n in range(DEPTH):
        for row in (DEPTH - 1 + n, rows - DEPTH - n):
            contract(row, 0 <= row - 1 - DEPTH < rows_x, 0 <= row + 1 - DEPTH < rows_x)

    near, far, _, flat = out_ref.shape
    groups, owned = near * far, flat // nright
    both_sides = acc[...].T
    half = both_sides.shape[0] // 2
    total = (both_sides[:half] - both_sides[half:]) * scale
    for k in range(MOMENTS):
        spaced[:, 0:nright] = total[:, k * nright : (k + 1) * nright]
        rows_of = [spaced[pl.ds(q, groups, stride=owned), :] for q in range(owned)]
        ranked[k] = jnp.concatenate([r[:, 0:nright] for r in rows_of], axis=1)
    for j in range(MOMENTS):
        for n in range(far):
            out_ref[:, n, j, :] = ranked[order_ref[j], n * near : (n + 1) * near]


def vmem_call(kernel, name, out_shape, scratch, flops, *args, scalars=()):
    several = isinstance(out_shape, tuple)
    spec = pl.BlockSpec(memory_space=pltpu.VMEM)
    return pl.pallas_call(
        kernel,
        out_shape=out_shape,
        in_specs=[pl.BlockSpec(memory_space=pltpu.SMEM)] * len(scalars) + [spec] * len(args),
        out_specs=(spec,) * len(out_shape) if several else spec,
        scratch_shapes=scratch,
        compiler_params=pltpu.CompilerParams(vmem_limit_bytes=28 << 20),
        cost_estimate=pl.CostEstimate(flops=flops, bytes_accessed=1 << 22, transcendentals=0),
        name=name,
    )(*scalars, *args)


def scratch_of(rows_x, nright, width):
    rows = rows_x + 2 * DEPTH
    return [
        pltpu.VMEM((MOMENTS + 1, rows, nright, width), jnp.float32),
        pltpu.VMEM((MOMENTS + 1, rows, SUB, LANES), jnp.float32),
        pltpu.VMEM((rows, COUPLINGS, SUB, width + LANES), jnp.float32),
        pltpu.VMEM((rows, 2 * SUB, width), jnp.bfloat16),
    ]


def pairs(axis, start):
    size = lax.axis_size(axis)
    swaps = [(i % size, (i + 1) % size) for i in range(start, size + start, 2)]
    return swaps + [(b, a) for a, b in swaps]


def near_part(size):
    return 8 if size % 8 == 0 else size


def shards(right_vectors, left_vectors, classes, class_energy, bond_mask_grid, order):
    rows_x, rows_y = classes.shape
    nright, nleft = right_vectors.shape[0], left_vectors.shape[0]
    nsx, nsy = lax.axis_size("sx"), lax.axis_size("sy")
    owned = nleft // nsy
    even_x, even_y = lax.axis_index("sx") % 2 == 0, lax.axis_index("sy") % 2 == 0

    own, coup, near_payload, next_payload, beside, across = prepare(
        right_vectors, classes, class_energy, bond_mask_grid
    )
    with jax.named_scope("halo_y"):
        beside = lax.ppermute(beside, "sy", pairs("sy", -1))
        across = lax.ppermute(across, "sy", pairs("sy", 0))
    before, after = jnp.where(even_y, beside, across), jnp.where(even_y, across, beside)
    with jax.named_scope("halo_x"):
        def with_corners(payload, upper):
            corners = [
                jnp.concatenate([jnp.where(upper, part[0], part[-2]), part[-1]], axis=1) for part in (before, after)
            ]
            corners = jnp.concatenate(corners, axis=0)
            return lax.dynamic_update_slice(payload, corners, (payload.shape[0] - corners.shape[0], 0))

        near_payload = with_corners(near_payload, even_x)
        next_payload, _ = lax.optimization_barrier((next_payload, near_payload))
        near_rows = lax.ppermute(near_payload, "sx", pairs("sx", -1))
        next_rows = lax.ppermute(with_corners(next_payload, ~even_x), "sx", pairs("sx", 0))
    left = left_vectors.transpose(1, 0, 2)
    f32 = jnp.float32
    part, edge_field, edge_rim, ends = vmem_call(
        interior_kernel,
        "interior",
        (
            jax.ShapeDtypeStruct((MOMENTS * nright, 2 * nleft), f32),
            jax.ShapeDtypeStruct((2, MOMENTS - 1, MOMENTS, nright, rows_y), f32),
            jax.ShapeDtypeStruct((2, MOMENTS - 1, MOMENTS, SUB, LANES), f32),
            jax.ShapeDtypeStruct((4, nright, rows_y), f32),
        ),
        scratch_of(rows_x, nright, rows_y),
        1 << 33,
        own, coup, before, after, left,
    )
    near, depth_z = near_part(nsy), near_part(nsx)
    sites = rows_x * rows_y * nsx * nsy
    tile = vmem_call(
        functools.partial(border_kernel, -HALF_ROOT / sites**0.5),
        "border",
        jax.ShapeDtypeStruct((near, nsy // near, MOMENTS, owned * nright), f32),
        scratch_of(rows_x, nright, rows_y)
        + [
            pltpu.VMEM((MOMENTS * nright, 2 * nleft), f32),
            pltpu.VMEM((nleft, LANES), f32),
            pltpu.VMEM((MOMENTS, nsy, owned * nright), f32),
        ],
        1 << 32,
        ends, coup, near_rows, next_rows, before, after, left, part, edge_field, edge_rim,
        scalars=(order,),
    )
    far_y, far_x = nsy // near, nsx // depth_z
    block = tile.shape[2:]
    with jax.named_scope("reduce_near"):
        runs = [[n * near + i for i in range(near)] for n in range(far_y)]
        mine = jnp.sum(lax.all_to_all(tile, "sy", 0, 0, axis_index_groups=runs), axis=0)
    with jax.named_scope("reduce_far"):
        if far_y * far_x > 1:
            spread = jnp.broadcast_to(mine[:, None], (far_y, far_x) + block).reshape((far_y * far_x,) + block)
            rings = [
                [(m * depth_z + z) * nsy + n * near + i for n in range(far_y) for m in range(far_x)]
                for z in range(depth_z)
                for i in range(near)
            ]
            mine = lax.all_to_all(spread, ("sx", "sy"), 0, 0, axis_index_groups=rings)
        mine = jnp.sum(mine, axis=0)
    with jax.named_scope("reduce_z"):
        runs = [[m * depth_z + z for z in range(depth_z)] for m in range(far_x)]
        spread = jnp.broadcast_to(mine[None], (depth_z,) + block)
        shares = lax.all_to_all(spread, "sx", 0, 0, axis_index_groups=runs)
    total = jnp.sum(shares, axis=0)
    return jnp.stack([total[:, q * nright : (q + 1) * nright] for q in range(owned)], axis=1)


def solution(mesh):
    in_specs = (
        P(None, "sx", "sy"),
        P(None, "sx", "sy"),
        P("sx", "sy"),
        P(),
        P(None, "sx", "sy"),
        P(),
    )
    out_specs = P(None, "sy", None)
    return jax.shard_map(shards, mesh=mesh, in_specs=in_specs, out_specs=out_specs, check_vma=False)
```

```python
import functools

import jax
import jax.numpy as jnp
from jax import lax
from jax.experimental import pallas as pl
from jax.experimental.pallas import tpu as pltpu
from jax.sharding import PartitionSpec as P

MOMENTS = 5
HALF_ROOT = 0.8660254037844386
SPECTRAL = 4.6
TWICE = 2.0 / SPECTRAL
DEPTH = MOMENTS + 1
REACH = 3
SLOT = 4
COUPLINGS = 3
LANES = 128
SUB = 8
SPAN = 32


def lane_iota():
    return lax.broadcasted_iota(jnp.int32, (SUB, LANES), 1)


def turn(value, by):
    by %= LANES
    return pltpu.roll(value, by, 1) if by else value


def swap_major(blocks, sub):
    for s in (4, 2, 1):
        keep = (sub & s) == 0
        for i in range(SUB):
            if i & s == 0:
                a, b = blocks[i], blocks[i + s]
                blocks[i] = jnp.where(keep, a, pltpu.roll(b, s, 0))
                blocks[i + s] = jnp.where(keep, pltpu.roll(a, SUB - s, 0), b)
    return blocks


def prepare_kernel(energy_hbm, right_hbm, class_hbm, bond_hbm, own_hbm, coup_hbm, near_hbm, next_hbm, beside_hbm, across_hbm,
                   energy_ref, right_ref, class_ref, bond_ref, own_ref, coup_ref, rows_ref, strips_ref, in_sem, out_sem):
    nright, rows, width = right_ref.shape
    lane = lane_iota()
    sub = lax.broadcasted_iota(jnp.int32, (SUB, LANES), 0)
    xtiles, rtiles, inner = rows // SUB, nright // SUB, width // LANES
    halves = [pl.ds(h * 2 * SUB, 2 * SUB) for h in range(xtiles // 2)]
    reads = [pltpu.make_async_copy(right_hbm.at[:, h, :], right_ref.at[:, h, :], in_sem.at[n]) for n, h in enumerate(halves)]
    for n, (a, b) in enumerate(((energy_hbm, energy_ref), (class_hbm, class_ref), (bond_hbm, bond_ref))):
        reads.append(pltpu.make_async_copy(a, b, in_sem.at[len(halves) + n]))
    for copy in reads:
        copy.start()
    writes = []

    def write(source, target):
        copy = pltpu.make_async_copy(source, target, out_sem.at[len(writes)])
        copy.start()
        writes.append(copy)

    top_at, first_at = lax.axis_index("sx") % 2, lax.axis_index("sy") % 2
    zero = jnp.zeros((SUB, LANES), jnp.float32)
    first, last = [zero] * (xtiles + 1), [zero] * (xtiles + 1)

    def strip(v, at, i, block):
        here = (lane >= at) & (lane < at + REACH)
        if i == 0:
            first[v] = jnp.where(here, turn(block, at), first[v])
        if i == inner - 1:
            last[v] = jnp.where(here, turn(block, at + REACH), last[v])

    for half in range(xtiles // 2):
        reads[half].wait()
        for i in range(inner):
            lanes = slice(i * LANES, (i + 1) * LANES)
            for t in range(rtiles):
                wide = [
                    right_ref[t * SUB + q, half * 2 * SUB : (half + 1) * 2 * SUB, lanes].astype(jnp.float32)
                    for q in range(SUB)
                ]
                for part in range(2):
                    xt = half * 2 + part
                    turned = swap_major([w[part * SUB : (part + 1) * SUB] for w in wide], sub)
                    for j in range(SUB):
                        x = xt * SUB + j
                        own_ref[x, t * SUB : (t + 1) * SUB, lanes] = turned[j]
                        if x < DEPTH:
                            rows_ref[top_at, x * nright + t * SUB : x * nright + (t + 1) * SUB, lanes] = turned[j]
                        if x >= rows - DEPTH:
                            at = (x - rows + DEPTH) * nright + t * SUB
                            rows_ref[1 - top_at, at : at + SUB, lanes] = turned[j]
                        strip(xt, t * SPAN + j * SLOT, i, turned[j])
        write(own_ref.at[halves[half]], own_hbm.at[halves[half]])
    for copy in reads[len(halves) :]:
        copy.wait()
    for xt in range(xtiles):
        here = slice(xt * SUB, (xt + 1) * SUB)
        for i in range(inner):
            lanes = slice(i * LANES, (i + 1) * LANES)
            kinds = class_ref[here, lanes]
            energy = zero
            for level in range(energy_ref.shape[0]):
                energy = jnp.where(kinds == level, energy_ref[level] * TWICE, energy)
            fields = [bond_ref[c, here, lanes].astype(jnp.float32) * TWICE for c in range(2)] + [energy]
            for c in range(COUPLINGS):
                coup_ref[c, here, lanes] = fields[c]
                strip(xtiles, (c * xtiles + xt) * SLOT, i, fields[c])
                at = DEPTH * nright + c * SUB
                if xt == 0:
                    rows_ref[top_at, at : at + SUB, lanes] = fields[c]
                if xt == xtiles - 1:
                    rows_ref[1 - top_at, at : at + SUB, lanes] = fields[c]
    for v in range(xtiles + 1):
        strips_ref[first_at, v] = first[v]
        strips_ref[1 - first_at, v] = last[v]
    write(strips_ref.at[0], beside_hbm)
    write(strips_ref.at[1], across_hbm)
    filled = pl.ds(0, rows_ref.shape[1])
    write(rows_ref.at[0], near_hbm.at[filled])
    write(rows_ref.at[1], next_hbm.at[filled])
    write(coup_ref, coup_hbm)
    for copy in writes:
        copy.wait()


def prepare(right, classes, energy, bonds):
    nright, rows, width = right.shape
    edge = DEPTH * nright + COUPLINGS * SUB
    f32 = jnp.float32
    own, coup = (rows, nright, width), (COUPLINGS, rows, width)
    strip = (rows // SUB + 1, SUB, LANES)
    halves = rows // (2 * SUB)
    return pl.pallas_call(
        prepare_kernel,
        out_shape=tuple(
            jax.ShapeDtypeStruct(shape, f32)
            for shape in (own, coup, (edge + 2 * SUB, width), (edge + 2 * SUB, width), strip, strip)
        ),
        in_specs=[pl.BlockSpec(memory_space=pltpu.HBM)] * 4,
        out_specs=(pl.BlockSpec(memory_space=pltpu.HBM),) * 6,
        scratch_shapes=[
            pltpu.SMEM(energy.shape, energy.dtype),
            pltpu.VMEM(right.shape, right.dtype),
            pltpu.VMEM(classes.shape, classes.dtype),
            pltpu.VMEM(bonds.shape, bonds.dtype),
            pltpu.VMEM(own, f32),
            pltpu.VMEM(coup, f32),
            pltpu.VMEM((2, edge, width), f32),
            pltpu.VMEM((2,) + strip, f32),
            pltpu.SemaphoreType.DMA((halves + 3,)),
            pltpu.SemaphoreType.DMA((halves + 5,)),
        ],
        name="prepare",
    )(energy, right, classes, bonds)


def swapped(block, lane, odd):
    low = (lane & 1) == (1 if odd else 0)
    target = jnp.where(low, lane + 1, lane + LANES - 1) & (LANES - 1)
    return jnp.take_along_axis(block, target, axis=1)


def coupling_rows(blocks_of, strips_of, groups, xtiles, inner, coup, open_bond, rows):
    lane = lane_iota()
    sub = lax.broadcasted_iota(jnp.int32, (SUB, LANES), 0)
    zero = jnp.zeros((SUB, LANES), jnp.float32)
    for g in groups:
        xt = (g - 1) % xtiles
        before, after = strips_of(g)
        whole = []
        for c in range(COUPLINGS):
            blocks = blocks_of(g, c, xt)
            shift = (c * xtiles + xt) * SLOT
            blocks.append(
                jnp.where(
                    lane < REACH,
                    turn(after, -shift),
                    jnp.where(lane >= LANES - REACH, turn(before, -shift - REACH), zero),
                )
            )
            if c == 1:
                even = [swapped(b, lane, False) for b in blocks]
                odd = [swapped(b, lane, True) for b in blocks]
                n = len(blocks)
                odd = [
                    jnp.where(lane == 0, odd[(i - 1) % n], jnp.where(lane == LANES - 1, odd[(i + 1) % n], odd[i]))
                    for i in range(n)
                ]
                blocks = [
                    jnp.where(((lane + sub) & 1) == 0, b, jnp.where((sub & 1) == 1, o, v))
                    for b, o, v in zip(blocks, odd, even)
                ]
            edge = blocks[inner]
            edge = edge + turn(edge, LANES // 2)
            blocks[inner] = edge + turn(edge, LANES // 4)
            whole.append(blocks)
        for s in range(SUB):
            e = (g - 1) * SUB + s + DEPTH
            if 0 <= e < rows:
                for c in range(COUPLINGS):
                    for i in range(inner + 1):
                        wide = jnp.broadcast_to(whole[c][i][s : s + 1], (SUB, LANES))
                        coup[e, c, :, i * LANES : (i + 1) * LANES] = wide
                        if c == 0 and i < inner:
                            shown = (wide > 0.0).astype(jnp.float32)
                            open_bond[e, :, i * LANES : (i + 1) * LANES] = jnp.concatenate(
                                [shown, shown], axis=0
                            ).astype(jnp.bfloat16)


def rim_row(before, after, x):
    lane = lane_iota()
    shift = (x % SUB) * SLOT
    return jnp.where(
        lane % SPAN < REACH,
        turn(after, -shift),
        jnp.where(lane % SPAN >= SPAN - REACH, turn(before, -shift - REACH), jnp.zeros((SUB, LANES), jnp.float32)),
    )


def stepper(field, rim, coup, open_bond, acc, left_ref, source=None):
    nright, width = field.shape[2:]
    rtiles, inner = nright // SUB, width // LANES
    rows_x = left_ref.shape[0]
    lane = lane_iota()

    def lanes_of(i):
        return slice(i * LANES, (i + 1) * LANES)

    def load(k, row, t, i):
        if i == inner:
            return rim[k, row]
        if k == 0 and source is not None:
            return source[row - DEPTH, t * SUB : (t + 1) * SUB, lanes_of(i)]
        return field[k, row, t * SUB : (t + 1) * SUB, lanes_of(i)]

    def coupling(c, row, i):
        return coup[row, c, :, lanes_of(i)]

    where = [(t, i) for t in range(rtiles) for i in range(inner)] + [(0, inner)]

    def partners(here, odd):
        moved = {at: swapped(value, lane, odd) for at, value in here.items()}
        if not odd:
            return moved
        edge = moved[0, inner]
        start, end = lane == 0, lane == LANES - 1
        result, fill = {}, edge
        for t in range(rtiles):
            outer = turn(edge, -t * SPAN)
            for i in range(inner):
                left = moved[t, i - 1] if i else outer
                right = moved[t, i + 1] if i < inner - 1 else outer
                result[t, i] = jnp.where(start, left, jnp.where(end, right, moved[t, i]))
            facing = turn(jnp.where(lane < LANES // 2, moved[t, inner - 1], moved[t, 0]), t * SPAN)
            fill = jnp.where((lane == t * SPAN) | (lane == (t * SPAN - 1) % LANES), facing, fill)
        result[0, inner] = fill
        return result

    def advance(k, row, odd):
        here = {at: load(k, row, *at) for at in where}
        turned = partners(here, odd)
        east = [coupling(0, row, i) for i in range(inner + 1)]
        west = [coupling(0, row - 1, i) for i in range(inner + 1)]
        vertical = [coupling(1, row, i) for i in range(inner + 1)]
        site = [coupling(2, row, i) for i in range(inner + 1)] if k else None
        sign = jnp.where((lane & 1) == (1 if odd else 0), 1.0 / TWICE, -1.0 / TWICE)
        new = {}
        for t, i in where:
            beside = east[i] * load(k, row + 1, t, i) + west[i] * load(k, row - 1, t, i)
            across = vertical[i] * turned[t, i]
            if k == 0:
                new[t, i] = sign * (0.5 * beside - across)
            else:
                image = site[i] * here[t, i] - beside - across
                new[t, i] = 0.5 * image if k == 1 else image - load(k - 1, row, t, i)
        for t, i in where:
            if i == inner:
                rim[k + 1, row] = new[t, i]
            else:
                field[k + 1, row, t * SUB : (t + 1) * SUB, lanes_of(i)] = new[t, i]

    def contract(row, below=True, above=True):
        parts = []
        for t in range(rtiles * MOMENTS):
            k, q = divmod(t, rtiles)
            parts.append(field[k + 1, row, q * SUB : (q + 1) * SUB, :])
        value = jnp.concatenate(parts, axis=0)
        high = value.astype(jnp.bfloat16)
        low = (value - high.astype(jnp.float32)).astype(jnp.bfloat16)
        sides = []
        for there, bond, wanted in ((row - 1, row - 1, below), (row + 1, row, above)):
            for q in range(left_ref.shape[1] // (2 * SUB)):
                if wanted:
                    sides.append(left_ref[there - DEPTH, q * 2 * SUB : (q + 1) * 2 * SUB, :] * open_bond[bond])
                else:
                    sides.append(jnp.zeros((2 * SUB, width), jnp.bfloat16))
        block = jnp.concatenate(sides, axis=0)
        acc[...] += lax.dot_general(
            jnp.concatenate([high, low], axis=1),
            jnp.concatenate([block, block], axis=1),
            (((1,), (1,)), ((), ())),
            preferred_element_type=jnp.float32,
        )

    return advance, contract


def interior_kernel(own_ref, coup_ref, before_ref, after_ref, left_ref, acc, edge_field, edge_rim, ends_ref, field, rim, coup, open_bond):
    rows_x, nright, width = own_ref.shape
    rows = rows_x + 2 * DEPTH
    inner, xtiles = width // LANES, rows_x // SUB
    for x in range(rows_x):
        rim[0, x + DEPTH] = rim_row(before_ref[x // SUB], after_ref[x // SUB], x)

    def blocks_of(g, c, xt):
        return [coup_ref[c, xt * SUB : (xt + 1) * SUB, i * LANES : (i + 1) * LANES] for i in range(inner)]

    def strips_of(g):
        return before_ref[xtiles], after_ref[xtiles]

    coupling_rows(blocks_of, strips_of, range(1, xtiles + 1), xtiles, inner, coup, open_bond, rows)
    acc[...] = jnp.zeros_like(acc)
    advance, contract = stepper(field, rim, coup, open_bond, acc, left_ref, own_ref)

    first, last = DEPTH + 1, DEPTH + rows_x - 2
    lag = 2 * MOMENTS - 1

    def front_step(front):
        if first + MOMENTS - 1 <= front - lag <= last - MOMENTS + 1:
            contract(front - lag)
        for k in reversed(range(MOMENTS)):
            if first + 3 * k <= front <= last + k:
                advance(k, front - 2 * k, front % 2 == 1)

    lead = first + MOMENTS - 1 + lag
    pairs = (last - lead + 1) // 2
    for front in range(first, lead):
        front_step(front)

    def both(n, _):
        for part in range(2):
            front = lead + 2 * n + part
            contract(front - lag)
            for k in reversed(range(MOMENTS)):
                advance(k, front - 2 * k, (lead + part) % 2 == 1)
        return 0

    lax.fori_loop(0, pairs, both, 0)
    for front in range(lead + 2 * pairs, last - MOMENTS + 1 + lag + 1):
        front_step(front)
    for k in range(MOMENTS - 1):
        for side, at in enumerate((first, last - MOMENTS + 1)):
            edge_field[side, k] = field[k + 1, at : at + MOMENTS]
            edge_rim[side, k] = rim[k + 1, at : at + MOMENTS]
    for n, x in enumerate((0, 1, rows_x - 2, rows_x - 1)):
        ends_ref[n] = own_ref[x]


class Either:
    def __init__(self, flag, one, other):
        self.flag, self.one, self.other = flag, one, other

    def __getitem__(self, at):
        return jnp.where(self.flag, self.one[at], self.other[at])


def border_kernel(scale, order_ref, ends_ref, coup_ref, near_ref, next_ref, before_ref, after_ref, left_ref, part_ref, edge_field, edge_rim, out_ref, field, rim, coup, open_bond, acc, spaced, ranked):
    nright, width = ends_ref.shape[1:]
    rows_x = left_ref.shape[0]
    rows = rows_x + 2 * DEPTH
    inner, xtiles = width // LANES, rows_x // SUB
    base = DEPTH * nright + COUPLINGS * SUB
    even = lax.axis_index("sx") % 2 == 0
    lo_ref, hi_ref = Either(even, near_ref, next_ref), Either(even, next_ref, near_ref)

    def corner(ref, which, v):
        return ref[base + which * SUB : base + (which + 1) * SUB, v * LANES : (v + 1) * LANES]

    for e in range(DEPTH):
        rim[0, e] = rim_row(corner(lo_ref, 0, 0), corner(lo_ref, 1, 0), e - DEPTH)
        field[0, e] = lo_ref[e * nright : (e + 1) * nright, :]
        rim[0, e + DEPTH + rows_x] = rim_row(corner(hi_ref, 0, 0), corner(hi_ref, 1, 0), e)
        field[0, e + DEPTH + rows_x] = hi_ref[e * nright : (e + 1) * nright, :]
    for n, x in enumerate((0, 1, rows_x - 2, rows_x - 1)):
        rim[0, x + DEPTH] = rim_row(before_ref[x // SUB], after_ref[x // SUB], x)
        field[0, x + DEPTH] = ends_ref[n]

    def blocks_of(g, c, xt):
        at = DEPTH * nright + c * SUB
        lanes = [slice(i * LANES, (i + 1) * LANES) for i in range(inner)]
        if g == 0:
            return [lo_ref[at : at + SUB, i] for i in lanes]
        if g == xtiles + 1:
            return [hi_ref[at : at + SUB, i] for i in lanes]
        return [coup_ref[c, xt * SUB : (xt + 1) * SUB, i] for i in lanes]

    def strips_of(g):
        if g == 0:
            return corner(lo_ref, 0, 1), corner(lo_ref, 1, 1)
        if g == xtiles + 1:
            return corner(hi_ref, 0, 1), corner(hi_ref, 1, 1)
        return before_ref[xtiles], after_ref[xtiles]

    coupling_rows(blocks_of, strips_of, (0, 1, xtiles, xtiles + 1), xtiles, inner, coup, open_bond, rows)
    first, last = DEPTH + 1, DEPTH + rows_x - 2
    for k in range(MOMENTS - 1):
        for side, at in enumerate((first, last - MOMENTS + 1)):
            field[k + 1, at : at + MOMENTS] = edge_field[side, k]
            rim[k + 1, at : at + MOMENTS] = edge_rim[side, k]
    acc[...] = part_ref[...]
    advance, contract = stepper(field, rim, coup, open_bond, acc, left_ref)

    for front in range(1, DEPTH + 3 * (MOMENTS - 1) + 1):
        for k in reversed(range(MOMENTS)):
            if 3 * k + 1 <= front <= 3 * k + DEPTH:
                row = front - 2 * k
                advance(k, row, row % 2 == 1)
                advance(k, rows - 1 - row, (rows - 1 - row) % 2 == 1)
    for n in range(DEPTH):
        for row in (DEPTH - 1 + n, rows - DEPTH - n):
            contract(row, 0 <= row - 1 - DEPTH < rows_x, 0 <= row + 1 - DEPTH < rows_x)

    near, far, _, flat = out_ref.shape
    groups, owned = near * far, flat // nright
    both_sides = acc[...].T
    half = both_sides.shape[0] // 2
    total = (both_sides[:half] - both_sides[half:]) * scale
    for k in range(MOMENTS):
        spaced[:, 0:nright] = total[:, k * nright : (k + 1) * nright]
        rows_of = [spaced[pl.ds(q, groups, stride=owned), :] for q in range(owned)]
        ranked[k] = jnp.concatenate([r[:, 0:nright] for r in rows_of], axis=1)
    for j in range(MOMENTS):
        for n in range(far):
            out_ref[:, n, j, :] = ranked[order_ref[j], n * near : (n + 1) * near]


def vmem_call(kernel, name, out_shape, scratch, flops, *args, scalars=()):
    several = isinstance(out_shape, tuple)
    spec = pl.BlockSpec(memory_space=pltpu.VMEM)
    return pl.pallas_call(
        kernel,
        out_shape=out_shape,
        in_specs=[pl.BlockSpec(memory_space=pltpu.SMEM)] * len(scalars) + [spec] * len(args),
        out_specs=(spec,) * len(out_shape) if several else spec,
        scratch_shapes=scratch,
        compiler_params=pltpu.CompilerParams(vmem_limit_bytes=28 << 20),
        cost_estimate=pl.CostEstimate(flops=flops, bytes_accessed=1 << 22, transcendentals=0),
        name=name,
    )(*scalars, *args)


def scratch_of(rows_x, nright, width):
    rows = rows_x + 2 * DEPTH
    return [
        pltpu.VMEM((MOMENTS + 1, rows, nright, width), jnp.float32),
        pltpu.VMEM((MOMENTS + 1, rows, SUB, LANES), jnp.float32),
        pltpu.VMEM((rows, COUPLINGS, SUB, width + LANES), jnp.float32),
        pltpu.VMEM((rows, 2 * SUB, width), jnp.bfloat16),
    ]


def pairs(axis, start):
    size = lax.axis_size(axis)
    swaps = [(i % size, (i + 1) % size) for i in range(start, size + start, 2)]
    return swaps + [(b, a) for a, b in swaps]


def near_part(size):
    return 8 if size % 8 == 0 else size


def shards(right_vectors, left_vectors, classes, class_energy, bond_mask_grid, order):
    rows_x, rows_y = classes.shape
    nright, nleft = right_vectors.shape[0], left_vectors.shape[0]
    nsx, nsy = lax.axis_size("sx"), lax.axis_size("sy")
    owned = nleft // nsy
    even_x, even_y = lax.axis_index("sx") % 2 == 0, lax.axis_index("sy") % 2 == 0

    own, coup, near_payload, next_payload, beside, across = prepare(
        right_vectors, classes, class_energy, bond_mask_grid
    )
    with jax.named_scope("halo_y"):
        beside = lax.ppermute(beside, "sy", pairs("sy", -1))
        across = lax.ppermute(across, "sy", pairs("sy", 0))
    before, after = jnp.where(even_y, beside, across), jnp.where(even_y, across, beside)
    with jax.named_scope("halo_x"):
        def with_corners(payload, upper):
            corners = [
                jnp.concatenate([jnp.where(upper, part[0], part[-2]), part[-1]], axis=1) for part in (before, after)
            ]
            corners = jnp.concatenate(corners, axis=0)
            return lax.dynamic_update_slice(payload, corners, (payload.shape[0] - corners.shape[0], 0))

        near_payload = with_corners(near_payload, even_x)
        next_payload, _ = lax.optimization_barrier((next_payload, near_payload))
        near_rows = lax.ppermute(near_payload, "sx", pairs("sx", -1))
        next_rows = lax.ppermute(with_corners(next_payload, ~even_x), "sx", pairs("sx", 0))
    left = left_vectors.transpose(1, 0, 2)
    f32 = jnp.float32
    part, edge_field, edge_rim, ends = vmem_call(
        interior_kernel,
        "interior",
        (
            jax.ShapeDtypeStruct((MOMENTS * nright, 2 * nleft), f32),
            jax.ShapeDtypeStruct((2, MOMENTS - 1, MOMENTS, nright, rows_y), f32),
            jax.ShapeDtypeStruct((2, MOMENTS - 1, MOMENTS, SUB, LANES), f32),
            jax.ShapeDtypeStruct((4, nright, rows_y), f32),
        ),
        scratch_of(rows_x, nright, rows_y),
        1 << 33,
        own, coup, before, after, left,
    )
    near = near_part(nsy)
    sites = rows_x * rows_y * nsx * nsy
    tile = vmem_call(
        functools.partial(border_kernel, -HALF_ROOT / sites**0.5),
        "border",
        jax.ShapeDtypeStruct((near, nsy // near, MOMENTS, owned * nright), f32),
        scratch_of(rows_x, nright, rows_y)
        + [
            pltpu.VMEM((MOMENTS * nright, 2 * nleft), f32),
            pltpu.VMEM((nleft, LANES), f32),
            pltpu.VMEM((MOMENTS, nsy, owned * nright), f32),
        ],
        1 << 32,
        ends, coup, near_rows, next_rows, before, after, left, part, edge_field, edge_rim,
        scalars=(order,),
    )
    far_y = nsy // near
    block = tile.shape[2:]
    with jax.named_scope("reduce_near"):
        runs = [[n * near + i for i in range(near)] for n in range(far_y)]
        mine = jnp.sum(lax.all_to_all(tile, "sy", 0, 0, axis_index_groups=runs), axis=0)
    with jax.named_scope("reduce_far"):
        spread = jnp.broadcast_to(mine[:, None], (far_y, nsx) + block).reshape((far_y * nsx,) + block)
        planes = [[m * nsy + n * near + i for n in range(far_y) for m in range(nsx)] for i in range(near)]
        shares = lax.all_to_all(spread, ("sx", "sy"), 0, 0, axis_index_groups=planes)
    total = jnp.sum(shares, axis=0)
    return jnp.stack([total[:, q * nright : (q + 1) * nright] for q in range(owned)], axis=1)


def solution(mesh):
    in_specs = (
        P(None, "sx", "sy"),
        P(None, "sx", "sy"),
        P("sx", "sy"),
        P(),
        P(None, "sx", "sy"),
        P(),
    )
    out_specs = P(None, "sy", None)
    return jax.shard_map(shards, mesh=mesh, in_specs=in_specs, out_specs=out_specs, check_vma=False)
```

```python
import functools

import jax
import jax.numpy as jnp
from jax import lax
from jax.experimental import pallas as pl
from jax.experimental.pallas import tpu as pltpu
from jax.sharding import PartitionSpec as P

MOMENTS = 5
HALF_ROOT = 0.8660254037844386
SPECTRAL = 4.6
TWICE = 2.0 / SPECTRAL
DEPTH = MOMENTS + 1
REACH = 3
SLOT = 4
COUPLINGS = 3
LANES = 128
SUB = 8
SPAN = 32


def lane_iota():
    return lax.broadcasted_iota(jnp.int32, (SUB, LANES), 1)


def turn(value, by):
    by %= LANES
    return pltpu.roll(value, by, 1) if by else value


def swap_major(blocks, sub):
    for s in (4, 2, 1):
        keep = (sub & s) == 0
        for i in range(SUB):
            if i & s == 0:
                a, b = blocks[i], blocks[i + s]
                blocks[i] = jnp.where(keep, a, pltpu.roll(b, s, 0))
                blocks[i + s] = jnp.where(keep, pltpu.roll(a, SUB - s, 0), b)
    return blocks


def prepare_kernel(energy_hbm, right_hbm, class_hbm, bond_hbm, own_hbm, coup_hbm, near_hbm, next_hbm, beside_hbm, across_hbm,
                   energy_ref, right_ref, class_ref, bond_ref, own_ref, coup_ref, rows_ref, strips_ref, in_sem, out_sem):
    nright, rows, width = right_ref.shape
    lane = lane_iota()
    sub = lax.broadcasted_iota(jnp.int32, (SUB, LANES), 0)
    xtiles, rtiles, inner = rows // SUB, nright // SUB, width // LANES
    halves = [pl.ds(h * 2 * SUB, 2 * SUB) for h in range(xtiles // 2)]
    reads = [pltpu.make_async_copy(right_hbm.at[:, h, :], right_ref.at[:, h, :], in_sem.at[n]) for n, h in enumerate(halves)]
    for n, (a, b) in enumerate(((energy_hbm, energy_ref), (class_hbm, class_ref), (bond_hbm, bond_ref))):
        reads.append(pltpu.make_async_copy(a, b, in_sem.at[len(halves) + n]))
    for copy in reads:
        copy.start()
    writes = []

    def write(source, target):
        copy = pltpu.make_async_copy(source, target, out_sem.at[len(writes)])
        copy.start()
        writes.append(copy)

    top_at, first_at = lax.axis_index("sx") % 2, lax.axis_index("sy") % 2
    zero = jnp.zeros((SUB, LANES), jnp.float32)
    first, last = [zero] * (xtiles + 1), [zero] * (xtiles + 1)

    def strip(v, at, i, block):
        here = (lane >= at) & (lane < at + REACH)
        if i == 0:
            first[v] = jnp.where(here, turn(block, at), first[v])
        if i == inner - 1:
            last[v] = jnp.where(here, turn(block, at + REACH), last[v])

    for half in range(xtiles // 2):
        reads[half].wait()
        for i in range(inner):
            lanes = slice(i * LANES, (i + 1) * LANES)
            for t in range(rtiles):
                wide = [
                    right_ref[t * SUB + q, half * 2 * SUB : (half + 1) * 2 * SUB, lanes].astype(jnp.float32)
                    for q in range(SUB)
                ]
                for part in range(2):
                    xt = half * 2 + part
                    turned = swap_major([w[part * SUB : (part + 1) * SUB] for w in wide], sub)
                    for j in range(SUB):
                        x = xt * SUB + j
                        own_ref[x, t * SUB : (t + 1) * SUB, lanes] = turned[j]
                        if x < DEPTH:
                            rows_ref[top_at, x * nright + t * SUB : x * nright + (t + 1) * SUB, lanes] = turned[j]
                        if x >= rows - DEPTH:
                            at = (x - rows + DEPTH) * nright + t * SUB
                            rows_ref[1 - top_at, at : at + SUB, lanes] = turned[j]
                        strip(xt, t * SPAN + j * SLOT, i, turned[j])
        write(own_ref.at[halves[half]], own_hbm.at[halves[half]])
    for copy in reads[len(halves) :]:
        copy.wait()
    for xt in range(xtiles):
        here = slice(xt * SUB, (xt + 1) * SUB)
        for i in range(inner):
            lanes = slice(i * LANES, (i + 1) * LANES)
            kinds = class_ref[here, lanes]
            energy = zero
            for level in range(energy_ref.shape[0]):
                energy = jnp.where(kinds == level, energy_ref[level] * TWICE, energy)
            fields = [bond_ref[c, here, lanes].astype(jnp.float32) * TWICE for c in range(2)] + [energy]
            for c in range(COUPLINGS):
                coup_ref[c, here, lanes] = fields[c]
                strip(xtiles, (c * xtiles + xt) * SLOT, i, fields[c])
                at = DEPTH * nright + c * SUB
                if xt == 0:
                    rows_ref[top_at, at : at + SUB, lanes] = fields[c]
                if xt == xtiles - 1:
                    rows_ref[1 - top_at, at : at + SUB, lanes] = fields[c]
    for v in range(xtiles + 1):
        strips_ref[first_at, v] = first[v]
        strips_ref[1 - first_at, v] = last[v]
    write(strips_ref.at[0], beside_hbm)
    write(strips_ref.at[1], across_hbm)
    filled = pl.ds(0, rows_ref.shape[1])
    write(rows_ref.at[0], near_hbm.at[filled])
    write(rows_ref.at[1], next_hbm.at[filled])
    write(coup_ref, coup_hbm)
    for copy in writes:
        copy.wait()


def prepare(right, classes, energy, bonds):
    nright, rows, width = right.shape
    edge = DEPTH * nright + COUPLINGS * SUB
    f32 = jnp.float32
    own, coup = (rows, nright, width), (COUPLINGS, rows, width)
    strip = (rows // SUB + 1, SUB, LANES)
    halves = rows // (2 * SUB)
    return pl.pallas_call(
        prepare_kernel,
        out_shape=tuple(
            jax.ShapeDtypeStruct(shape, f32)
            for shape in (own, coup, (edge + 2 * SUB, width), (edge + 2 * SUB, width), strip, strip)
        ),
        in_specs=[pl.BlockSpec(memory_space=pltpu.HBM)] * 4,
        out_specs=(pl.BlockSpec(memory_space=pltpu.HBM),) * 6,
        scratch_shapes=[
            pltpu.SMEM(energy.shape, energy.dtype),
            pltpu.VMEM(right.shape, right.dtype),
            pltpu.VMEM(classes.shape, classes.dtype),
            pltpu.VMEM(bonds.shape, bonds.dtype),
            pltpu.VMEM(own, f32),
            pltpu.VMEM(coup, f32),
            pltpu.VMEM((2, edge, width), f32),
            pltpu.VMEM((2,) + strip, f32),
            pltpu.SemaphoreType.DMA((halves + 3,)),
            pltpu.SemaphoreType.DMA((halves + 5,)),
        ],
        name="prepare",
    )(energy, right, classes, bonds)


def swapped(block, lane, odd):
    low = (lane & 1) == (1 if odd else 0)
    target = jnp.where(low, lane + 1, lane + LANES - 1) & (LANES - 1)
    return jnp.take_along_axis(block, target, axis=1)


def coupling_rows(blocks_of, strips_of, groups, xtiles, inner, coup, open_bond, rows):
    lane = lane_iota()
    sub = lax.broadcasted_iota(jnp.int32, (SUB, LANES), 0)
    zero = jnp.zeros((SUB, LANES), jnp.float32)
    for g in groups:
        xt = (g - 1) % xtiles
        before, after = strips_of(g)
        whole = []
        for c in range(COUPLINGS):
            blocks = blocks_of(g, c, xt)
            shift = (c * xtiles + xt) * SLOT
            blocks.append(
                jnp.where(
                    lane < REACH,
                    turn(after, -shift),
                    jnp.where(lane >= LANES - REACH, turn(before, -shift - REACH), zero),
                )
            )
            if c == 1:
                even = [swapped(b, lane, False) for b in blocks]
                odd = [swapped(b, lane, True) for b in blocks]
                n = len(blocks)
                odd = [
                    jnp.where(lane == 0, odd[(i - 1) % n], jnp.where(lane == LANES - 1, odd[(i + 1) % n], odd[i]))
                    for i in range(n)
                ]
                blocks = [
                    jnp.where(((lane + sub) & 1) == 0, b, jnp.where((sub & 1) == 1, o, v))
                    for b, o, v in zip(blocks, odd, even)
                ]
            edge = blocks[inner]
            edge = edge + turn(edge, LANES // 2)
            blocks[inner] = edge + turn(edge, LANES // 4)
            whole.append(blocks)
        for s in range(SUB):
            e = (g - 1) * SUB + s + DEPTH
            if 0 <= e < rows:
                for c in range(COUPLINGS):
                    for i in range(inner + 1):
                        wide = jnp.broadcast_to(whole[c][i][s : s + 1], (SUB, LANES))
                        coup[e, c, :, i * LANES : (i + 1) * LANES] = wide
                        if c == 0 and i < inner:
                            shown = (wide > 0.0).astype(jnp.float32)
                            open_bond[e, :, i * LANES : (i + 1) * LANES] = jnp.concatenate(
                                [shown, shown], axis=0
                            ).astype(jnp.bfloat16)


def rim_row(before, after, x):
    lane = lane_iota()
    shift = (x % SUB) * SLOT
    return jnp.where(
        lane % SPAN < REACH,
        turn(after, -shift),
        jnp.where(lane % SPAN >= SPAN - REACH, turn(before, -shift - REACH), jnp.zeros((SUB, LANES), jnp.float32)),
    )


def stepper(field, rim, coup, open_bond, acc, left_ref, source=None):
    nright, width = field.shape[2:]
    rtiles, inner = nright // SUB, width // LANES
    rows_x = left_ref.shape[0]
    lane = lane_iota()

    def lanes_of(i):
        return slice(i * LANES, (i + 1) * LANES)

    def load(k, row, t, i):
        if i == inner:
            return rim[k, row]
        if k == 0 and source is not None:
            return source[row - DEPTH, t * SUB : (t + 1) * SUB, lanes_of(i)]
        return field[k, row, t * SUB : (t + 1) * SUB, lanes_of(i)]

    def coupling(c, row, i):
        return coup[row, c, :, lanes_of(i)]

    where = [(t, i) for t in range(rtiles) for i in range(inner)] + [(0, inner)]

    def partners(here, odd):
        moved = {at: swapped(value, lane, odd) for at, value in here.items()}
        if not odd:
            return moved
        edge = moved[0, inner]
        start, end = lane == 0, lane == LANES - 1
        result, fill = {}, edge
        for t in range(rtiles):
            outer = turn(edge, -t * SPAN)
            for i in range(inner):
                left = moved[t, i - 1] if i else outer
                right = moved[t, i + 1] if i < inner - 1 else outer
                result[t, i] = jnp.where(start, left, jnp.where(end, right, moved[t, i]))
            facing = turn(jnp.where(lane < LANES // 2, moved[t, inner - 1], moved[t, 0]), t * SPAN)
            fill = jnp.where((lane == t * SPAN) | (lane == (t * SPAN - 1) % LANES), facing, fill)
        result[0, inner] = fill
        return result

    def advance(k, row, odd):
        here = {at: load(k, row, *at) for at in where}
        turned = partners(here, odd)
        east = [coupling(0, row, i) for i in range(inner + 1)]
        west = [coupling(0, row - 1, i) for i in range(inner + 1)]
        vertical = [coupling(1, row, i) for i in range(inner + 1)]
        site = [coupling(2, row, i) for i in range(inner + 1)] if k else None
        sign = jnp.where((lane & 1) == (1 if odd else 0), 1.0 / TWICE, -1.0 / TWICE)
        new = {}
        for t, i in where:
            beside = east[i] * load(k, row + 1, t, i) + west[i] * load(k, row - 1, t, i)
            across = vertical[i] * turned[t, i]
            if k == 0:
                new[t, i] = sign * (0.5 * beside - across)
            else:
                image = site[i] * here[t, i] - beside - across
                new[t, i] = 0.5 * image if k == 1 else image - load(k - 1, row, t, i)
        for t, i in where:
            if i == inner:
                rim[k + 1, row] = new[t, i]
            else:
                field[k + 1, row, t * SUB : (t + 1) * SUB, lanes_of(i)] = new[t, i]

    def contract(row, below=True, above=True):
        parts = []
        for t in range(rtiles * MOMENTS):
            k, q = divmod(t, rtiles)
            parts.append(field[k + 1, row, q * SUB : (q + 1) * SUB, :])
        value = jnp.concatenate(parts, axis=0)
        high = value.astype(jnp.bfloat16)
        low = (value - high.astype(jnp.float32)).astype(jnp.bfloat16)
        sides = []
        for there, bond, wanted in ((row - 1, row - 1, below), (row + 1, row, above)):
            for q in range(left_ref.shape[1] // (2 * SUB)):
                if wanted:
                    sides.append(left_ref[there - DEPTH, q * 2 * SUB : (q + 1) * 2 * SUB, :] * open_bond[bond])
                else:
                    sides.append(jnp.zeros((2 * SUB, width), jnp.bfloat16))
        block = jnp.concatenate(sides, axis=0)
        acc[...] += lax.dot_general(
            jnp.concatenate([high, low], axis=1),
            jnp.concatenate([block, block], axis=1),
            (((1,), (1,)), ((), ())),
            preferred_element_type=jnp.float32,
        )

    return advance, contract


def interior_kernel(own_ref, coup_ref, before_ref, after_ref, left_ref, acc, edge_field, edge_rim, ends_ref, field, rim, coup, open_bond):
    rows_x, nright, width = own_ref.shape
    rows = rows_x + 2 * DEPTH
    inner, xtiles = width // LANES, rows_x // SUB
    for x in range(rows_x):
        rim[0, x + DEPTH] = rim_row(before_ref[x // SUB], after_ref[x // SUB], x)

    def blocks_of(g, c, xt):
        return [coup_ref[c, xt * SUB : (xt + 1) * SUB, i * LANES : (i + 1) * LANES] for i in range(inner)]

    def strips_of(g):
        return before_ref[xtiles], after_ref[xtiles]

    coupling_rows(blocks_of, strips_of, range(1, xtiles + 1), xtiles, inner, coup, open_bond, rows)
    acc[...] = jnp.zeros_like(acc)
    advance, contract = stepper(field, rim, coup, open_bond, acc, left_ref, own_ref)

    first, last = DEPTH + 1, DEPTH + rows_x - 2
    lag = 2 * MOMENTS - 1

    def front_step(front):
        if first + MOMENTS - 1 <= front - lag <= last - MOMENTS + 1:
            contract(front - lag)
        for k in reversed(range(MOMENTS)):
            if first + 3 * k <= front <= last + k:
                advance(k, front - 2 * k, front % 2 == 1)

    lead = first + MOMENTS - 1 + lag
    pairs = (last - lead + 1) // 2
    for front in range(first, lead):
        front_step(front)

    def both(n, _):
        for part in range(2):
            front = lead + 2 * n + part
            contract(front - lag)
            for k in reversed(range(MOMENTS)):
                advance(k, front - 2 * k, (lead + part) % 2 == 1)
        return 0

    lax.fori_loop(0, pairs, both, 0)
    for front in range(lead + 2 * pairs, last - MOMENTS + 1 + lag + 1):
        front_step(front)
    for k in range(MOMENTS - 1):
        for side, at in enumerate((first, last - MOMENTS + 1)):
            edge_field[side, k] = field[k + 1, at : at + MOMENTS]
            edge_rim[side, k] = rim[k + 1, at : at + MOMENTS]
    for n, x in enumerate((0, 1, rows_x - 2, rows_x - 1)):
        ends_ref[n] = own_ref[x]


class Either:
    def __init__(self, flag, one, other):
        self.flag, self.one, self.other = flag, one, other

    def __getitem__(self, at):
        return jnp.where(self.flag, self.one[at], self.other[at])


def border_kernel(scale, order_ref, ends_ref, coup_ref, near_ref, next_ref, before_ref, after_ref, left_ref, part_ref, edge_field, edge_rim, out_ref, field, rim, coup, open_bond, acc, spaced, ranked):
    nright, width = ends_ref.shape[1:]
    rows_x = left_ref.shape[0]
    rows = rows_x + 2 * DEPTH
    inner, xtiles = width // LANES, rows_x // SUB
    base = DEPTH * nright + COUPLINGS * SUB
    even = lax.axis_index("sx") % 2 == 0
    lo_ref, hi_ref = Either(even, near_ref, next_ref), Either(even, next_ref, near_ref)

    def corner(ref, which, v):
        return ref[base + which * SUB : base + (which + 1) * SUB, v * LANES : (v + 1) * LANES]

    for e in range(DEPTH):
        rim[0, e] = rim_row(corner(lo_ref, 0, 0), corner(lo_ref, 1, 0), e - DEPTH)
        field[0, e] = lo_ref[e * nright : (e + 1) * nright, :]
        rim[0, e + DEPTH + rows_x] = rim_row(corner(hi_ref, 0, 0), corner(hi_ref, 1, 0), e)
        field[0, e + DEPTH + rows_x] = hi_ref[e * nright : (e + 1) * nright, :]
    for n, x in enumerate((0, 1, rows_x - 2, rows_x - 1)):
        rim[0, x + DEPTH] = rim_row(before_ref[x // SUB], after_ref[x // SUB], x)
        field[0, x + DEPTH] = ends_ref[n]

    def blocks_of(g, c, xt):
        at = DEPTH * nright + c * SUB
        lanes = [slice(i * LANES, (i + 1) * LANES) for i in range(inner)]
        if g == 0:
            return [lo_ref[at : at + SUB, i] for i in lanes]
        if g == xtiles + 1:
            return [hi_ref[at : at + SUB, i] for i in lanes]
        return [coup_ref[c, xt * SUB : (xt + 1) * SUB, i] for i in lanes]

    def strips_of(g):
        if g == 0:
            return corner(lo_ref, 0, 1), corner(lo_ref, 1, 1)
        if g == xtiles + 1:
            return corner(hi_ref, 0, 1), corner(hi_ref, 1, 1)
        return before_ref[xtiles], after_ref[xtiles]

    coupling_rows(blocks_of, strips_of, (0, 1, xtiles, xtiles + 1), xtiles, inner, coup, open_bond, rows)
    first, last = DEPTH + 1, DEPTH + rows_x - 2
    for k in range(MOMENTS - 1):
        for side, at in enumerate((first, last - MOMENTS + 1)):
            field[k + 1, at : at + MOMENTS] = edge_field[side, k]
            rim[k + 1, at : at + MOMENTS] = edge_rim[side, k]
    acc[...] = part_ref[...]
    advance, contract = stepper(field, rim, coup, open_bond, acc, left_ref)

    for front in range(1, DEPTH + 3 * (MOMENTS - 1) + 1):
        for k in reversed(range(MOMENTS)):
            if 3 * k + 1 <= front <= 3 * k + DEPTH:
                row = front - 2 * k
                advance(k, row, row % 2 == 1)
                advance(k, rows - 1 - row, (rows - 1 - row) % 2 == 1)
    for n in range(DEPTH):
        for row in (DEPTH - 1 + n, rows - DEPTH - n):
            contract(row, 0 <= row - 1 - DEPTH < rows_x, 0 <= row + 1 - DEPTH < rows_x)

    near, far, _, flat = out_ref.shape
    flat //= MOMENTS
    groups, owned = near * far, flat // nright
    both_sides = acc[...].T
    half = both_sides.shape[0] // 2
    total = (both_sides[:half] - both_sides[half:]) * scale
    for k in range(MOMENTS):
        spaced[:, 0:nright] = total[:, k * nright : (k + 1) * nright]
        rows_of = [spaced[pl.ds(q, groups, stride=owned), :] for q in range(owned)]
        ranked[k] = jnp.concatenate([r[:, 0:nright] for r in rows_of], axis=1)
    for j in range(MOMENTS):
        for n in range(far):
            out_ref[:, n, 0, j * flat : (j + 1) * flat] = ranked[order_ref[j], n * near : (n + 1) * near]


def vmem_call(kernel, name, out_shape, scratch, flops, *args, scalars=()):
    several = isinstance(out_shape, tuple)
    spec = pl.BlockSpec(memory_space=pltpu.VMEM)
    return pl.pallas_call(
        kernel,
        out_shape=out_shape,
        in_specs=[pl.BlockSpec(memory_space=pltpu.SMEM)] * len(scalars) + [spec] * len(args),
        out_specs=(spec,) * len(out_shape) if several else spec,
        scratch_shapes=scratch,
        compiler_params=pltpu.CompilerParams(vmem_limit_bytes=28 << 20),
        cost_estimate=pl.CostEstimate(flops=flops, bytes_accessed=1 << 22, transcendentals=0),
        name=name,
    )(*scalars, *args)


def scratch_of(rows_x, nright, width):
    rows = rows_x + 2 * DEPTH
    return [
        pltpu.VMEM((MOMENTS + 1, rows, nright, width), jnp.float32),
        pltpu.VMEM((MOMENTS + 1, rows, SUB, LANES), jnp.float32),
        pltpu.VMEM((rows, COUPLINGS, SUB, width + LANES), jnp.float32),
        pltpu.VMEM((rows, 2 * SUB, width), jnp.bfloat16),
    ]


def pairs(axis, start):
    size = lax.axis_size(axis)
    swaps = [(i % size, (i + 1) % size) for i in range(start, size + start, 2)]
    return swaps + [(b, a) for a, b in swaps]


def near_part(size):
    return 8 if size % 8 == 0 else size


def shards(right_vectors, left_vectors, classes, class_energy, bond_mask_grid, order):
    rows_x, rows_y = classes.shape
    nright, nleft = right_vectors.shape[0], left_vectors.shape[0]
    nsx, nsy = lax.axis_size("sx"), lax.axis_size("sy")
    owned = nleft // nsy
    even_x, even_y = lax.axis_index("sx") % 2 == 0, lax.axis_index("sy") % 2 == 0

    own, coup, near_payload, next_payload, beside, across = prepare(
        right_vectors, classes, class_energy, bond_mask_grid
    )
    with jax.named_scope("halo_y"):
        beside = lax.ppermute(beside, "sy", pairs("sy", -1))
        across = lax.ppermute(across, "sy", pairs("sy", 0))
    before, after = jnp.where(even_y, beside, across), jnp.where(even_y, across, beside)
    with jax.named_scope("halo_x"):
        def with_corners(payload, upper):
            corners = [
                jnp.concatenate([jnp.where(upper, part[0], part[-2]), part[-1]], axis=1) for part in (before, after)
            ]
            corners = jnp.concatenate(corners, axis=0)
            return lax.dynamic_update_slice(payload, corners, (payload.shape[0] - corners.shape[0], 0))

        near_payload = with_corners(near_payload, even_x)
        next_payload, _ = lax.optimization_barrier((next_payload, near_payload))
        near_rows = lax.ppermute(near_payload, "sx", pairs("sx", -1))
        next_rows = lax.ppermute(with_corners(next_payload, ~even_x), "sx", pairs("sx", 0))
    left = left_vectors.transpose(1, 0, 2)
    f32 = jnp.float32
    part, edge_field, edge_rim, ends = vmem_call(
        interior_kernel,
        "interior",
        (
            jax.ShapeDtypeStruct((MOMENTS * nright, 2 * nleft), f32),
            jax.ShapeDtypeStruct((2, MOMENTS - 1, MOMENTS, nright, rows_y), f32),
            jax.ShapeDtypeStruct((2, MOMENTS - 1, MOMENTS, SUB, LANES), f32),
            jax.ShapeDtypeStruct((4, nright, rows_y), f32),
        ),
        scratch_of(rows_x, nright, rows_y),
        1 << 33,
        own, coup, before, after, left,
    )
    near = near_part(nsy)
    sites = rows_x * rows_y * nsx * nsy
    tile = vmem_call(
        functools.partial(border_kernel, -HALF_ROOT / sites**0.5),
        "border",
        jax.ShapeDtypeStruct((near, nsy // near, 1, MOMENTS * owned * nright), f32),
        scratch_of(rows_x, nright, rows_y)
        + [
            pltpu.VMEM((MOMENTS * nright, 2 * nleft), f32),
            pltpu.VMEM((nleft, LANES), f32),
            pltpu.VMEM((MOMENTS, nsy, owned * nright), f32),
        ],
        1 << 32,
        ends, coup, near_rows, next_rows, before, after, left, part, edge_field, edge_rim,
        scalars=(order,),
    )
    far_y = nsy // near
    block = tile.shape[2:]
    with jax.named_scope("reduce_near"):
        runs = [[n * near + i for i in range(near)] for n in range(far_y)]
        mine = jnp.sum(lax.all_to_all(tile, "sy", 0, 0, axis_index_groups=runs), axis=0)
    with jax.named_scope("reduce_far"):
        spread = jnp.broadcast_to(mine[:, None], (far_y, nsx) + block).reshape((far_y * nsx,) + block)
        planes = [[m * nsy + n * near + i for n in range(far_y) for m in range(nsx)] for i in range(near)]
        shares = lax.all_to_all(spread, ("sx", "sy"), 0, 0, axis_index_groups=planes)
    total = jnp.sum(shares, axis=0)
    wide = owned * nright
    total = jnp.concatenate([total[:, j * wide : (j + 1) * wide] for j in range(MOMENTS)], axis=0)
    return jnp.stack([total[:, q * nright : (q + 1) * nright] for q in range(owned)], axis=1)


def solution(mesh):
    in_specs = (
        P(None, "sx", "sy"),
        P(None, "sx", "sy"),
        P("sx", "sy"),
        P(),
        P(None, "sx", "sy"),
        P(),
    )
    out_specs = P(None, "sy", None)
    return jax.shard_map(shards, mesh=mesh, in_specs=in_specs, out_specs=out_specs, check_vma=False)
```

```python
import functools

import jax
import jax.numpy as jnp
from jax import lax
from jax.experimental import pallas as pl
from jax.experimental.pallas import tpu as pltpu
from jax.sharding import PartitionSpec as P

MOMENTS = 5
HALF_ROOT = 0.8660254037844386
SPECTRAL = 4.6
TWICE = 2.0 / SPECTRAL
DEPTH = MOMENTS + 1
REACH = 3
SLOT = 4
COUPLINGS = 3
LANES = 128
SUB = 8
SPAN = 32


def lane_iota():
    return lax.broadcasted_iota(jnp.int32, (SUB, LANES), 1)


def turn(value, by):
    by %= LANES
    return pltpu.roll(value, by, 1) if by else value


def swap_major(blocks, sub):
    for s in (4, 2, 1):
        keep = (sub & s) == 0
        for i in range(SUB):
            if i & s == 0:
                a, b = blocks[i], blocks[i + s]
                blocks[i] = jnp.where(keep, a, pltpu.roll(b, s, 0))
                blocks[i + s] = jnp.where(keep, pltpu.roll(a, SUB - s, 0), b)
    return blocks


def prepare_kernel(energy_hbm, right_hbm, class_hbm, bond_hbm, own_hbm, coup_hbm, near_hbm, next_hbm, beside_hbm, across_hbm,
                   energy_ref, right_ref, class_ref, bond_ref, own_ref, coup_ref, rows_ref, strips_ref, in_sem, out_sem):
    nright, rows, width = right_ref.shape
    lane = lane_iota()
    sub = lax.broadcasted_iota(jnp.int32, (SUB, LANES), 0)
    xtiles, rtiles, inner = rows // SUB, nright // SUB, width // LANES
    halves = [pl.ds(h * 2 * SUB, 2 * SUB) for h in range(xtiles // 2)]
    reads = [pltpu.make_async_copy(right_hbm.at[:, h, :], right_ref.at[:, h, :], in_sem.at[n]) for n, h in enumerate(halves)]
    for n, (a, b) in enumerate(((energy_hbm, energy_ref), (class_hbm, class_ref), (bond_hbm, bond_ref))):
        reads.append(pltpu.make_async_copy(a, b, in_sem.at[len(halves) + n]))
    for copy in reads:
        copy.start()
    writes = []

    def write(source, target):
        copy = pltpu.make_async_copy(source, target, out_sem.at[len(writes)])
        copy.start()
        writes.append(copy)

    top_at, first_at = lax.axis_index("sx") % 2, lax.axis_index("sy") % 2
    zero = jnp.zeros((SUB, LANES), jnp.float32)
    first, last = [zero] * (xtiles + 1), [zero] * (xtiles + 1)

    def strip(v, at, i, block):
        here = (lane >= at) & (lane < at + REACH)
        if i == 0:
            first[v] = jnp.where(here, turn(block, at), first[v])
        if i == inner - 1:
            last[v] = jnp.where(here, turn(block, at + REACH), last[v])

    for half in range(xtiles // 2):
        reads[half].wait()
        for i in range(inner):
            lanes = slice(i * LANES, (i + 1) * LANES)
            for t in range(rtiles):
                wide = [
                    right_ref[t * SUB + q, half * 2 * SUB : (half + 1) * 2 * SUB, lanes].astype(jnp.float32)
                    for q in range(SUB)
                ]
                for part in range(2):
                    xt = half * 2 + part
                    turned = swap_major([w[part * SUB : (part + 1) * SUB] for w in wide], sub)
                    for j in range(SUB):
                        x = xt * SUB + j
                        own_ref[x, t * SUB : (t + 1) * SUB, lanes] = turned[j]
                        if x < DEPTH:
                            rows_ref[top_at, x * nright + t * SUB : x * nright + (t + 1) * SUB, lanes] = turned[j]
                        if x >= rows - DEPTH:
                            at = (x - rows + DEPTH) * nright + t * SUB
                            rows_ref[1 - top_at, at : at + SUB, lanes] = turned[j]
                        strip(xt, t * SPAN + j * SLOT, i, turned[j])
        write(own_ref.at[halves[half]], own_hbm.at[halves[half]])
    for copy in reads[len(halves) :]:
        copy.wait()
    for xt in range(xtiles):
        here = slice(xt * SUB, (xt + 1) * SUB)
        for i in range(inner):
            lanes = slice(i * LANES, (i + 1) * LANES)
            kinds = class_ref[here, lanes]
            energy = zero
            for level in range(energy_ref.shape[0]):
                energy = jnp.where(kinds == level, energy_ref[level] * TWICE, energy)
            fields = [bond_ref[c, here, lanes].astype(jnp.float32) * TWICE for c in range(2)] + [energy]
            for c in range(COUPLINGS):
                coup_ref[c, here, lanes] = fields[c]
                strip(xtiles, (c * xtiles + xt) * SLOT, i, fields[c])
                at = DEPTH * nright + c * SUB
                if xt == 0:
                    rows_ref[top_at, at : at + SUB, lanes] = fields[c]
                if xt == xtiles - 1:
                    rows_ref[1 - top_at, at : at + SUB, lanes] = fields[c]
    for v in range(xtiles + 1):
        strips_ref[first_at, v] = first[v]
        strips_ref[1 - first_at, v] = last[v]
    write(strips_ref.at[0], beside_hbm)
    write(strips_ref.at[1], across_hbm)
    filled = pl.ds(0, rows_ref.shape[1])
    write(rows_ref.at[0], near_hbm.at[filled])
    write(rows_ref.at[1], next_hbm.at[filled])
    write(coup_ref, coup_hbm)
    for copy in writes:
        copy.wait()


def prepare(right, classes, energy, bonds):
    nright, rows, width = right.shape
    edge = DEPTH * nright + COUPLINGS * SUB
    f32 = jnp.float32
    own, coup = (rows, nright, width), (COUPLINGS, rows, width)
    strip = (rows // SUB + 1, SUB, LANES)
    halves = rows // (2 * SUB)
    return pl.pallas_call(
        prepare_kernel,
        out_shape=tuple(
            jax.ShapeDtypeStruct(shape, f32)
            for shape in (own, coup, (edge + 2 * SUB, width), (edge + 2 * SUB, width), strip, strip)
        ),
        in_specs=[pl.BlockSpec(memory_space=pltpu.HBM)] * 4,
        out_specs=(pl.BlockSpec(memory_space=pltpu.HBM),) * 6,
        scratch_shapes=[
            pltpu.SMEM(energy.shape, energy.dtype),
            pltpu.VMEM(right.shape, right.dtype),
            pltpu.VMEM(classes.shape, classes.dtype),
            pltpu.VMEM(bonds.shape, bonds.dtype),
            pltpu.VMEM(own, f32),
            pltpu.VMEM(coup, f32),
            pltpu.VMEM((2, edge, width), f32),
            pltpu.VMEM((2,) + strip, f32),
            pltpu.SemaphoreType.DMA((halves + 3,)),
            pltpu.SemaphoreType.DMA((halves + 5,)),
        ],
        name="prepare",
    )(energy, right, classes, bonds)


def swapped(block, lane, odd):
    low = (lane & 1) == (1 if odd else 0)
    target = jnp.where(low, lane + 1, lane + LANES - 1) & (LANES - 1)
    return jnp.take_along_axis(block, target, axis=1)


def coupling_rows(blocks_of, strips_of, groups, xtiles, inner, coup, open_bond, rows):
    lane = lane_iota()
    sub = lax.broadcasted_iota(jnp.int32, (SUB, LANES), 0)
    zero = jnp.zeros((SUB, LANES), jnp.float32)
    for g in groups:
        xt = (g - 1) % xtiles
        before, after = strips_of(g)
        whole = []
        for c in range(COUPLINGS):
            blocks = blocks_of(g, c, xt)
            shift = (c * xtiles + xt) * SLOT
            blocks.append(
                jnp.where(
                    lane < REACH,
                    turn(after, -shift),
                    jnp.where(lane >= LANES - REACH, turn(before, -shift - REACH), zero),
                )
            )
            if c == 1:
                even = [swapped(b, lane, False) for b in blocks]
                odd = [swapped(b, lane, True) for b in blocks]
                n = len(blocks)
                odd = [
                    jnp.where(lane == 0, odd[(i - 1) % n], jnp.where(lane == LANES - 1, odd[(i + 1) % n], odd[i]))
                    for i in range(n)
                ]
                blocks = [
                    jnp.where(((lane + sub) & 1) == 0, b, jnp.where((sub & 1) == 1, o, v))
                    for b, o, v in zip(blocks, odd, even)
                ]
            edge = blocks[inner]
            edge = edge + turn(edge, LANES // 2)
            blocks[inner] = edge + turn(edge, LANES // 4)
            whole.append(blocks)
        for s in range(SUB):
            e = (g - 1) * SUB + s + DEPTH
            if 0 <= e < rows:
                for c in range(COUPLINGS):
                    for i in range(inner + 1):
                        wide = jnp.broadcast_to(whole[c][i][s : s + 1], (SUB, LANES))
                        coup[e, c, :, i * LANES : (i + 1) * LANES] = wide
                        if c == 0 and i < inner:
                            shown = (wide > 0.0).astype(jnp.float32)
                            open_bond[e, :, i * LANES : (i + 1) * LANES] = jnp.concatenate(
                                [shown, shown], axis=0
                            ).astype(jnp.bfloat16)


def rim_row(before, after, x):
    lane = lane_iota()
    shift = (x % SUB) * SLOT
    return jnp.where(
        lane % SPAN < REACH,
        turn(after, -shift),
        jnp.where(lane % SPAN >= SPAN - REACH, turn(before, -shift - REACH), jnp.zeros((SUB, LANES), jnp.float32)),
    )


def stepper(field, rim, coup, open_bond, acc, left_ref, source=None):
    nright, width = field.shape[2:]
    rtiles, inner = nright // SUB, width // LANES
    rows_x = left_ref.shape[0]
    lane = lane_iota()

    def lanes_of(i):
        return slice(i * LANES, (i + 1) * LANES)

    def load(k, row, t, i):
        if i == inner:
            return rim[k, row]
        if k == 0 and source is not None:
            return source[row - DEPTH, t * SUB : (t + 1) * SUB, lanes_of(i)]
        return field[k, row, t * SUB : (t + 1) * SUB, lanes_of(i)]

    def coupling(c, row, i):
        return coup[row, c, :, lanes_of(i)]

    where = [(t, i) for t in range(rtiles) for i in range(inner)] + [(0, inner)]

    def partners(here, odd):
        moved = {at: swapped(value, lane, odd) for at, value in here.items()}
        if not odd:
            return moved
        edge = moved[0, inner]
        start, end = lane == 0, lane == LANES - 1
        result, fill = {}, edge
        for t in range(rtiles):
            outer = turn(edge, -t * SPAN)
            for i in range(inner):
                left = moved[t, i - 1] if i else outer
                right = moved[t, i + 1] if i < inner - 1 else outer
                result[t, i] = jnp.where(start, left, jnp.where(end, right, moved[t, i]))
            facing = turn(jnp.where(lane < LANES // 2, moved[t, inner - 1], moved[t, 0]), t * SPAN)
            fill = jnp.where((lane == t * SPAN) | (lane == (t * SPAN - 1) % LANES), facing, fill)
        result[0, inner] = fill
        return result

    def advance(k, row, odd):
        here = {at: load(k, row, *at) for at in where}
        turned = partners(here, odd)
        east = [coupling(0, row, i) for i in range(inner + 1)]
        west = [coupling(0, row - 1, i) for i in range(inner + 1)]
        vertical = [coupling(1, row, i) for i in range(inner + 1)]
        site = [coupling(2, row, i) for i in range(inner + 1)] if k else None
        sign = jnp.where((lane & 1) == (1 if odd else 0), 1.0 / TWICE, -1.0 / TWICE)
        new = {}
        for t, i in where:
            beside = east[i] * load(k, row + 1, t, i) + west[i] * load(k, row - 1, t, i)
            across = vertical[i] * turned[t, i]
            if k == 0:
                new[t, i] = sign * (0.5 * beside - across)
            else:
                image = site[i] * here[t, i] - beside - across
                new[t, i] = 0.5 * image if k == 1 else image - load(k - 1, row, t, i)
        for t, i in where:
            if i == inner:
                rim[k + 1, row] = new[t, i]
            else:
                field[k + 1, row, t * SUB : (t + 1) * SUB, lanes_of(i)] = new[t, i]

    def contract(row, below=True, above=True):
        parts = []
        for t in range(rtiles * MOMENTS):
            k, q = divmod(t, rtiles)
            parts.append(field[k + 1, row, q * SUB : (q + 1) * SUB, :])
        value = jnp.concatenate(parts, axis=0)
        high = value.astype(jnp.bfloat16)
        low = (value - high.astype(jnp.float32)).astype(jnp.bfloat16)
        sides = []
        for there, bond, wanted in ((row - 1, row - 1, below), (row + 1, row, above)):
            for q in range(left_ref.shape[1] // (2 * SUB)):
                if wanted:
                    sides.append(left_ref[there - DEPTH, q * 2 * SUB : (q + 1) * 2 * SUB, :] * open_bond[bond])
                else:
                    sides.append(jnp.zeros((2 * SUB, width), jnp.bfloat16))
        block = jnp.concatenate(sides, axis=0)
        acc[...] += lax.dot_general(
            jnp.concatenate([high, low], axis=1),
            jnp.concatenate([block, block], axis=1),
            (((1,), (1,)), ((), ())),
            preferred_element_type=jnp.float32,
        )

    return advance, contract


def interior_kernel(own_ref, coup_ref, before_ref, after_ref, left_ref, acc, edge_field, edge_rim, ends_ref, field, rim, coup, open_bond):
    rows_x, nright, width = own_ref.shape
    rows = rows_x + 2 * DEPTH
    inner, xtiles = width // LANES, rows_x // SUB
    for x in range(rows_x):
        rim[0, x + DEPTH] = rim_row(before_ref[x // SUB], after_ref[x // SUB], x)

    def blocks_of(g, c, xt):
        return [coup_ref[c, xt * SUB : (xt + 1) * SUB, i * LANES : (i + 1) * LANES] for i in range(inner)]

    def strips_of(g):
        return before_ref[xtiles], after_ref[xtiles]

    coupling_rows(blocks_of, strips_of, range(1, xtiles + 1), xtiles, inner, coup, open_bond, rows)
    acc[...] = jnp.zeros_like(acc)
    advance, contract = stepper(field, rim, coup, open_bond, acc, left_ref, own_ref)

    first, last = DEPTH + 1, DEPTH + rows_x - 2
    lag = 2 * MOMENTS - 1

    def front_step(front):
        if first + MOMENTS - 1 <= front - lag <= last - MOMENTS + 1:
            contract(front - lag)
        for k in reversed(range(MOMENTS)):
            if first + 3 * k <= front <= last + k:
                advance(k, front - 2 * k, front % 2 == 1)

    for front in range(first, last - MOMENTS + 1 + lag + 1):
        front_step(front)
    for k in range(MOMENTS - 1):
        for side, at in enumerate((first, last - MOMENTS + 1)):
            edge_field[side, k] = field[k + 1, at : at + MOMENTS]
            edge_rim[side, k] = rim[k + 1, at : at + MOMENTS]
    for n, x in enumerate((0, 1, rows_x - 2, rows_x - 1)):
        ends_ref[n] = own_ref[x]


class Either:
    def __init__(self, flag, one, other):
        self.flag, self.one, self.other = flag, one, other

    def __getitem__(self, at):
        return jnp.where(self.flag, self.one[at], self.other[at])


def border_kernel(scale, order_ref, ends_ref, coup_ref, near_ref, next_ref, before_ref, after_ref, left_ref, part_ref, edge_field, edge_rim, out_ref, field, rim, coup, open_bond, acc, spaced, ranked):
    nright, width = ends_ref.shape[1:]
    rows_x = left_ref.shape[0]
    rows = rows_x + 2 * DEPTH
    inner, xtiles = width // LANES, rows_x // SUB
    base = DEPTH * nright + COUPLINGS * SUB
    even = lax.axis_index("sx") % 2 == 0
    lo_ref, hi_ref = Either(even, near_ref, next_ref), Either(even, next_ref, near_ref)

    def corner(ref, which, v):
        return ref[base + which * SUB : base + (which + 1) * SUB, v * LANES : (v + 1) * LANES]

    for e in range(DEPTH):
        rim[0, e] = rim_row(corner(lo_ref, 0, 0), corner(lo_ref, 1, 0), e - DEPTH)
        field[0, e] = lo_ref[e * nright : (e + 1) * nright, :]
        rim[0, e + DEPTH + rows_x] = rim_row(corner(hi_ref, 0, 0), corner(hi_ref, 1, 0), e)
        field[0, e + DEPTH + rows_x] = hi_ref[e * nright : (e + 1) * nright, :]
    for n, x in enumerate((0, 1, rows_x - 2, rows_x - 1)):
        rim[0, x + DEPTH] = rim_row(before_ref[x // SUB], after_ref[x // SUB], x)
        field[0, x + DEPTH] = ends_ref[n]

    def blocks_of(g, c, xt):
        at = DEPTH * nright + c * SUB
        lanes = [slice(i * LANES, (i + 1) * LANES) for i in range(inner)]
        if g == 0:
            return [lo_ref[at : at + SUB, i] for i in lanes]
        if g == xtiles + 1:
            return [hi_ref[at : at + SUB, i] for i in lanes]
        return [coup_ref[c, xt * SUB : (xt + 1) * SUB, i] for i in lanes]

    def strips_of(g):
        if g == 0:
            return corner(lo_ref, 0, 1), corner(lo_ref, 1, 1)
        if g == xtiles + 1:
            return corner(hi_ref, 0, 1), corner(hi_ref, 1, 1)
        return before_ref[xtiles], after_ref[xtiles]

    coupling_rows(blocks_of, strips_of, (0, 1, xtiles, xtiles + 1), xtiles, inner, coup, open_bond, rows)
    first, last = DEPTH + 1, DEPTH + rows_x - 2
    for k in range(MOMENTS - 1):
        for side, at in enumerate((first, last - MOMENTS + 1)):
            field[k + 1, at : at + MOMENTS] = edge_field[side, k]
            rim[k + 1, at : at + MOMENTS] = edge_rim[side, k]
    acc[...] = part_ref[...]
    advance, contract = stepper(field, rim, coup, open_bond, acc, left_ref)

    for front in range(1, DEPTH + 3 * (MOMENTS - 1) + 1):
        for k in reversed(range(MOMENTS)):
            if 3 * k + 1 <= front <= 3 * k + DEPTH:
                row = front - 2 * k
                advance(k, row, row % 2 == 1)
                advance(k, rows - 1 - row, (rows - 1 - row) % 2 == 1)
    for n in range(DEPTH):
        for row in (DEPTH - 1 + n, rows - DEPTH - n):
            contract(row, 0 <= row - 1 - DEPTH < rows_x, 0 <= row + 1 - DEPTH < rows_x)

    near, far, _, flat = out_ref.shape
    flat //= MOMENTS
    groups, owned = near * far, flat // nright
    both_sides = acc[...].T
    half = both_sides.shape[0] // 2
    total = (both_sides[:half] - both_sides[half:]) * scale
    for k in range(MOMENTS):
        spaced[:, 0:nright] = total[:, k * nright : (k + 1) * nright]
        rows_of = [spaced[pl.ds(q, groups, stride=owned), :] for q in range(owned)]
        ranked[k] = jnp.concatenate([r[:, 0:nright] for r in rows_of], axis=1)
    for j in range(MOMENTS):
        for n in range(far):
            out_ref[:, n, 0, j * flat : (j + 1) * flat] = ranked[order_ref[j], n * near : (n + 1) * near]


def vmem_call(kernel, name, out_shape, scratch, flops, *args, scalars=()):
    several = isinstance(out_shape, tuple)
    spec = pl.BlockSpec(memory_space=pltpu.VMEM)
    return pl.pallas_call(
        kernel,
        out_shape=out_shape,
        in_specs=[pl.BlockSpec(memory_space=pltpu.SMEM)] * len(scalars) + [spec] * len(args),
        out_specs=(spec,) * len(out_shape) if several else spec,
        scratch_shapes=scratch,
        compiler_params=pltpu.CompilerParams(vmem_limit_bytes=28 << 20),
        cost_estimate=pl.CostEstimate(flops=flops, bytes_accessed=1 << 22, transcendentals=0),
        name=name,
    )(*scalars, *args)


def scratch_of(rows_x, nright, width):
    rows = rows_x + 2 * DEPTH
    return [
        pltpu.VMEM((MOMENTS + 1, rows, nright, width), jnp.float32),
        pltpu.VMEM((MOMENTS + 1, rows, SUB, LANES), jnp.float32),
        pltpu.VMEM((rows, COUPLINGS, SUB, width + LANES), jnp.float32),
        pltpu.VMEM((rows, 2 * SUB, width), jnp.bfloat16),
    ]


def pairs(axis, start):
    size = lax.axis_size(axis)
    swaps = [(i % size, (i + 1) % size) for i in range(start, size + start, 2)]
    return swaps + [(b, a) for a, b in swaps]


def near_part(size):
    return 8 if size % 8 == 0 else size


def shards(right_vectors, left_vectors, classes, class_energy, bond_mask_grid, order):
    rows_x, rows_y = classes.shape
    nright, nleft = right_vectors.shape[0], left_vectors.shape[0]
    nsx, nsy = lax.axis_size("sx"), lax.axis_size("sy")
    owned = nleft // nsy
    even_x, even_y = lax.axis_index("sx") % 2 == 0, lax.axis_index("sy") % 2 == 0

    own, coup, near_payload, next_payload, beside, across = prepare(
        right_vectors, classes, class_energy, bond_mask_grid
    )
    with jax.named_scope("halo_y"):
        beside = lax.ppermute(beside, "sy", pairs("sy", -1))
        across = lax.ppermute(across, "sy", pairs("sy", 0))
    before, after = jnp.where(even_y, beside, across), jnp.where(even_y, across, beside)
    with jax.named_scope("halo_x"):
        def with_corners(payload, upper):
            corners = [
                jnp.concatenate([jnp.where(upper, part[0], part[-2]), part[-1]], axis=1) for part in (before, after)
            ]
            corners = jnp.concatenate(corners, axis=0)
            return lax.dynamic_update_slice(payload, corners, (payload.shape[0] - corners.shape[0], 0))

        near_payload = with_corners(near_payload, even_x)
        next_payload, _ = lax.optimization_barrier((next_payload, near_payload))
        near_rows = lax.ppermute(near_payload, "sx", pairs("sx", -1))
        next_rows = lax.ppermute(with_corners(next_payload, ~even_x), "sx", pairs("sx", 0))
    left = left_vectors.transpose(1, 0, 2)
    f32 = jnp.float32
    part, edge_field, edge_rim, ends = vmem_call(
        interior_kernel,
        "interior",
        (
            jax.ShapeDtypeStruct((MOMENTS * nright, 2 * nleft), f32),
            jax.ShapeDtypeStruct((2, MOMENTS - 1, MOMENTS, nright, rows_y), f32),
            jax.ShapeDtypeStruct((2, MOMENTS - 1, MOMENTS, SUB, LANES), f32),
            jax.ShapeDtypeStruct((4, nright, rows_y), f32),
        ),
        scratch_of(rows_x, nright, rows_y),
        1 << 33,
        own, coup, before, after, left,
    )
    near = near_part(nsy)
    sites = rows_x * rows_y * nsx * nsy
    tile = vmem_call(
        functools.partial(border_kernel, -HALF_ROOT / sites**0.5),
        "border",
        jax.ShapeDtypeStruct((near, nsy // near, 1, MOMENTS * owned * nright), f32),
        scratch_of(rows_x, nright, rows_y)
        + [
            pltpu.VMEM((MOMENTS * nright, 2 * nleft), f32),
            pltpu.VMEM((nleft, LANES), f32),
            pltpu.VMEM((MOMENTS, nsy, owned * nright), f32),
        ],
        1 << 32,
        ends, coup, near_rows, next_rows, before, after, left, part, edge_field, edge_rim,
        scalars=(order,),
    )
    far_y = nsy // near
    block = tile.shape[2:]
    with jax.named_scope("reduce_near"):
        runs = [[n * near + i for i in range(near)] for n in range(far_y)]
        mine = jnp.sum(lax.all_to_all(tile, "sy", 0, 0, axis_index_groups=runs), axis=0)
    with jax.named_scope("reduce_far"):
        spread = jnp.broadcast_to(mine[:, None], (far_y, nsx) + block).reshape((far_y * nsx,) + block)
        planes = [[m * nsy + n * near + i for n in range(far_y) for m in range(nsx)] for i in range(near)]
        shares = lax.all_to_all(spread, ("sx", "sy"), 0, 0, axis_index_groups=planes)
    total = jnp.sum(shares, axis=0)
    wide = owned * nright
    total = jnp.concatenate([total[:, j * wide : (j + 1) * wide] for j in range(MOMENTS)], axis=0)
    return jnp.stack([total[:, q * nright : (q + 1) * nright] for q in range(owned)], axis=1)


def solution(mesh):
    in_specs = (
        P(None, "sx", "sy"),
        P(None, "sx", "sy"),
        P("sx", "sy"),
        P(),
        P(None, "sx", "sy"),
        P(),
    )
    out_specs = P(None, "sy", None)
    return jax.shard_map(shards, mesh=mesh, in_specs=in_specs, out_specs=out_specs, check_vma=False)
```

```python
import functools

import jax
import jax.numpy as jnp
from jax import lax
from jax.experimental import pallas as pl
from jax.experimental.pallas import tpu as pltpu
from jax.sharding import PartitionSpec as P

MOMENTS = 5
HALF_ROOT = 0.8660254037844386
SPECTRAL = 4.6
TWICE = 2.0 / SPECTRAL
DEPTH = MOMENTS + 1
REACH = 3
SLOT = 4
COUPLINGS = 3
LANES = 128
SUB = 8
SPAN = 32


def lane_iota():
    return lax.broadcasted_iota(jnp.int32, (SUB, LANES), 1)


def turn(value, by):
    by %= LANES
    return pltpu.roll(value, by, 1) if by else value


def swap_major(blocks, sub):
    for s in (4, 2, 1):
        keep = (sub & s) == 0
        for i in range(SUB):
            if i & s == 0:
                a, b = blocks[i], blocks[i + s]
                blocks[i] = jnp.where(keep, a, pltpu.roll(b, s, 0))
                blocks[i + s] = jnp.where(keep, pltpu.roll(a, SUB - s, 0), b)
    return blocks


def prepare_kernel(energy_hbm, right_hbm, class_hbm, bond_hbm, own_hbm, coup_hbm, near_hbm, next_hbm, beside_hbm, across_hbm,
                   energy_ref, right_ref, class_ref, bond_ref, own_ref, coup_ref, rows_ref, strips_ref, in_sem, out_sem):
    nright, rows, width = right_ref.shape
    lane = lane_iota()
    sub = lax.broadcasted_iota(jnp.int32, (SUB, LANES), 0)
    xtiles, rtiles, inner = rows // SUB, nright // SUB, width // LANES
    halves = [pl.ds(h * 2 * SUB, 2 * SUB) for h in range(xtiles // 2)]
    reads = [pltpu.make_async_copy(right_hbm.at[:, h, :], right_ref.at[:, h, :], in_sem.at[n]) for n, h in enumerate(halves)]
    for n, (a, b) in enumerate(((energy_hbm, energy_ref), (class_hbm, class_ref), (bond_hbm, bond_ref))):
        reads.append(pltpu.make_async_copy(a, b, in_sem.at[len(halves) + n]))
    for copy in reads:
        copy.start()
    writes = []

    def write(source, target):
        copy = pltpu.make_async_copy(source, target, out_sem.at[len(writes)])
        copy.start()
        writes.append(copy)

    top_at, first_at = lax.axis_index("sx") % 2, lax.axis_index("sy") % 2
    zero = jnp.zeros((SUB, LANES), jnp.float32)
    first, last = [zero] * (xtiles + 1), [zero] * (xtiles + 1)

    def strip(v, at, i, block):
        here = (lane >= at) & (lane < at + REACH)
        if i == 0:
            first[v] = jnp.where(here, turn(block, at), first[v])
        if i == inner - 1:
            last[v] = jnp.where(here, turn(block, at + REACH), last[v])

    for half in range(xtiles // 2):
        reads[half].wait()
        for i in range(inner):
            lanes = slice(i * LANES, (i + 1) * LANES)
            for t in range(rtiles):
                wide = [
                    right_ref[t * SUB + q, half * 2 * SUB : (half + 1) * 2 * SUB, lanes].astype(jnp.float32)
                    for q in range(SUB)
                ]
                for part in range(2):
                    xt = half * 2 + part
                    turned = swap_major([w[part * SUB : (part + 1) * SUB] for w in wide], sub)
                    for j in range(SUB):
                        x = xt * SUB + j
                        own_ref[x, t * SUB : (t + 1) * SUB, lanes] = turned[j]
                        if x < DEPTH:
                            rows_ref[top_at, x * nright + t * SUB : x * nright + (t + 1) * SUB, lanes] = turned[j]
                        if x >= rows - DEPTH:
                            at = (x - rows + DEPTH) * nright + t * SUB
                            rows_ref[1 - top_at, at : at + SUB, lanes] = turned[j]
                        strip(xt, t * SPAN + j * SLOT, i, turned[j])
        write(own_ref.at[halves[half]], own_hbm.at[halves[half]])
    for copy in reads[len(halves) :]:
        copy.wait()
    for xt in range(xtiles):
        here = slice(xt * SUB, (xt + 1) * SUB)
        for i in range(inner):
            lanes = slice(i * LANES, (i + 1) * LANES)
            kinds = class_ref[here, lanes]
            energy = zero
            for level in range(energy_ref.shape[0]):
                energy = jnp.where(kinds == level, energy_ref[level] * TWICE, energy)
            fields = [bond_ref[c, here, lanes].astype(jnp.float32) * TWICE for c in range(2)] + [energy]
            for c in range(COUPLINGS):
                coup_ref[c, here, lanes] = fields[c]
                strip(xtiles, (c * xtiles + xt) * SLOT, i, fields[c])
                at = DEPTH * nright + c * SUB
                if xt == 0:
                    rows_ref[top_at, at : at + SUB, lanes] = fields[c]
                if xt == xtiles - 1:
                    rows_ref[1 - top_at, at : at + SUB, lanes] = fields[c]
    for v in range(xtiles + 1):
        strips_ref[first_at, v] = first[v]
        strips_ref[1 - first_at, v] = last[v]
    write(strips_ref.at[0], beside_hbm)
    write(strips_ref.at[1], across_hbm)
    filled = pl.ds(0, rows_ref.shape[1])
    write(rows_ref.at[0], near_hbm.at[filled])
    write(rows_ref.at[1], next_hbm.at[filled])
    write(coup_ref, coup_hbm)
    for copy in writes:
        copy.wait()


def prepare(right, classes, energy, bonds):
    nright, rows, width = right.shape
    edge = DEPTH * nright + COUPLINGS * SUB
    f32 = jnp.float32
    own, coup = (rows, nright, width), (COUPLINGS, rows, width)
    strip = (rows // SUB + 1, SUB, LANES)
    halves = rows // (2 * SUB)
    return pl.pallas_call(
        prepare_kernel,
        out_shape=tuple(
            jax.ShapeDtypeStruct(shape, f32)
            for shape in (own, coup, (edge + 2 * SUB, width), (edge + 2 * SUB, width), strip, strip)
        ),
        in_specs=[pl.BlockSpec(memory_space=pltpu.HBM)] * 4,
        out_specs=(pl.BlockSpec(memory_space=pltpu.HBM),) * 6,
        scratch_shapes=[
            pltpu.SMEM(energy.shape, energy.dtype),
            pltpu.VMEM(right.shape, right.dtype),
            pltpu.VMEM(classes.shape, classes.dtype),
            pltpu.VMEM(bonds.shape, bonds.dtype),
            pltpu.VMEM(own, f32),
            pltpu.VMEM(coup, f32),
            pltpu.VMEM((2, edge, width), f32),
            pltpu.VMEM((2,) + strip, f32),
            pltpu.SemaphoreType.DMA((halves + 3,)),
            pltpu.SemaphoreType.DMA((halves + 5,)),
        ],
        name="prepare",
    )(energy, right, classes, bonds)


def swapped(block, lane, odd):
    low = (lane & 1) == (1 if odd else 0)
    target = jnp.where(low, lane + 1, lane + LANES - 1) & (LANES - 1)
    return jnp.take_along_axis(block, target, axis=1)


def coupling_rows(blocks_of, strips_of, groups, xtiles, inner, coup, open_bond, rows):
    lane = lane_iota()
    sub = lax.broadcasted_iota(jnp.int32, (SUB, LANES), 0)
    zero = jnp.zeros((SUB, LANES), jnp.float32)
    for g in groups:
        xt = (g - 1) % xtiles
        before, after = strips_of(g)
        whole = []
        for c in range(COUPLINGS):
            blocks = blocks_of(g, c, xt)
            shift = (c * xtiles + xt) * SLOT
            blocks.append(
                jnp.where(
                    lane < REACH,
                    turn(after, -shift),
                    jnp.where(lane >= LANES - REACH, turn(before, -shift - REACH), zero),
                )
            )
            if c == 1:
                even = [swapped(b, lane, False) for b in blocks]
                odd = [swapped(b, lane, True) for b in blocks]
                n = len(blocks)
                odd = [
                    jnp.where(lane == 0, odd[(i - 1) % n], jnp.where(lane == LANES - 1, odd[(i + 1) % n], odd[i]))
                    for i in range(n)
                ]
                blocks = [
                    jnp.where(((lane + sub) & 1) == 0, b, jnp.where((sub & 1) == 1, o, v))
                    for b, o, v in zip(blocks, odd, even)
                ]
            edge = blocks[inner]
            edge = edge + turn(edge, LANES // 2)
            blocks[inner] = edge + turn(edge, LANES // 4)
            whole.append(blocks)
        for s in range(SUB):
            e = (g - 1) * SUB + s + DEPTH
            if 0 <= e < rows:
                for c in range(COUPLINGS):
                    for i in range(inner + 1):
                        wide = jnp.broadcast_to(whole[c][i][s : s + 1], (SUB, LANES))
                        coup[e, c, :, i * LANES : (i + 1) * LANES] = wide
                        if c == 0 and i < inner:
                            shown = (wide > 0.0).astype(jnp.float32)
                            open_bond[e, :, i * LANES : (i + 1) * LANES] = jnp.concatenate(
                                [shown, shown], axis=0
                            ).astype(jnp.bfloat16)


def rim_row(before, after, x):
    lane = lane_iota()
    shift = (x % SUB) * SLOT
    return jnp.where(
        lane % SPAN < REACH,
        turn(after, -shift),
        jnp.where(lane % SPAN >= SPAN - REACH, turn(before, -shift - REACH), jnp.zeros((SUB, LANES), jnp.float32)),
    )


def stepper(field, rim, coup, open_bond, acc, left_ref, source=None):
    nright, width = field.shape[2:]
    rtiles, inner = nright // SUB, width // LANES
    rows_x = left_ref.shape[0]
    lane = lane_iota()

    def lanes_of(i):
        return slice(i * LANES, (i + 1) * LANES)

    def load(k, row, t, i):
        if i == inner:
            return rim[k, row]
        if k == 0 and source is not None:
            return source[row - DEPTH, t * SUB : (t + 1) * SUB, lanes_of(i)]
        return field[k, row, t * SUB : (t + 1) * SUB, lanes_of(i)]

    def coupling(c, row, i):
        return coup[row, c, :, lanes_of(i)]

    where = [(t, i) for t in range(rtiles) for i in range(inner)] + [(0, inner)]

    def partners(here, odd):
        moved = {at: swapped(value, lane, odd) for at, value in here.items()}
        if not odd:
            return moved
        edge = moved[0, inner]
        start, end = lane == 0, lane == LANES - 1
        result, fill = {}, edge
        for t in range(rtiles):
            outer = turn(edge, -t * SPAN)
            for i in range(inner):
                left = moved[t, i - 1] if i else outer
                right = moved[t, i + 1] if i < inner - 1 else outer
                result[t, i] = jnp.where(start, left, jnp.where(end, right, moved[t, i]))
            facing = turn(jnp.where(lane < LANES // 2, moved[t, inner - 1], moved[t, 0]), t * SPAN)
            fill = jnp.where((lane == t * SPAN) | (lane == (t * SPAN - 1) % LANES), facing, fill)
        result[0, inner] = fill
        return result

    def advance(k, row, odd):
        here = {at: load(k, row, *at) for at in where}
        turned = partners(here, odd)
        east = [coupling(0, row, i) for i in range(inner + 1)]
        west = [coupling(0, row - 1, i) for i in range(inner + 1)]
        vertical = [coupling(1, row, i) for i in range(inner + 1)]
        site = [coupling(2, row, i) for i in range(inner + 1)] if k else None
        sign = jnp.where((lane & 1) == (1 if odd else 0), 1.0 / TWICE, -1.0 / TWICE)
        new = {}
        for t, i in where:
            beside = east[i] * load(k, row + 1, t, i) + west[i] * load(k, row - 1, t, i)
            across = vertical[i] * turned[t, i]
            if k == 0:
                new[t, i] = sign * (0.5 * beside - across)
            else:
                image = site[i] * here[t, i] - beside - across
                new[t, i] = 0.5 * image if k == 1 else image - load(k - 1, row, t, i)
        for t, i in where:
            if i == inner:
                rim[k + 1, row] = new[t, i]
            else:
                field[k + 1, row, t * SUB : (t + 1) * SUB, lanes_of(i)] = new[t, i]

    def contract(row, below=True, above=True):
        parts = []
        for t in range(rtiles * MOMENTS):
            k, q = divmod(t, rtiles)
            parts.append(field[k + 1, row, q * SUB : (q + 1) * SUB, :])
        value = jnp.concatenate(parts, axis=0)
        high = value.astype(jnp.bfloat16)
        low = (value - high.astype(jnp.float32)).astype(jnp.bfloat16)
        sides = []
        for there, bond, wanted in ((row - 1, row - 1, below), (row + 1, row, above)):
            for q in range(left_ref.shape[1] // (2 * SUB)):
                if wanted:
                    sides.append(left_ref[there - DEPTH, q * 2 * SUB : (q + 1) * 2 * SUB, :] * open_bond[bond])
                else:
                    sides.append(jnp.zeros((2 * SUB, width), jnp.bfloat16))
        block = jnp.concatenate(sides, axis=0)
        acc[...] += lax.dot_general(
            jnp.concatenate([high, low], axis=1),
            jnp.concatenate([block, block], axis=1),
            (((1,), (1,)), ((), ())),
            preferred_element_type=jnp.float32,
        )

    return advance, contract


def interior_kernel(own_ref, coup_ref, before_ref, after_ref, left_ref, acc, edge_field, edge_rim, ends_ref, field, rim, coup, open_bond):
    rows_x, nright, width = own_ref.shape
    rows = rows_x + 2 * DEPTH
    inner, xtiles = width // LANES, rows_x // SUB
    for x in range(rows_x):
        rim[0, x + DEPTH] = rim_row(before_ref[x // SUB], after_ref[x // SUB], x)

    def blocks_of(g, c, xt):
        return [coup_ref[c, xt * SUB : (xt + 1) * SUB, i * LANES : (i + 1) * LANES] for i in range(inner)]

    def strips_of(g):
        return before_ref[xtiles], after_ref[xtiles]

    coupling_rows(blocks_of, strips_of, range(1, xtiles + 1), xtiles, inner, coup, open_bond, rows)
    acc[...] = jnp.zeros_like(acc)
    advance, contract = stepper(field, rim, coup, open_bond, acc, left_ref, own_ref)

    first, last = DEPTH + 1, DEPTH + rows_x - 2
    lag = 2 * MOMENTS - 1

    def front_step(front):
        if first + MOMENTS - 1 <= front - lag <= last - MOMENTS + 1:
            contract(front - lag)
        for k in reversed(range(MOMENTS)):
            if first + 3 * k <= front <= last + k:
                advance(k, front - 2 * k, front % 2 == 1)

    for front in range(first, last - MOMENTS + 1 + lag + 1):
        front_step(front)
    for k in range(MOMENTS - 1):
        for side, at in enumerate((first, last - MOMENTS + 1)):
            edge_field[side, k] = field[k + 1, at : at + MOMENTS]
            edge_rim[side, k] = rim[k + 1, at : at + MOMENTS]
    for n, x in enumerate((0, 1, rows_x - 2, rows_x - 1)):
        ends_ref[n] = own_ref[x]


class Either:
    def __init__(self, flag, one, other):
        self.flag, self.one, self.other = flag, one, other

    def __getitem__(self, at):
        return jnp.where(self.flag, self.one[at], self.other[at])


def border_kernel(scale, order_ref, ends_ref, coup_ref, near_ref, next_ref, before_ref, after_ref, left_ref, part_ref, edge_field, edge_rim, out_ref, field, rim, coup, open_bond, acc, spaced, ranked):
    nright, width = ends_ref.shape[1:]
    rows_x = left_ref.shape[0]
    rows = rows_x + 2 * DEPTH
    inner, xtiles = width // LANES, rows_x // SUB
    base = DEPTH * nright + COUPLINGS * SUB
    even = lax.axis_index("sx") % 2 == 0
    lo_ref, hi_ref = Either(even, near_ref, next_ref), Either(even, next_ref, near_ref)

    def corner(ref, which, v):
        return ref[base + which * SUB : base + (which + 1) * SUB, v * LANES : (v + 1) * LANES]

    for e in range(DEPTH):
        rim[0, e] = rim_row(corner(lo_ref, 0, 0), corner(lo_ref, 1, 0), e - DEPTH)
        field[0, e] = lo_ref[e * nright : (e + 1) * nright, :]
        rim[0, e + DEPTH + rows_x] = rim_row(corner(hi_ref, 0, 0), corner(hi_ref, 1, 0), e)
        field[0, e + DEPTH + rows_x] = hi_ref[e * nright : (e + 1) * nright, :]
    for n, x in enumerate((0, 1, rows_x - 2, rows_x - 1)):
        rim[0, x + DEPTH] = rim_row(before_ref[x // SUB], after_ref[x // SUB], x)
        field[0, x + DEPTH] = ends_ref[n]

    def blocks_of(g, c, xt):
        at = DEPTH * nright + c * SUB
        lanes = [slice(i * LANES, (i + 1) * LANES) for i in range(inner)]
        if g == 0:
            return [lo_ref[at : at + SUB, i] for i in lanes]
        if g == xtiles + 1:
            return [hi_ref[at : at + SUB, i] for i in lanes]
        return [coup_ref[c, xt * SUB : (xt + 1) * SUB, i] for i in lanes]

    def strips_of(g):
        if g == 0:
            return corner(lo_ref, 0, 1), corner(lo_ref, 1, 1)
        if g == xtiles + 1:
            return corner(hi_ref, 0, 1), corner(hi_ref, 1, 1)
        return before_ref[xtiles], after_ref[xtiles]

    coupling_rows(blocks_of, strips_of, (0, 1, xtiles, xtiles + 1), xtiles, inner, coup, open_bond, rows)
    first, last = DEPTH + 1, DEPTH + rows_x - 2
    for k in range(MOMENTS - 1):
        for side, at in enumerate((first, last - MOMENTS + 1)):
            field[k + 1, at : at + MOMENTS] = edge_field[side, k]
            rim[k + 1, at : at + MOMENTS] = edge_rim[side, k]
    acc[...] = part_ref[...]
    advance, contract = stepper(field, rim, coup, open_bond, acc, left_ref)

    for front in range(1, DEPTH + 3 * (MOMENTS - 1) + 1):
        for k in reversed(range(MOMENTS)):
            if 3 * k + 1 <= front <= 3 * k + DEPTH:
                row = front - 2 * k
                advance(k, row, row % 2 == 1)
                advance(k, rows - 1 - row, (rows - 1 - row) % 2 == 1)
    for n in range(DEPTH):
        for row in (DEPTH - 1 + n, rows - DEPTH - n):
            contract(row, 0 <= row - 1 - DEPTH < rows_x, 0 <= row + 1 - DEPTH < rows_x)

    near, far, _, flat = out_ref.shape
    flat //= MOMENTS
    groups, owned = near * far, flat // nright
    both_sides = acc[...].T
    half = both_sides.shape[0] // 2
    total = (both_sides[:half] - both_sides[half:]) * scale
    for k in range(MOMENTS):
        spaced[:, 0:nright] = total[:, k * nright : (k + 1) * nright]
        rows_of = [spaced[pl.ds(q, groups, stride=owned), :] for q in range(owned)]
        ranked[k] = jnp.concatenate([r[:, 0:nright] for r in rows_of], axis=1)
    for j in range(MOMENTS):
        for n in range(far):
            out_ref[:, n, 0, j * flat : (j + 1) * flat] = ranked[order_ref[j], n * near : (n + 1) * near]


def vmem_call(kernel, name, out_shape, scratch, flops, *args, scalars=()):
    several = isinstance(out_shape, tuple)
    spec = pl.BlockSpec(memory_space=pltpu.VMEM)
    return pl.pallas_call(
        kernel,
        out_shape=out_shape,
        in_specs=[pl.BlockSpec(memory_space=pltpu.SMEM)] * len(scalars) + [spec] * len(args),
        out_specs=(spec,) * len(out_shape) if several else spec,
        scratch_shapes=scratch,
        compiler_params=pltpu.CompilerParams(vmem_limit_bytes=28 << 20),
        cost_estimate=pl.CostEstimate(flops=flops, bytes_accessed=1 << 22, transcendentals=0),
        name=name,
    )(*scalars, *args)


def scratch_of(rows_x, nright, width):
    rows = rows_x + 2 * DEPTH
    return [
        pltpu.VMEM((MOMENTS + 1, rows, nright, width), jnp.float32),
        pltpu.VMEM((MOMENTS + 1, rows, SUB, LANES), jnp.float32),
        pltpu.VMEM((rows, COUPLINGS, SUB, width + LANES), jnp.float32),
        pltpu.VMEM((rows, 2 * SUB, width), jnp.bfloat16),
    ]


def pairs(axis, start):
    size = lax.axis_size(axis)
    swaps = [(i % size, (i + 1) % size) for i in range(start, size + start, 2)]
    return swaps + [(b, a) for a, b in swaps]


def near_part(size):
    return 8 if size % 8 == 0 else size


def shards(right_vectors, left_vectors, classes, class_energy, bond_mask_grid, order):
    rows_x, rows_y = classes.shape
    nright, nleft = right_vectors.shape[0], left_vectors.shape[0]
    nsx, nsy = lax.axis_size("sx"), lax.axis_size("sy")
    owned = nleft // nsy
    even_x, even_y = lax.axis_index("sx") % 2 == 0, lax.axis_index("sy") % 2 == 0

    own, coup, near_payload, next_payload, beside, across = prepare(
        right_vectors, classes, class_energy, bond_mask_grid
    )
    with jax.named_scope("halo_y"):
        beside = lax.ppermute(beside, "sy", pairs("sy", -1))
        across = lax.ppermute(across, "sy", pairs("sy", 0))
    before, after = jnp.where(even_y, beside, across), jnp.where(even_y, across, beside)
    with jax.named_scope("halo_x"):
        def with_corners(payload, upper):
            corners = [
                jnp.concatenate([jnp.where(upper, part[0], part[-2]), part[-1]], axis=1) for part in (before, after)
            ]
            corners = jnp.concatenate(corners, axis=0)
            return lax.dynamic_update_slice(payload, corners, (payload.shape[0] - corners.shape[0], 0))

        near_payload = with_corners(near_payload, even_x)
        next_payload, _ = lax.optimization_barrier((next_payload, near_payload))
        near_rows = lax.ppermute(near_payload, "sx", pairs("sx", -1))
        next_rows = lax.ppermute(with_corners(next_payload, ~even_x), "sx", pairs("sx", 0))
    left, _ = lax.optimization_barrier((left_vectors, near_payload))
    left = left.transpose(1, 0, 2)
    f32 = jnp.float32
    part, edge_field, edge_rim, ends = vmem_call(
        interior_kernel,
        "interior",
        (
            jax.ShapeDtypeStruct((MOMENTS * nright, 2 * nleft), f32),
            jax.ShapeDtypeStruct((2, MOMENTS - 1, MOMENTS, nright, rows_y), f32),
            jax.ShapeDtypeStruct((2, MOMENTS - 1, MOMENTS, SUB, LANES), f32),
            jax.ShapeDtypeStruct((4, nright, rows_y), f32),
        ),
        scratch_of(rows_x, nright, rows_y),
        1 << 33,
        own, coup, before, after, left,
    )
    near = near_part(nsy)
    sites = rows_x * rows_y * nsx * nsy
    tile = vmem_call(
        functools.partial(border_kernel, -HALF_ROOT / sites**0.5),
        "border",
        jax.ShapeDtypeStruct((near, nsy // near, 1, MOMENTS * owned * nright), f32),
        scratch_of(rows_x, nright, rows_y)
        + [
            pltpu.VMEM((MOMENTS * nright, 2 * nleft), f32),
            pltpu.VMEM((nleft, LANES), f32),
            pltpu.VMEM((MOMENTS, nsy, owned * nright), f32),
        ],
        1 << 32,
        ends, coup, near_rows, next_rows, before, after, left, part, edge_field, edge_rim,
        scalars=(order,),
    )
    far_y = nsy // near
    block = tile.shape[2:]
    with jax.named_scope("reduce_near"):
        runs = [[n * near + i for i in range(near)] for n in range(far_y)]
        mine = jnp.sum(lax.all_to_all(tile, "sy", 0, 0, axis_index_groups=runs), axis=0)
    with jax.named_scope("reduce_far"):
        spread = jnp.broadcast_to(mine[:, None], (far_y, nsx) + block).reshape((far_y * nsx,) + block)
        planes = [[m * nsy + n * near + i for n in range(far_y) for m in range(nsx)] for i in range(near)]
        shares = lax.all_to_all(spread, ("sx", "sy"), 0, 0, axis_index_groups=planes)
    total = jnp.sum(shares, axis=0)
    wide = owned * nright
    total = jnp.concatenate([total[:, j * wide : (j + 1) * wide] for j in range(MOMENTS)], axis=0)
    return jnp.stack([total[:, q * nright : (q + 1) * nright] for q in range(owned)], axis=1)


def solution(mesh):
    in_specs = (
        P(None, "sx", "sy"),
        P(None, "sx", "sy"),
        P("sx", "sy"),
        P(),
        P(None, "sx", "sy"),
        P(),
    )
    out_specs = P(None, "sy", None)
    return jax.shard_map(shards, mesh=mesh, in_specs=in_specs, out_specs=out_specs, check_vma=False)
```
